32 devices in a mesh: ctx: 16 (over z, y, core), fsdp: 2 (over x).
Axes of the slice: x: 2, y: 2, z: 4, core: 2. Of those that a mesh axis runs over, the one named last changes fastest.
Arguments:
- tokens: bfloat16 [2, 16, 2, 128, 2048], P('fsdp', 'ctx'), may hold values from -6 to 6
- grad_out: bfloat16 [2, 16, 2, 128, 2048], P('fsdp', 'ctx'), may hold values from -6 to 6
- segments: int32 [2, 4096], replicated, may hold values from 0 to 3, as said below
- w_query: bfloat16 [2048, 2048], P('ctx', 'fsdp'), may hold values from -0.125 to 0.125
- key_weight_matrix: bfloat16 [2048, 1024], P('ctx', 'fsdp'), may hold values from -0.125 to 0.125
- value_weight_matrix: bfloat16 [2048, 1024], P('ctx', 'fsdp'), may hold values from -0.125 to 0.125
- w_output: bfloat16 [2048, 2048], P('ctx', 'fsdp'), may hold values from -0.75 to 0.75
- w_gate: bfloat16 [2048, 6144], P('ctx', 'fsdp'), may hold values from -0.125 to 0.125
- w_up: bfloat16 [2048, 6144], P('ctx', 'fsdp'), may hold values from -0.125 to 0.125
- w_down: bfloat16 [2048, 6144], P('ctx', 'fsdp'), may hold values from -0.078125 to 0.078125
- norm_attn: float32 [2048], replicated, may hold values from 0.5 to 1.5
- norm_mlp: float32 [2048], replicated, may hold values from 0.5 to 1.5
- norm_query: float32 [128], replicated, may hold values from 0.25 to 1.75
- norm_key: float32 [128], replicated, may hold values from 0.25 to 1.75
Outputs:
- out_tokens: bfloat16 [2, 16, 2, 128, 2048], P('fsdp', 'ctx')
- grad_tokens: float32 [2, 16, 2, 128, 2048], P('fsdp', 'ctx')
- grad_query: float32 [2048, 2048], P('ctx', 'fsdp')
- grad_key: float32 [2048, 1024], P('ctx', 'fsdp')
- grad_value: float32 [2048, 1024], P('ctx', 'fsdp')
- grad_output: float32 [2048, 2048], P('ctx', 'fsdp')
- grad_gate: float32 [2048, 6144], P('ctx', 'fsdp')
- grad_up: float32 [2048, 6144], P('ctx', 'fsdp')
- grad_down: float32 [2048, 6144], P('ctx', 'fsdp')
- grad_norm_attn: float32 [2048], replicated
- grad_norm_mlp: float32 [2048], replicated
- grad_norm_query: float32 [128], replicated
- grad_norm_key: float32 [128], replicated
The draws below stay inside these ranges and needn't reach their ends.
Inputs may be any that keep to these rules, and one draw needn't show every extreme that they name: `segments`: in every sequence segment numbers never fall and each of 0 to 3 occurs; every document has 205 to 1843 tokens, and in every sequence one document has exactly 1843.
All inputs are finite; a program needn't handle non-finite values.
Results may differ from the reference program's by a relative error of at most 0.023.
Values may be sent and summed in bfloat16 or wider, within the bound.
No kernel may reach another device: no remote copies, remote signals or barrier semaphores. Data moves between devices by JAX's collectives and lax.ppermute only.
A program may use at most 320 MiB of HBM per device.

```python
import math
import jax
import jax.numpy as jnp
from jax import lax

MODEL_WIDTH = 2048
QUERY_HEADS = 16
KEY_VALUE_HEADS = 8
HEAD_FEATURES = 128
FF = 6144
BLK = 128
DOC = 1024
PAIRS = 16
SEQS = 2
L = 4096
NDOC = 4


def draw_segments(key, part):
    half_range = 4 * DOC // 5

    def one_sequence(sequence_key):
        pair_count = NDOC // 2
        spread = jax.random.randint(sequence_key, (pair_count,), -half_range, half_range + 1, dtype=jnp.int32)
        spread = spread.at[0].set(half_range)
        lengths = jnp.concatenate([DOC + spread, DOC - spread, jnp.full((NDOC % 2,), DOC, dtype=jnp.int32)])
        order = jax.random.permutation(jax.random.fold_in(sequence_key, 7), NDOC)
        lengths = lengths[order]
        ends = jnp.cumsum(lengths)[:-1]
        index = jnp.arange(L, dtype=jnp.int32)
        return jnp.sum((index[:, None] >= ends[None, :]).astype(jnp.int32), axis=1)
    return jax.vmap(one_sequence)(jax.random.split(key, SEQS))


def levels(rng, dims, shards, least, high):
    level = 1.0
    for position, blocks in shards:
        steps = jax.random.uniform(jax.random.fold_in(jax.random.fold_in(rng, 6), position), (blocks,), jnp.float32, least / len(shards), high / len(shards))
        level = level * jnp.repeat(jnp.exp(steps), dims[position] // blocks).reshape((-1,) + (1,) * (len(dims) - 1 - position))
    return level


def bell_draw(key, shape, scale, limit, pieces=(), kind=jnp.bfloat16):
    loudness = levels(key, shape, pieces, -0.22, 0.18) if pieces else 1.0
    drawn = jax.random.normal(key, shape, jnp.float32) * scale * loudness
    return jnp.minimum(jnp.maximum(drawn, -limit), limit).astype(kind)


def setup_inputs(seed: int = 0) -> dict:
    arg_keys = jax.random.split(jax.random.key(seed), 15)
    return {
        "tokens": bell_draw(arg_keys[0], (SEQS, PAIRS, 2, BLK, MODEL_WIDTH), 1.0, 6.0, ((0, 2), (1, 16))),
        "grad_out": bell_draw(arg_keys[1], (SEQS, PAIRS, 2, BLK, MODEL_WIDTH), 1.0, 6.0, ((0, 2), (1, 16))),
        "segments": draw_segments(jax.random.fold_in(arg_keys[14], 71), 0),
        "w_query": bell_draw(arg_keys[3], (MODEL_WIDTH, QUERY_HEADS * HEAD_FEATURES), MODEL_WIDTH ** -0.5, 0.125, ((0, 16), (1, 2))),
        "key_weight_matrix": bell_draw(arg_keys[4], (MODEL_WIDTH, KEY_VALUE_HEADS * HEAD_FEATURES), MODEL_WIDTH ** -0.5, 0.125, ((0, 16), (1, 2))),
        "value_weight_matrix": bell_draw(arg_keys[5], (MODEL_WIDTH, KEY_VALUE_HEADS * HEAD_FEATURES), MODEL_WIDTH ** -0.5, 0.125, ((0, 16), (1, 2))),
        "w_output": bell_draw(arg_keys[6], (MODEL_WIDTH, QUERY_HEADS * HEAD_FEATURES), 64 ** -0.5, 0.75, ((0, 16), (1, 2))),
        "w_gate": bell_draw(arg_keys[7], (MODEL_WIDTH, FF), MODEL_WIDTH ** -0.5, 0.125, ((0, 16), (1, 2))),
        "w_up": bell_draw(arg_keys[8], (MODEL_WIDTH, FF), MODEL_WIDTH ** -0.5, 0.125, ((0, 16), (1, 2))),
        "w_down": bell_draw(arg_keys[9], (MODEL_WIDTH, FF), FF ** -0.5, 0.078125, ((0, 16), (1, 2))),
        "norm_attn": jnp.clip(1.0 + 0.1 * jax.random.normal(arg_keys[10], (MODEL_WIDTH,), jnp.float32), 0.5, 1.5),
        "norm_mlp": jnp.clip(1.0 + 0.1 * jax.random.normal(arg_keys[11], (MODEL_WIDTH,), jnp.float32), 0.5, 1.5),
        "norm_query": jnp.clip(1.0 + 0.15 * jax.random.normal(arg_keys[12], (HEAD_FEATURES,), jnp.float32), 0.25, 1.75),
        "norm_key": jnp.clip(1.0 + 0.15 * jax.random.normal(arg_keys[13], (HEAD_FEATURES,), jnp.float32), 0.25, 1.75),
    }


@jax.custom_vjp
def reduced_precision(v):
    return lax.optimization_barrier(v.astype(jnp.bfloat16)).astype(jnp.float32)

@jax.custom_vjp
def reduced_backward(v):
    return v

def low_keep(v):
    return (reduced_precision(v), None)

def low_pass(kept, grad):
    return (grad,)

def back_keep(v):
    return (v, None)

def back_low(kept, grad):
    return (reduced_precision(grad),)
reduced_precision.defvjp(low_keep, low_pass)
reduced_backward.defvjp(back_keep, back_low)
eps = 1e-06
rope_base = 1000000.0
masked_value = -1e+30

def matrix_product(left, right):
    return jnp.dot(left, right, precision=lax.Precision.HIGHEST, preferred_element_type=jnp.float32)

def rms_scale(values, gain):
    return values * lax.rsqrt(lax.optimization_barrier(jnp.mean(values * values, axis=-1, keepdims=True)) + eps) * gain

def rotate(values, cosine, sine):
    half_width = values.shape[-1] // 2
    turned = jnp.concatenate([-values[..., half_width:], values[..., :half_width]], axis=-1)
    return values * cosine + turned * sine

def doc_positions(segments):
    index = jnp.arange(segments.shape[-1], dtype=jnp.int32)
    first = jnp.concatenate([jnp.ones_like(segments[..., :1], dtype=bool), segments[..., 1:] != segments[..., :-1]], axis=-1)
    starts = lax.cummax(jnp.where(first, index, 0), axis=segments.ndim - 1)
    return index - starts

def rope_tables(positions):
    freq = jnp.exp(jnp.arange(HEAD_FEATURES // 2, dtype=jnp.float32) * (-2.0 * math.log(rope_base) / HEAD_FEATURES))
    angle = positions.astype(jnp.float32)[..., None] * freq
    angle = jnp.concatenate([angle, angle], axis=-1)
    return (jnp.cos(angle), jnp.sin(angle))

def to_sequence(blocks):
    ordered = jnp.concatenate([blocks[:, :, 0], blocks[:, ::-1, 1]], axis=1)
    return ordered.reshape(blocks.shape[0], -1, blocks.shape[-1])

def to_blocks(ordered, block_rows):
    pair_count = ordered.shape[1] // (2 * block_rows)
    split = ordered.reshape(ordered.shape[0], 2 * pair_count, block_rows, ordered.shape[-1])
    return jnp.stack([split[:, :pair_count], split[:, pair_count:][:, ::-1]], axis=2)

def attention(query_vectors, key, value, segment, rows):
    token_length = key.shape[1]
    index = jnp.arange(token_length, dtype=jnp.int32)

    def one_block(start):
        part = lax.dynamic_slice_in_dim(query_vectors, start, rows, 2)
        part_index = lax.dynamic_slice_in_dim(index, start, rows, 0)
        part_segment = lax.dynamic_slice_in_dim(segment, start, rows, 0)
        products = jnp.einsum('gqrd,gkd->gqrk', part, key, precision=lax.Precision.HIGHEST)
        scores = reduced_backward(products * HEAD_FEATURES ** (-0.5))
        valid = (part_segment[:, None] == segment[None, :]) & (index[None, :] <= part_index[:, None])
        scores = jnp.where(valid, scores, masked_value)
        peak = lax.optimization_barrier(jnp.max(scores, axis=-1, keepdims=True))
        exponent = jnp.exp(scores - peak)
        probs = reduced_precision(exponent / lax.optimization_barrier(jnp.sum(exponent, axis=-1, keepdims=True)))
        return jnp.einsum('gqrk,gkd->gqrd', probs, value, precision=lax.Precision.HIGHEST)
    starts = jnp.arange(0, token_length, rows, dtype=jnp.int32)
    outputs = lax.map(jax.checkpoint(one_block), starts)
    return jnp.moveaxis(outputs, 0, 2).reshape(query_vectors.shape)

def layer(ordered, params, segment, cosine, sine):
    w_query, key_weight_matrix, value_weight_matrix, w_output, w_gate, w_up, w_down, norm_attn, norm_mlp, norm_query, norm_key = params
    token_length = ordered.shape[0]
    heads_per_group = QUERY_HEADS // KEY_VALUE_HEADS
    normalized_input = reduced_precision(rms_scale(ordered, norm_attn))
    query_raw = reduced_backward(matrix_product(normalized_input, w_query)).reshape(token_length, QUERY_HEADS, HEAD_FEATURES)
    unrotated_key = reduced_backward(matrix_product(normalized_input, key_weight_matrix)).reshape(token_length, KEY_VALUE_HEADS, HEAD_FEATURES)
    unprojected_value = reduced_backward(reduced_precision(matrix_product(normalized_input, value_weight_matrix))).reshape(token_length, KEY_VALUE_HEADS, HEAD_FEATURES)
    query_vectors = reduced_precision(rotate(rms_scale(query_raw, norm_query), cosine[:, None], sine[:, None]))
    key = reduced_precision(rotate(rms_scale(unrotated_key, norm_key), cosine[:, None], sine[:, None]))
    query_vectors = jnp.transpose(query_vectors, (1, 0, 2)).reshape(KEY_VALUE_HEADS, heads_per_group, token_length, HEAD_FEATURES)
    heads = attention(query_vectors, jnp.transpose(key, (1, 0, 2)), jnp.transpose(unprojected_value, (1, 0, 2)), segment, min(token_length, 512))
    mixed = reduced_backward(reduced_precision(jnp.transpose(heads.reshape(QUERY_HEADS, token_length, HEAD_FEATURES), (1, 0, 2)).reshape(token_length, QUERY_HEADS * HEAD_FEATURES)))
    middle = ordered + reduced_backward(matrix_product(mixed, w_output.T))
    normed_mid = reduced_precision(rms_scale(middle, norm_mlp))
    gate = reduced_backward(matrix_product(normed_mid, w_gate))
    up_part = reduced_backward(matrix_product(normed_mid, w_up))
    active = reduced_precision(gate / (1.0 + jnp.exp(-gate)) * up_part)
    return middle + reduced_backward(matrix_product(active, w_down.T))

def reference(tokens, grad_out, segments, w_query, key_weight_matrix, value_weight_matrix, w_output, w_gate, w_up, w_down, norm_attn, norm_mlp, norm_query, norm_key):
    matrices = tuple((weight.astype(jnp.float32) for weight in (w_query, key_weight_matrix, value_weight_matrix, w_output, w_gate, w_up, w_down)))
    params = matrices + (norm_attn, norm_mlp, norm_query, norm_key)
    ordered = to_sequence(tokens.astype(jnp.float32))
    cotangent = to_sequence(grad_out.astype(jnp.float32))
    cosine, sine = rope_tables(doc_positions(segments))

    def step(running, bundle):
        inputs, cot_part, segment, cos_part, sin_part = bundle
        result, pull = jax.vjp(lambda values, weights_all: layer(values, weights_all, segment, cos_part, sin_part), inputs, params)
        grad_inputs, grad_params = pull(cot_part)
        return (jax.tree.map(jnp.add, running, grad_params), (result, grad_inputs))
    running, (results, grads) = lax.scan(step, jax.tree.map(jnp.zeros_like, params), (ordered, cotangent, segments, cosine, sine))
    block_rows = tokens.shape[3]
    out_tokens = to_blocks(results, block_rows).astype(jnp.bfloat16)
    grad_tokens = to_blocks(grads, block_rows)
    return (out_tokens, grad_tokens, running[0], running[1], running[2], running[3], running[4], running[5], running[6], running[7], running[8], running[9], running[10])
```

```python
import functools
import math

import jax
import jax.numpy as jnp
from jax import lax
from jax.experimental import pallas as pl
from jax.experimental.pallas import tpu as pltpu
from jax.sharding import PartitionSpec as P

QUERY_HEADS = 16
KEY_VALUE_HEADS = 8
HD = 128
DOCS = 4
CHUNK = 256
eps = 1e-06
rope_base = 1000000.0
SCALE = HD ** (-0.5)
EXP2_SCALE = SCALE * math.log2(math.e)
F32 = jnp.float32
BF16 = jnp.bfloat16


def xor_send(value, axis, step):
    count = lax.axis_size(axis)
    return lax.ppermute(value, axis, [(i, i ^ step) for i in range(count)])


def stage_offsets(count):
    quarter = count // 4
    base = [4 * i for i in range(quarter)]
    return [b ^ low for low in (0, 2, 1, 3) for b in base]


def stage_gather(piece, axis):
    count = lax.axis_size(axis)
    first = jnp.concatenate(
        [piece[None]] + [xor_send(piece[None], axis, 4 * i) for i in range(1, count // 4)], axis=0
    )
    second = xor_send(first, axis, 2)
    return first, second, xor_send(first, axis, 1), xor_send(second, axis, 1)


def stage_scatter_tail(half, axis):
    count = lax.axis_size(axis)
    quarter = half.shape[0] // 2
    kept = half[:quarter].astype(F32) + xor_send(half[quarter:], axis, 2).astype(F32)
    kept = kept.astype(BF16)
    block = quarter // (count // 4)
    total = kept[:block].astype(F32)
    for i in range(1, count // 4):
        total = total + xor_send(kept[i * block : (i + 1) * block], axis, 4 * i).astype(F32)
    return total


def exchange_rows(rows, axis):
    return [rows] + [xor_send(rows, axis, r) for r in range(1, lax.axis_size(axis))]


def scatter_rows(partial, axis):
    count = lax.axis_size(axis)
    rows = partial.shape[0] // count
    total = partial[:rows].astype(F32)
    for r in range(1, count):
        total = total + xor_send(partial[r * rows : (r + 1) * rows], axis, r).astype(F32)
    return total


def dot(left, right):
    return jnp.dot(left, right, preferred_element_type=F32)


def dot_rows(left, right):
    return lax.dot_general(left, right, (((0,), (0,)), ((), ())), preferred_element_type=F32)


def dot_cols(left, right):
    return lax.dot_general(left, right, (((1,), (1,)), ((), ())), preferred_element_type=F32)


def vmem_limit(mib):
    return pltpu.CompilerParams(vmem_limit_bytes=mib * 1024 * 1024)


def permute_kernel(offsets, me_ref, x_ref, o_ref):
    me = me_ref[0]
    width = x_ref.shape[1] // len(offsets)
    for place, offset in enumerate(offsets):
        start = pl.multiple_of(lax.bitwise_xor(me, offset) * width, width)
        o_ref[:, place * width : (place + 1) * width] = x_ref[:, pl.ds(start, width)]


def permute_columns(x, me, count):
    rows, width = x.shape
    tile = min(rows, 256)
    return pl.pallas_call(
        functools.partial(permute_kernel, stage_offsets(count)),
        out_shape=jax.ShapeDtypeStruct(x.shape, x.dtype),
        grid_spec=pltpu.PrefetchScalarGridSpec(
            num_scalar_prefetch=1,
            grid=(rows // tile,),
            in_specs=[pl.BlockSpec((tile, width), lambda i, m: (i, 0))],
            out_specs=pl.BlockSpec((tile, width), lambda i, m: (i, 0)),
        ),
        cost_estimate=pl.CostEstimate(flops=0, bytes_accessed=2 * x.size * 2, transcendentals=0),
        name="permute_columns",
    )(me, x)


def prep_kernel(query_heads, groups, raw_ref, cos_ref, sin_ref, gq_ref, gk_ref, q_ref, kv_ref):
    cos = cos_ref[...]
    sin = sin_ref[...]

    def rotate_norm(x, gain):
        scale = lax.rsqrt(jnp.mean(x * x, axis=-1, keepdims=True) + eps)
        u = x * scale * gain
        return u * cos + pltpu.roll(u, HD // 2, 1) * sin

    for h in range(query_heads):
        cols = slice(h * HD, (h + 1) * HD)
        q_ref[:, cols] = rotate_norm(raw_ref[:, cols], gq_ref[...]).astype(BF16)
    for h in range(groups):
        k = raw_ref[:, (query_heads + h) * HD : (query_heads + h + 1) * HD]
        v = raw_ref[:, (query_heads + groups + h) * HD : (query_heads + groups + h + 1) * HD]
        kv_ref[:, 2 * h * HD : (2 * h + 1) * HD] = rotate_norm(k, gk_ref[...]).astype(BF16)
        kv_ref[:, (2 * h + 1) * HD : (2 * h + 2) * HD] = v.astype(BF16)


def head_prep(raw, cos, sin, gq, gk, query_heads, groups):
    rows, width = raw.shape
    tile = 128
    vec = pl.BlockSpec((1, HD), lambda i: (0, 0))
    tab = pl.BlockSpec((tile, HD), lambda i: (i, 0))
    return pl.pallas_call(
        functools.partial(prep_kernel, query_heads, groups),
        out_shape=(
            jax.ShapeDtypeStruct((rows, query_heads * HD), BF16),
            jax.ShapeDtypeStruct((rows, 2 * groups * HD), BF16),
        ),
        grid=(rows // tile,),
        in_specs=[pl.BlockSpec((tile, width), lambda i: (i, 0)), tab, tab, vec, vec],
        out_specs=(
            pl.BlockSpec((tile, query_heads * HD), lambda i: (i, 0)),
            pl.BlockSpec((tile, 2 * groups * HD), lambda i: (i, 0)),
        ),
        cost_estimate=pl.CostEstimate(
            flops=20 * raw.size, bytes_accessed=6 * raw.size, transcendentals=0
        ),
        name="head_prep",
    )(raw, cos, sin, gq, gk)


def prep_back_kernel(heads, stride, d_ref, raw_ref, cos_ref, sin_ref, g_ref, out_ref, gain_ref):
    cos = cos_ref[...]
    sin = sin_ref[...]
    gain = g_ref[...]
    gain_sum = jnp.zeros((1, HD), F32)
    for h in range(heads):
        cols = slice(h * HD, (h + 1) * HD)
        x = raw_ref[:, cols]
        d = d_ref[:, stride * h * HD : (stride * h + 1) * HD].astype(F32)
        t = d * cos - pltpu.roll(d, HD // 2, 1) * sin
        scale = lax.rsqrt(jnp.mean(x * x, axis=-1, keepdims=True) + eps)
        n = x * scale
        gain_sum = gain_sum + jnp.sum(t * n, axis=0, keepdims=True)
        e = t * gain
        out_ref[:, cols] = (scale * (e - n * jnp.mean(e * n, axis=-1, keepdims=True))).astype(BF16)

    @pl.when(pl.program_id(0) == 0)
    def _():
        gain_ref[...] = jnp.zeros_like(gain_ref)

    gain_ref[...] += gain_sum


def head_prep_back(grad, raw, cos, sin, gain, heads, stride, raw_block):
    rows = raw.shape[0]
    tile = 128
    width = heads * HD
    tab = pl.BlockSpec((tile, HD), lambda i: (i, 0))
    return pl.pallas_call(
        functools.partial(prep_back_kernel, heads, stride),
        out_shape=(
            jax.ShapeDtypeStruct((rows, width), BF16),
            jax.ShapeDtypeStruct((1, HD), F32),
        ),
        grid=(rows // tile,),
        in_specs=[
            pl.BlockSpec((tile, grad.shape[1]), lambda i: (i, 0)),
            pl.BlockSpec((tile, width), lambda i: (i, raw_block)),
            tab,
            tab,
            pl.BlockSpec((1, HD), lambda i: (0, 0)),
        ],
        out_specs=(
            pl.BlockSpec((tile, width), lambda i: (i, 0)),
            pl.BlockSpec((1, HD), lambda i: (0, 0)),
        ),
        cost_estimate=pl.CostEstimate(
            flops=20 * rows * width, bytes_accessed=10 * rows * width, transcendentals=0
        ),
        name="head_prep_back",
    )(grad, raw, cos, sin, gain)


def load_sequence(me, offsets, quarters, keys, values):
    per = len(offsets) // 4
    block = quarters[0].shape[2]
    for place, offset in enumerate(offsets):
        ref = quarters[place // per]
        owner = lax.bitwise_xor(me, offset)
        for half, index in ((0, owner), (1, 2 * len(offsets) - 1 - owner)):
            rows = pl.ds(pl.multiple_of(index * block, block), block)
            keys[rows, :] = ref[place % per, half, :, :HD]
            values[rows, :] = ref[place % per, half, :, HD:]


def stack_heads(tile, count):
    return jnp.concatenate([tile[:, h * HD : (h + 1) * HD] for h in range(count)], axis=0)


def row_positions(info_ref, half, block, count):
    first = info_ref[1 + 3 * half]
    lane = lax.broadcasted_iota(jnp.int32, (1, count * block), 1)
    position = first + lax.rem(lane, block)
    start_first, start_last = info_ref[2 + 3 * half], info_ref[3 + 3 * half]
    start = jnp.where(position >= start_last, start_last, start_first)
    return position, start, start_first // CHUNK, (first + block - 1) // CHUNK + 1


def valid_tile(chunk, position, start, shape):
    key_index = chunk * CHUNK + lax.broadcasted_iota(jnp.int32, shape, 0)
    return (key_index <= position) & (key_index >= start)


def forward_kernel(offsets, count, info_ref, q_ref, s0, s1, s2, s3, o_ref, lse_ref, keys, values):
    load_sequence(info_ref[0], offsets, (s0, s1, s2, s3), keys, values)
    block = q_ref.shape[1]
    columns = count * block
    for half in range(2):
        queries = stack_heads(q_ref[half], count)
        position, start, low, high = row_positions(info_ref, half, block, count)

        def body(chunk, carry):
            total, norm = carry
            rows = pl.ds(pl.multiple_of(chunk * CHUNK, CHUNK), CHUNK)
            score = dot_cols(keys[rows, :], queries)
            weight = jnp.where(
                valid_tile(chunk, position, start, score.shape), jnp.exp2(score * EXP2_SCALE), 0.0
            )
            norm = norm + jnp.sum(weight, axis=0, keepdims=True)
            total = total + dot_rows(values[rows, :], weight.astype(BF16))
            return total, norm

        total, norm = lax.fori_loop(
            low, high, body, (jnp.zeros((HD, columns), F32), jnp.zeros((1, columns), F32))
        )
        out = (total / norm).T.astype(BF16)
        for h in range(count):
            o_ref[half, :, h * HD : (h + 1) * HD] = out[h * block : (h + 1) * block]
        lse_ref[0, half] = jnp.log2(norm)


def backward_kernel(
    offsets, count, info_ref, q_ref, do_ref, o_ref, lse_ref, s0, s1, s2, s3,
    dq_ref, keep_ref, send_ref, keys, values, grad_k, grad_v,
):
    me = info_ref[0]
    load_sequence(me, offsets, (s0, s1, s2, s3), keys, values)
    block = q_ref.shape[1]
    columns = count * block
    grad_k[...] = jnp.zeros_like(grad_k)
    grad_v[...] = jnp.zeros_like(grad_v)
    for half in range(2):
        queries = stack_heads(q_ref[half], count)
        grads = stack_heads(do_ref[half], count)
        outs = stack_heads(o_ref[half], count)
        delta = jnp.sum((grads.astype(F32) * outs.astype(F32)).T, axis=0, keepdims=True)
        lse = lse_ref[0, half]
        position, start, low, high = row_positions(info_ref, half, block, count)

        def body(chunk, total):
            rows = pl.ds(pl.multiple_of(chunk * CHUNK, CHUNK), CHUNK)
            key_rows = keys[rows, :]
            score = dot_cols(key_rows, queries)
            prob = jnp.where(
                valid_tile(chunk, position, start, score.shape),
                jnp.exp2(score * EXP2_SCALE - lse),
                0.0,
            )
            grad_prob = dot_cols(values[rows, :], grads)
            grad_score = (prob * (grad_prob - delta)).astype(BF16)
            grad_v[rows, :] += dot(prob.astype(BF16), grads)
            grad_k[rows, :] += dot(grad_score, queries)
            return total + dot_rows(key_rows, grad_score)

        total = lax.fori_loop(low, high, body, jnp.zeros((HD, columns), F32))
        out = total.T * SCALE
        for h in range(count):
            dq_ref[half, :, h * HD : (h + 1) * HD] = out[h * block : (h + 1) * block]
    half_count = len(offsets) // 2
    for place, offset in enumerate(offsets):
        ref = (keep_ref, send_ref)[place // half_count]
        owner = lax.bitwise_xor(me, offset)
        for half, index in ((0, owner), (1, 2 * len(offsets) - 1 - owner)):
            rows = pl.ds(pl.multiple_of(index * block, block), block)
            ref[place % half_count, half, :, :HD] = (grad_k[rows, :] * SCALE).astype(BF16)
            ref[place % half_count, half, :, HD:] = grad_v[rows, :].astype(BF16)


def attend(info, q, quarters, count):
    _, block, width = q.shape
    per = quarters[0].shape[0]
    groups = quarters[0].shape[3] // (2 * HD)
    length = per * 8 * block
    row = pl.BlockSpec((2, block, count * HD), lambda n, i: (0, 0, n))
    part = pl.BlockSpec((per, 2, block, 2 * HD), lambda n, i: (0, 0, 0, n))
    return pl.pallas_call(
        functools.partial(forward_kernel, stage_offsets(4 * per), count),
        out_shape=(
            jax.ShapeDtypeStruct(q.shape, BF16),
            jax.ShapeDtypeStruct((groups, 2, 1, count * block), F32),
        ),
        grid_spec=pltpu.PrefetchScalarGridSpec(
            num_scalar_prefetch=1,
            grid=(groups,),
            in_specs=[row, part, part, part, part],
            out_specs=(
                row,
                pl.BlockSpec((1, 2, 1, count * block), lambda n, i: (n, 0, 0, 0)),
            ),
            scratch_shapes=[pltpu.VMEM((length, HD), BF16)] * 2,
        ),
        compiler_params=vmem_limit(48),
        cost_estimate=pl.CostEstimate(
            flops=groups * 2 * 8 * CHUNK * columns_of(count, block) * HD,
            bytes_accessed=groups * length * HD * 4,
            transcendentals=0,
        ),
        name="attend",
    )(info, q, *quarters)


def columns_of(count, block):
    return 2 * count * block


def attend_back(info, q, grad, out, lse, quarters, count):
    _, block, width = q.shape
    per = quarters[0].shape[0]
    groups = quarters[0].shape[3] // (2 * HD)
    length = per * 8 * block
    row = pl.BlockSpec((2, block, count * HD), lambda n, i: (0, 0, n))
    part = pl.BlockSpec((per, 2, block, 2 * HD), lambda n, i: (0, 0, 0, n))
    double = pl.BlockSpec((2 * per, 2, block, 2 * HD), lambda n, i: (0, 0, 0, n))
    kv_half = jax.ShapeDtypeStruct((2 * per,) + quarters[0].shape[1:], BF16)
    return pl.pallas_call(
        functools.partial(backward_kernel, stage_offsets(4 * per), count),
        out_shape=(jax.ShapeDtypeStruct(q.shape, F32), kv_half, kv_half),
        grid_spec=pltpu.PrefetchScalarGridSpec(
            num_scalar_prefetch=1,
            grid=(groups,),
            in_specs=[
                row,
                row,
                row,
                pl.BlockSpec((1, 2, 1, count * block), lambda n, i: (n, 0, 0, 0)),
                part,
                part,
                part,
                part,
            ],
            out_specs=(row, double, double),
            scratch_shapes=[pltpu.VMEM((length, HD), BF16)] * 2
            + [pltpu.VMEM((length, HD), F32)] * 2,
        ),
        compiler_params=vmem_limit(56),
        cost_estimate=pl.CostEstimate(
            flops=groups * 5 * 8 * CHUNK * columns_of(count, block) * HD,
            bytes_accessed=groups * length * HD * 8,
            transcendentals=0,
        ),
        name="attend_back",
    )(info, q, grad, out, lse, *quarters)


def unit_rows(values):
    scale = lax.rsqrt(jnp.mean(values * values, axis=-1, keepdims=True) + eps)
    return scale, values * scale


def unit_back(grad, gain, scale, unit):
    scaled = grad * gain
    return scale * (scaled - unit * jnp.mean(scaled * unit, axis=-1, keepdims=True))


def local(
    tokens,
    grad_out,
    segments,
    w_query,
    key_weight_matrix,
    value_weight_matrix,
    w_output,
    w_gate,
    w_up,
    w_down,
    norm_attn,
    norm_mlp,
    norm_query,
    norm_key,
):
    ctx_count = lax.axis_size("ctx")
    seq_count = lax.axis_size("fsdp")
    me = lax.axis_index("ctx").astype(jnp.int32)
    my_seq = lax.axis_index("fsdp").astype(jnp.int32)
    block = tokens.shape[3]
    width = tokens.shape[4]
    own = 2 * block
    query_heads = w_query.shape[1] // HD
    groups = key_weight_matrix.shape[1] // HD
    count = query_heads // groups
    q_width, k_width = query_heads * HD, groups * HD
    me_array = me.reshape(1)

    full_qkv = lax.all_gather(
        jnp.concatenate([w_query, key_weight_matrix, value_weight_matrix], axis=1),
        "ctx",
        axis=0,
        tiled=True,
    )
    full_output = lax.all_gather(w_output, "ctx", axis=0, tiled=True)
    full_gate = lax.all_gather(w_gate, "ctx", axis=0, tiled=True)
    full_up = lax.all_gather(w_up, "ctx", axis=0, tiled=True)
    full_down = lax.all_gather(w_down, "ctx", axis=0, tiled=True)

    inputs = tokens.reshape(own, width).astype(F32)
    r1, n1 = unit_rows(inputs)
    h1 = exchange_rows((n1 * norm_attn).astype(BF16), "fsdp")
    cot_own = grad_out.reshape(own, width)
    cot_all = jnp.concatenate(exchange_rows(cot_own, "fsdp"), axis=0)

    offsets = jnp.arange(block, dtype=jnp.int32)
    firsts = (me * block, (2 * ctx_count - 1 - me) * block)
    rows_index = jnp.concatenate([firsts[0] + offsets, firsts[1] + offsets])
    freq = jnp.exp(jnp.arange(HD // 2, dtype=F32) * (-2.0 * math.log(rope_base) / HD))
    infos, tables = [], []
    for r in range(seq_count):
        line = lax.dynamic_index_in_dim(
            segments, lax.bitwise_xor(my_seq, jnp.int32(r)), 0, keepdims=False
        )
        doc_first = [jnp.sum((line < d).astype(jnp.int32)) for d in range(DOCS)]
        mine = jnp.concatenate([lax.dynamic_slice_in_dim(line, f, block) for f in firsts])
        start = sum(jnp.where(mine == d, doc_first[d], 0) for d in range(DOCS))
        scalars = [me]
        for half in range(2):
            scalars += [firsts[half], start[half * block], start[(half + 1) * block - 1]]
        infos.append(jnp.stack(scalars))
        angle = (rows_index - start).astype(F32)[:, None] * freq
        cos, sin = jnp.cos(angle), jnp.sin(angle)
        tables.append((jnp.concatenate([cos, cos], 1), jnp.concatenate([-sin, sin], 1)))
    gain_q, gain_k = norm_query.reshape(1, HD), norm_key.reshape(1, HD)

    raws, queries, quarters = [], [], []
    for r in range(seq_count):
        raw = dot(h1[r], full_qkv)
        q, kv = head_prep(raw, *tables[r], gain_q, gain_k, query_heads, groups)
        raws.append(raw)
        queries.append(q.reshape(2, block, q_width))
        quarters.append(stage_gather(kv.reshape(2, block, 2 * k_width), "ctx"))
    heads, sums = [], []
    for r in range(seq_count):
        o, lse = attend(infos[r], queries[r], quarters[r], count)
        heads.append(o)
        sums.append(lse)
    mixed = jnp.concatenate([o.reshape(own, q_width) for o in heads], axis=0)
    x2 = inputs + scatter_rows(dot_cols(mixed, full_output).astype(BF16), "fsdp")

    r2, n2 = unit_rows(x2)
    h2 = jnp.concatenate(exchange_rows((n2 * norm_mlp).astype(BF16), "fsdp"), axis=0)
    gate = dot(h2, full_gate)
    up = dot(h2, full_up)
    sg = 1.0 / (1.0 + jnp.exp(-gate))
    silu = gate * sg
    act = (silu * up).astype(BF16)
    y = x2 + scatter_rows(dot_cols(act, full_down).astype(BF16), "fsdp")
    out_tokens = y.astype(BF16).reshape(tokens.shape)

    def scatter_weight(grad):
        return lax.psum_scatter(
            grad.astype(BF16), "ctx", scatter_dimension=0, tiled=True
        ).astype(F32)

    shard_down = scatter_weight(dot_rows(cot_all, act))
    d_act = dot(cot_all, full_down)
    d_gate = (d_act * up * sg * (1.0 + gate * (1.0 - sg))).astype(BF16)
    d_up = (d_act * silu).astype(BF16)
    d_h2 = scatter_rows(
        (dot_cols(d_gate, full_gate) + dot_cols(d_up, full_up)).astype(BF16), "fsdp"
    )
    shard_gate = scatter_weight(dot_rows(h2, d_gate))
    shard_up = scatter_weight(dot_rows(h2, d_up))
    gain_mlp = jnp.sum(d_h2 * n2, axis=0)
    d_x2 = cot_own.astype(F32) + unit_back(d_h2, norm_mlp, r2, n2)
    branch = jnp.concatenate(exchange_rows(d_x2.astype(BF16), "fsdp"), axis=0)
    d_att = dot(branch, full_output).astype(BF16)

    half_width = width // 2

    def scatter_staged(left, right):
        sent = dot_rows(left[:, half_width:], right).astype(BF16)
        kept = dot_rows(left[:, :half_width], right)
        return stage_scatter_tail(
            (kept + xor_send(sent, "ctx", 1).astype(F32)).astype(BF16), "ctx"
        )

    shard_output = scatter_staged(permute_columns(branch, me_array, ctx_count), mixed)
    h1_all = jnp.concatenate(h1, axis=0)
    h1_staged = permute_columns(h1_all, me_array, ctx_count)

    d_queries, d_kvs = [], []
    for r in range(seq_count):
        d_q, kept, sent = attend_back(
            infos[r],
            queries[r],
            d_att[r * own : (r + 1) * own].reshape(2, block, q_width),
            heads[r],
            sums[r],
            quarters[r],
            count,
        )
        d_queries.append(d_q.reshape(own, q_width))
        half = kept.astype(F32) + xor_send(sent, "ctx", 1).astype(F32)
        d_kvs.append(
            stage_scatter_tail(half.astype(BF16), "ctx").reshape(own, 2 * k_width)
        )
    d_qps, d_kps, d_vs = [], [], []
    gain_q_sum = jnp.zeros((1, HD), F32)
    gain_k_sum = jnp.zeros((1, HD), F32)
    for r in range(seq_count):
        d_qp, part = head_prep_back(
            d_queries[r], raws[r], *tables[r], gain_q, query_heads, 1, 0
        )
        gain_q_sum = gain_q_sum + part
        d_qps.append(d_qp)
        d_kp, part = head_prep_back(
            d_kvs[r], raws[r], *tables[r], gain_k, groups, 2, query_heads // groups
        )
        gain_k_sum = gain_k_sum + part
        d_kps.append(d_kp)
        d_vs.append(
            d_kvs[r].reshape(own, groups, 2, HD)[:, :, 1].reshape(own, k_width).astype(BF16)
        )
    d_qp_all = jnp.concatenate(d_qps, axis=0)
    d_kv_all = jnp.concatenate(
        [jnp.concatenate([k, v], axis=1) for k, v in zip(d_kps, d_vs)], axis=0
    )
    shard_query = scatter_staged(h1_staged, d_qp_all)
    shard_kv = scatter_staged(h1_staged, d_kv_all)
    d_h1 = scatter_rows(
        (
            dot_cols(d_qp_all, full_qkv[:, :q_width]) + dot_cols(d_kv_all, full_qkv[:, q_width:])
        ).astype(BF16),
        "fsdp",
    )
    gain_attn = jnp.sum(d_h1 * n1, axis=0)
    grad_tokens = (d_x2 + unit_back(d_h1, norm_attn, r1, n1)).reshape(tokens.shape)
    gains = lax.psum(
        jnp.concatenate([gain_attn, gain_mlp, gain_q_sum[0], gain_k_sum[0]]), ("ctx", "fsdp")
    )
    return (
        out_tokens,
        grad_tokens,
        shard_query,
        shard_kv[:, :k_width],
        shard_kv[:, k_width:],
        shard_output,
        shard_gate,
        shard_up,
        shard_down,
        gains[:width],
        gains[width : 2 * width],
        gains[2 * width : 2 * width + HD],
        gains[2 * width + HD :],
    )


def solution(mesh):
    block = P("fsdp", "ctx", None, None, None)
    weight = P("ctx", "fsdp")
    return jax.shard_map(
        local,
        mesh=mesh,
        in_specs=(block, block, P()) + (weight,) * 7 + (P(),) * 4,
        out_specs=(block, block) + (weight,) * 7 + (P(),) * 4,
        check_vma=False,
    )
```

```python
import functools
import math

import jax
import jax.numpy as jnp
from jax import lax
from jax.experimental import pallas as pl
from jax.experimental.pallas import tpu as pltpu
from jax.sharding import PartitionSpec as P

QUERY_HEADS = 16
KEY_VALUE_HEADS = 8
HD = 128
DOCS = 4
CHUNK = 256
eps = 1e-06
rope_base = 1000000.0
SCALE = HD ** (-0.5)
EXP2_SCALE = SCALE * math.log2(math.e)
F32 = jnp.float32
BF16 = jnp.bfloat16


def xor_send(value, axis, step):
    count = lax.axis_size(axis)
    return lax.ppermute(value, axis, [(i, i ^ step) for i in range(count)])


def exchange_rows(rows, axis):
    return [rows] + [xor_send(rows, axis, r) for r in range(1, lax.axis_size(axis))]


def scatter_rows(partial, axis):
    count = lax.axis_size(axis)
    rows = partial.shape[0] // count
    total = partial[:rows].astype(F32)
    for r in range(1, count):
        total = total + xor_send(partial[r * rows : (r + 1) * rows], axis, r).astype(F32)
    return total


def pair_groups(count):
    return [[i for i in range(count) if (i >> 1) & 1 == bit] for bit in (0, 1)]


def swap_blocks(x, count, axis):
    shape = x.shape
    split = x.reshape(shape[:axis] + (count // 4, 2, 2, shape[axis] // count) + shape[axis + 1 :])
    return split.swapaxes(axis + 1, axis + 2).reshape(shape)


def assemble_kernel(plan, *refs):
    out_ref = refs[-1]
    place = 0
    for index, start, number in plan:
        out_ref[place : place + number, :] = refs[index][start : start + number, :]
        place += number


def assemble(arrays, plan):
    width = arrays[0].shape[1]
    rows = sum(number for _, _, number in plan)
    return pl.pallas_call(
        functools.partial(assemble_kernel, plan),
        out_shape=jax.ShapeDtypeStruct((rows, width), arrays[0].dtype),
        compiler_params=vmem_limit(32),
        cost_estimate=pl.CostEstimate(
            flops=0, bytes_accessed=4 * rows * width, transcendentals=0
        ),
        name="assemble",
    )(*arrays)


def gather_rows(rows, ways):
    count = lax.axis_size("fsdp")
    total = rows.shape[0]
    if ways == 1:
        return assemble(exchange_rows(rows, "fsdp"), [(r, 0, total) for r in range(count)])
    block = total // 2
    low = rows[:block]
    lows = exchange_rows(low, "fsdp")
    high = jnp.concatenate([rows[block:], xor_send(rows[block:], "ctx", 2)], axis=0)
    highs = exchange_rows(high, "fsdp")
    others = xor_send(jnp.concatenate(lows, axis=0), "ctx", 2)
    plan = []
    for r in range(count):
        plan += [(1 + r, 0, block), (0, r * block, block), (1 + count + r, 0, 2 * block)]
    return assemble([others] + lows + highs, plan)


def return_rows(partial, ways):
    count = lax.axis_size("fsdp")
    if ways == 1:
        rows = partial.shape[0] // count
        terms = [partial[:rows]] + [
            xor_send(partial[r * rows : (r + 1) * rows], "fsdp", r) for r in range(1, count)
        ]
        return [t[: rows // 2] for t in terms], [t[rows // 2 :] for t in terms]
    block = partial.shape[0] // (4 * count)

    def rows(start, number):
        return partial[start * block : (start + number) * block]

    sent = jnp.concatenate([rows(4 * r + 1, 1) for r in range(count)], axis=0)
    pairs = [xor_send(rows(4 * r + 2, 2), "fsdp", r) for r in range(1, count)]
    other = xor_send(sent, "ctx", 2)
    first = [
        (rows(4 * r, 1).astype(F32) + other[r * block : (r + 1) * block].astype(F32)).astype(BF16)
        for r in range(count)
    ]
    second = rows(2, 2).astype(F32)
    for term in pairs:
        second = second + term.astype(F32)
    second = second.astype(BF16)
    lows = [first[0]] + [xor_send(first[r], "fsdp", r) for r in range(1, count)]
    return lows, [second[:block], xor_send(second[block:], "ctx", 2)]


def natural_columns(x, count):
    width = x.shape[1] // count
    order = [(i & ~3) | ((i & 1) << 1) | ((i >> 1) & 1) for i in range(count)]
    return jnp.concatenate([x[:, i * width : (i + 1) * width] for i in order], axis=1)


ROWS = 16


def over_rows(number, body, carry=None):
    def step(i, carry):
        return body(pl.multiple_of(i * ROWS, ROWS), carry)

    return lax.fori_loop(0, number // ROWS, step, carry)


def row_scale(x):
    return lax.rsqrt(jnp.mean(x * x, axis=-1, keepdims=True) + eps)


def entry_kernel(count, tok_ref, cot_ref, gain_ref, h_ref, x_ref, c_ref):
    def body(at, carry):
        rows = pl.ds(at, ROWS)
        x = natural_columns(tok_ref[rows, :], count)
        x_ref[rows, :] = x
        wide = x.astype(F32)
        h_ref[rows, :] = (wide * row_scale(wide) * gain_ref[...]).astype(BF16)
        c_ref[rows, :] = natural_columns(cot_ref[rows, :], count)
        return carry

    over_rows(tok_ref.shape[0], body, 0)


def sum_terms(refs, rows):
    total = refs[0][rows, :].astype(F32)
    for ref in refs[1:]:
        total = total + ref[rows, :].astype(F32)
    return total


def middle_kernel(lows, highs, *refs):
    x_ref, gain_ref, x2_ref, h_ref = refs[0], refs[1], refs[-2], refs[-1]
    block = x_ref.shape[0] // 2
    for half, terms in ((0, refs[2 : 2 + lows]), (1, refs[2 + lows : 2 + lows + highs])):

        def body(at, carry):
            rows = pl.ds(half * block + at, ROWS)
            x2 = x_ref[rows, :].astype(F32) + sum_terms(terms, pl.ds(at, ROWS))
            x2_ref[rows, :] = x2
            h_ref[rows, :] = (x2 * row_scale(x2) * gain_ref[...]).astype(BF16)
            return carry

        over_rows(block, body, 0)


def result_kernel(lows, highs, count, *refs):
    x_ref, out_ref = refs[0], refs[-1]
    block = x_ref.shape[0] // 2
    for half, terms in ((0, refs[1 : 1 + lows]), (1, refs[1 + lows : 1 + lows + highs])):

        def body(at, carry):
            rows = pl.ds(half * block + at, ROWS)
            total = x_ref[rows, :] + sum_terms(terms, pl.ds(at, ROWS))
            out_ref[rows, :] = natural_columns(total, count).astype(BF16)
            return carry

        over_rows(block, body, 0)


def back_kernel(lows, highs, count, *refs):
    base_ref, x_ref, gain_ref = refs[:3]
    wide_ref, gain_out = refs[3 + lows + highs], refs[-1]
    low_ref = refs[4 + lows + highs] if count is None else None
    block = x_ref.shape[0] // 2
    total = jnp.zeros((ROWS, x_ref.shape[1]), F32)
    for half, terms in ((0, refs[3 : 3 + lows]), (1, refs[3 + lows : 3 + lows + highs])):

        def body(at, carry):
            rows = pl.ds(half * block + at, ROWS)
            grad = sum_terms(terms, pl.ds(at, ROWS))
            x = x_ref[rows, :].astype(F32)
            scale = row_scale(x)
            unit = x * scale
            scaled = grad * gain_ref[...]
            out = base_ref[rows, :].astype(F32) + scale * (
                scaled - unit * jnp.mean(scaled * unit, axis=-1, keepdims=True)
            )
            if count is None:
                wide_ref[rows, :] = out
                low_ref[rows, :] = out.astype(BF16)
            else:
                wide_ref[rows, :] = natural_columns(out, count)
            return carry + grad * unit

        total = over_rows(block, body, total)
    gain_out[...] = jnp.sum(total, axis=0, keepdims=True)


def row_pass(kernel, args, outs, name):
    return pl.pallas_call(
        kernel,
        out_shape=outs,
        compiler_params=vmem_limit(40),
        cost_estimate=pl.CostEstimate(
            flops=10 * args[0].size, bytes_accessed=10 * args[0].size, transcendentals=0
        ),
        name=name,
    )(*args)


def pair_columns(weights, pair, ways):
    shares = []
    for place in (pair, 1 - pair):
        parts = []
        for weight in weights:
            columns = weight.shape[1] // ways
            parts.append(lax.dynamic_slice_in_dim(weight, place * columns, columns, 1))
        shares.append(jnp.concatenate(parts, axis=1))
    return shares


def swap_shards(mine, theirs, pair):
    theirs = xor_send(theirs, "ctx", 2)
    return jnp.concatenate(
        [jnp.where(pair == 0, mine, theirs), jnp.where(pair == 0, theirs, mine)], axis=0
    )


def ctx_gather(rows, ways):
    groups = pair_groups(lax.axis_size("ctx")) if ways == 2 else None
    return lax.all_gather(rows, "ctx", axis=0, tiled=True, axis_index_groups=groups)


def ctx_scatter(rows, ways):
    groups = pair_groups(lax.axis_size("ctx")) if ways == 2 else None
    return lax.psum_scatter(
        rows, "ctx", scatter_dimension=0, tiled=True, axis_index_groups=groups
    )


def gather_weight(shard, ways):
    full = ctx_gather(shard, ways)
    return swap_blocks(full, lax.axis_size("ctx"), 0) if ways == 1 else full


def scatter_weight(grad, ways):
    if ways == 1:
        grad = swap_blocks(grad, lax.axis_size("ctx"), 0)
    return ctx_scatter(grad, ways)


def own_rows(both, pair, ways):
    if ways == 1:
        return both.astype(F32)
    rows = both.shape[0] // 2
    kept = lax.dynamic_slice_in_dim(both, pair * rows, rows, 0)
    other = xor_send(lax.dynamic_slice_in_dim(both, (1 - pair) * rows, rows, 0), "ctx", 2)
    low, high = jnp.where(pair == 0, kept, other), jnp.where(pair == 0, other, kept)
    return jnp.concatenate([low, high], axis=1).astype(F32)


def butterfly_sum(value):
    for axis in ("ctx", "fsdp"):
        step = 1
        while step < lax.axis_size(axis):
            value = value + xor_send(value, axis, step)
            step *= 2
    return value


def dot(left, right):
    return jnp.dot(left, right, preferred_element_type=F32)


def dot_rows(left, right):
    return lax.dot_general(left, right, (((0,), (0,)), ((), ())), preferred_element_type=F32)


def dot_cols(left, right):
    return lax.dot_general(left, right, (((1,), (1,)), ((), ())), preferred_element_type=F32)


def vmem_limit(mib):
    return pltpu.CompilerParams(vmem_limit_bytes=mib * 1024 * 1024)


def prep_kernel(query_heads, groups, raw_ref, cos_ref, sin_ref, gq_ref, gk_ref, q_ref, kv_ref):
    cos = cos_ref[...]
    sin = sin_ref[...]

    def rotate_norm(x, gain):
        scale = lax.rsqrt(jnp.mean(x * x, axis=-1, keepdims=True) + eps)
        u = x * scale * gain
        return u * cos + pltpu.roll(u, HD // 2, 1) * sin

    for h in range(query_heads):
        cols = slice(h * HD, (h + 1) * HD)
        q_ref[:, cols] = rotate_norm(raw_ref[:, cols], gq_ref[...]).astype(BF16)
    for h in range(2 * groups):
        x = raw_ref[:, (query_heads + h) * HD : (query_heads + h + 1) * HD]
        if h % 2 == 0:
            x = rotate_norm(x, gk_ref[...])
        kv_ref[:, h * HD : (h + 1) * HD] = x.astype(BF16)


def head_prep(raw, cos, sin, gq, gk, query_heads, groups):
    rows, width = raw.shape
    tile = 256
    vec = pl.BlockSpec((1, HD), lambda i: (0, 0))
    tab = pl.BlockSpec((tile, HD), lambda i: (i, 0))
    return pl.pallas_call(
        functools.partial(prep_kernel, query_heads, groups),
        out_shape=(
            jax.ShapeDtypeStruct((rows, query_heads * HD), BF16),
            jax.ShapeDtypeStruct((rows, 2 * groups * HD), BF16),
        ),
        grid=(rows // tile,),
        in_specs=[pl.BlockSpec((tile, width), lambda i: (i, 0)), tab, tab, vec, vec],
        out_specs=(
            pl.BlockSpec((tile, query_heads * HD), lambda i: (i, 0)),
            pl.BlockSpec((tile, 2 * groups * HD), lambda i: (i, 0)),
        ),
        cost_estimate=pl.CostEstimate(
            flops=20 * raw.size, bytes_accessed=6 * raw.size, transcendentals=0
        ),
        name="head_prep",
    )(raw, cos, sin, gq, gk)


def prep_back_kernel(heads, plain, d_ref, raw_ref, cos_ref, sin_ref, g_ref, out_ref, gain_ref):
    cos = cos_ref[...]
    sin = sin_ref[...]
    gain = g_ref[...]
    gain_sum = jnp.zeros((1, HD), F32)
    for h in range(heads):
        cols = slice(h * HD, (h + 1) * HD)
        d = d_ref[:, cols]
        if plain and h % 2 == 1:
            out_ref[:, cols] = d.astype(BF16)
            continue
        x = raw_ref[:, cols]
        t = d * cos - pltpu.roll(d, HD // 2, 1) * sin
        scale = lax.rsqrt(jnp.mean(x * x, axis=-1, keepdims=True) + eps)
        n = x * scale
        gain_sum = gain_sum + jnp.sum(t * n, axis=0, keepdims=True)
        e = t * gain
        out_ref[:, cols] = (scale * (e - n * jnp.mean(e * n, axis=-1, keepdims=True))).astype(BF16)

    @pl.when(pl.program_id(0) == 0)
    def _():
        gain_ref[...] = jnp.zeros_like(gain_ref)

    gain_ref[...] += gain_sum


def head_prep_back(grad, raw, cos, sin, gain, raw_block, plain):
    rows, width = grad.shape
    tile = 256
    tab = pl.BlockSpec((tile, HD), lambda i: (i, 0))
    return pl.pallas_call(
        functools.partial(prep_back_kernel, width // HD, plain),
        out_shape=(
            jax.ShapeDtypeStruct((rows, width), BF16),
            jax.ShapeDtypeStruct((1, HD), F32),
        ),
        grid=(rows // tile,),
        in_specs=[
            pl.BlockSpec((tile, width), lambda i: (i, 0)),
            pl.BlockSpec((tile, width), lambda i: (i, raw_block)),
            tab,
            tab,
            pl.BlockSpec((1, HD), lambda i: (0, 0)),
        ],
        out_specs=(
            pl.BlockSpec((tile, width), lambda i: (i, 0)),
            pl.BlockSpec((1, HD), lambda i: (0, 0)),
        ),
        cost_estimate=pl.CostEstimate(
            flops=20 * rows * width, bytes_accessed=10 * rows * width, transcendentals=0
        ),
        name="head_prep_back",
    )(grad, raw, cos, sin, gain)


def block_place(pair, shard, place, ways, count):
    owner = shard
    if ways == 2:
        other = (pair + place % 2) % 2 if isinstance(pair, int) else lax.rem(pair + place % 2, 2)
        owner = (shard // 2) * 4 + 2 * other + shard % 2
    return owner if place < ways else 2 * count - 1 - owner


def load_sequence(pair, ways, kv_ref, keys, values):
    shards, _, _, block, _ = kv_ref.shape
    for shard in range(shards):
        for place in range(2 * ways):
            index = block_place(pair, shard, place, ways, shards * ways)
            rows = pl.ds(pl.multiple_of(index * block, block), block)
            keys[rows, :] = kv_ref[shard, 0, place, :, :HD]
            values[rows, :] = kv_ref[shard, 0, place, :, HD:]


def stack_heads(tile, count):
    return jnp.concatenate([tile[:, h * HD : (h + 1) * HD] for h in range(count)], axis=0)


def row_positions(info_ref, place, block, count):
    base = pl.program_id(0) * (info_ref.shape[0] // pl.num_programs(0)) + 1 + 3 * place
    first = info_ref[base]
    lane = lax.broadcasted_iota(jnp.int32, (1, count * block), 1)
    position = first + lax.rem(lane, block)
    start_first, start_last = info_ref[base + 1], info_ref[base + 2]
    start = jnp.where(position >= start_last, start_last, start_first)
    return position, start, start_first // CHUNK, (first + block - 1) // CHUNK + 1


def valid_tile(chunk, position, start, shape):
    key_index = chunk * CHUNK + lax.broadcasted_iota(jnp.int32, shape, 0)
    return (key_index <= position) & (key_index >= start)


def forward_kernel(ways, count, info_ref, q_ref, kv_ref, o_ref, lse_ref, keys, values):
    load_sequence(info_ref[0], ways, kv_ref, keys, values)
    block = q_ref.shape[2]
    columns = count * block
    for place in range(2 * ways):
        queries = stack_heads(q_ref[0, place], count)
        position, start, low, high = row_positions(info_ref, place, block, count)

        def body(chunk, carry):
            total, norm = carry
            rows = pl.ds(pl.multiple_of(chunk * CHUNK, CHUNK), CHUNK)
            score = dot_cols(keys[rows, :], queries)
            weight = jnp.where(
                valid_tile(chunk, position, start, score.shape), jnp.exp2(score * EXP2_SCALE), 0.0
            )
            norm = norm + jnp.sum(weight, axis=0, keepdims=True)
            total = total + dot_rows(values[rows, :], weight.astype(BF16))
            return total, norm

        total, norm = lax.fori_loop(
            low, high, body, (jnp.zeros((HD, columns), F32), jnp.zeros((1, columns), F32))
        )
        out = (total / norm).T.astype(BF16)
        for h in range(count):
            o_ref[0, place, :, h * HD : (h + 1) * HD] = out[h * block : (h + 1) * block]
        lse_ref[0, 0, place] = jnp.log2(norm)


def backward_kernel(
    ways, count, info_ref, q_ref, do_ref, o_ref, lse_ref, kv_ref,
    dq_ref, dkv_ref, keys, values, grad_k, grad_v,
):
    pair = info_ref[0]
    load_sequence(pair, ways, kv_ref, keys, values)
    block = q_ref.shape[2]
    columns = count * block
    grad_k[...] = jnp.zeros_like(grad_k)
    grad_v[...] = jnp.zeros_like(grad_v)
    for place in range(2 * ways):
        queries = stack_heads(q_ref[0, place], count)
        grads = stack_heads(do_ref[0, place], count)
        outs = stack_heads(o_ref[0, place], count)
        delta = jnp.sum((grads.astype(F32) * outs.astype(F32)).T, axis=0, keepdims=True)
        lse = lse_ref[0, 0, place]
        position, start, low, high = row_positions(info_ref, place, block, count)

        def body(chunk, total):
            rows = pl.ds(pl.multiple_of(chunk * CHUNK, CHUNK), CHUNK)
            key_rows = keys[rows, :]
            score = dot_cols(key_rows, queries)
            prob = jnp.where(
                valid_tile(chunk, position, start, score.shape),
                jnp.exp2(score * EXP2_SCALE - lse),
                0.0,
            )
            grad_prob = dot_cols(values[rows, :], grads)
            grad_score = (prob * (grad_prob - delta)).astype(BF16)
            grad_v[rows, :] += dot(prob.astype(BF16), grads)
            grad_k[rows, :] += dot(grad_score, queries)
            return total + dot_rows(key_rows, grad_score)

        total = lax.fori_loop(low, high, body, jnp.zeros((HD, columns), F32))
        out = total.T * SCALE
        for h in range(count):
            dq_ref[0, place, :, h * HD : (h + 1) * HD] = out[h * block : (h + 1) * block]
    shards = dkv_ref.shape[0]
    for shard in range(shards):
        for place in range(2 * ways):
            index = block_place(pair, shard, place, ways, shards * ways)
            rows = pl.ds(pl.multiple_of(index * block, block), block)
            dkv_ref[shard, 0, place, :, :HD] = (grad_k[rows, :] * SCALE).astype(BF16)
            dkv_ref[shard, 0, place, :, HD:] = grad_v[rows, :].astype(BF16)


def attention_specs(q, kv, count):
    shards, sequences, places, block, width = kv.shape
    row = pl.BlockSpec((1, places, block, count * HD), lambda s, n, i: (s, 0, 0, n))
    part = pl.BlockSpec((shards, 1, places, block, 2 * HD), lambda s, n, i: (0, s, 0, 0, n))
    sums = pl.BlockSpec((1, 1, places, 1, count * block), lambda s, n, i: (s, n, 0, 0, 0))
    sums_shape = (sequences, width // (2 * HD), places, 1, count * block)
    return row, part, sums, sums_shape, shards * places * block


def attend(info, q, kv, count, ways):
    row, part, sums, sums_shape, length = attention_specs(q, kv, count)
    return pl.pallas_call(
        functools.partial(forward_kernel, ways, count),
        out_shape=(
            jax.ShapeDtypeStruct(q.shape, BF16),
            jax.ShapeDtypeStruct(sums_shape, F32),
        ),
        grid_spec=pltpu.PrefetchScalarGridSpec(
            num_scalar_prefetch=1,
            grid=sums_shape[:2],
            in_specs=[row, part],
            out_specs=(row, sums),
            scratch_shapes=[pltpu.VMEM((length, HD), BF16)] * 2,
        ),
        compiler_params=vmem_limit(48),
        cost_estimate=pl.CostEstimate(
            flops=4 * 8 * CHUNK * q.size, bytes_accessed=2 * kv.size, transcendentals=0
        ),
        name="attend",
    )(info, q, kv)


def attend_back(info, q, grad, out, lse, kv, count, ways):
    row, part, sums, sums_shape, length = attention_specs(q, kv, count)
    return pl.pallas_call(
        functools.partial(backward_kernel, ways, count),
        out_shape=(
            jax.ShapeDtypeStruct(q.shape, F32),
            jax.ShapeDtypeStruct(kv.shape, BF16),
        ),
        grid_spec=pltpu.PrefetchScalarGridSpec(
            num_scalar_prefetch=1,
            grid=sums_shape[:2],
            in_specs=[row, row, row, sums, part],
            out_specs=(row, part),
            scratch_shapes=[pltpu.VMEM((length, HD), BF16)] * 2
            + [pltpu.VMEM((length, HD), F32)] * 2,
        ),
        compiler_params=vmem_limit(56),
        cost_estimate=pl.CostEstimate(
            flops=10 * 8 * CHUNK * q.size, bytes_accessed=4 * kv.size, transcendentals=0
        ),
        name="attend_back",
    )(info, q, grad, out, lse, kv)


def interleave_heads(first, second):
    rows, width = first.shape
    heads = width // HD
    both = jnp.stack([first.reshape(rows, heads, HD), second.reshape(rows, heads, HD)], axis=2)
    return both.reshape(rows, 2 * width)


def after(value, earlier):
    return lax.optimization_barrier((value, earlier))[0]


def local(
    tokens,
    grad_out,
    segments,
    w_query,
    key_weight_matrix,
    value_weight_matrix,
    w_output,
    w_gate,
    w_up,
    w_down,
    norm_attn,
    norm_mlp,
    norm_query,
    norm_key,
):
    ctx_count = lax.axis_size("ctx")
    seq_count = lax.axis_size("fsdp")
    me = lax.axis_index("ctx").astype(jnp.int32)
    my_seq = lax.axis_index("fsdp").astype(jnp.int32)
    pair = lax.rem(me // 2, 2)
    block = tokens.shape[3]
    width = tokens.shape[4]
    own = 2 * block
    ways = 2 if (key_weight_matrix.shape[1] // HD) % 2 == 0 else 1
    query_heads = w_query.shape[1] // HD // ways
    groups = key_weight_matrix.shape[1] // HD // ways
    count = query_heads // groups
    q_width, kv_width = query_heads * HD, 2 * groups * HD
    hidden = w_gate.shape[1] // 2

    w_kv = interleave_heads(key_weight_matrix, value_weight_matrix)
    gain_attn_row = swap_blocks(norm_attn[None], ctx_count, 1)
    gain_mlp_row = swap_blocks(norm_mlp[None], ctx_count, 1)

    qkv_width = q_width + kv_width
    if ways == 2:
        early = swap_shards(*pair_columns([w_query, w_kv, w_output], pair, 2), pair)
        qkv_shard, output_shard = early[:, :qkv_width], early[:, qkv_width:]
    else:
        qkv_shard, output_shard = jnp.concatenate([w_query, w_kv], axis=1), w_output
    full_qkv = gather_weight(qkv_shard, ways)
    full_output = gather_weight(output_shard, ways)

    row_bf16 = jax.ShapeDtypeStruct((own, width), BF16)
    row_f32 = jax.ShapeDtypeStruct((own, width), F32)
    gain_shape = jax.ShapeDtypeStruct((1, width), F32)
    h1_own, inputs, cot_own = row_pass(
        functools.partial(entry_kernel, ctx_count),
        (tokens.reshape(own, width), grad_out.reshape(own, width), gain_attn_row),
        (row_bf16, row_bf16, row_bf16),
        "entry",
    )
    h1 = gather_rows(h1_own, ways)

    offsets = jnp.arange(block, dtype=jnp.int32)
    owners = [me, me + 2 - 4 * pair][:ways]
    firsts = [o * block for o in owners + [2 * ctx_count - 1 - o for o in owners]]
    freq = jnp.exp(jnp.arange(HD // 2, dtype=F32) * (-2.0 * math.log(rope_base) / HD))
    infos, positions = [], []
    for r in range(seq_count):
        line = lax.dynamic_index_in_dim(
            segments, lax.bitwise_xor(my_seq, jnp.int32(r)), 0, keepdims=False
        )
        doc_first = [jnp.sum((line < d).astype(jnp.int32)) for d in range(DOCS)]
        scalars = [pair]
        for first in firsts:
            mine = lax.dynamic_slice_in_dim(line, first, block)
            start = sum(jnp.where(mine == d, doc_first[d], 0) for d in range(DOCS))
            scalars += [first, start[0], start[block - 1]]
            positions.append(first + offsets - start)
        infos += scalars
    info = jnp.stack(infos)
    angle = jnp.concatenate(positions).astype(F32)[:, None] * freq
    cos, sin = jnp.cos(angle), jnp.sin(angle)
    cos, sin = jnp.concatenate([cos, cos], 1), jnp.concatenate([-sin, sin], 1)
    gain_q, gain_k = norm_query.reshape(1, HD), norm_key.reshape(1, HD)

    raw = dot(h1, full_qkv)
    q, kv = head_prep(raw, cos, sin, gain_q, gain_k, query_heads, groups)
    q = q.reshape(seq_count, 2 * ways, block, q_width)

    mine, theirs = pair_columns([w_gate, w_up, w_down], pair, 2)
    shards = swap_shards(mine, after(theirs, h1), pair)
    full_kv = ctx_gather(after(kv, full_output), ways).reshape(-1, seq_count, 2 * ways, block, kv_width)
    shards = after(shards, kv)
    full_gate, full_up, full_down = (
        gather_weight(shards[:, i * hidden : (i + 1) * hidden], 2) for i in range(3)
    )
    cot_all = gather_rows(after(cot_own, shards), 2)

    q = after(q, cot_all)
    heads, lse = attend(info, q, full_kv, count, ways)
    mixed = heads.reshape(-1, q_width)
    lows, highs = return_rows(dot_cols(mixed, full_output).astype(BF16), ways)
    x2, h2_own = row_pass(
        functools.partial(middle_kernel, len(lows), len(highs)),
        (inputs, gain_mlp_row, *lows, *highs),
        (row_f32, row_bf16),
        "middle",
    )
    h2 = gather_rows(h2_own, 2)

    gate = dot(h2, full_gate)
    up = dot(h2, full_up)
    act = lax.optimization_barrier((gate / (1.0 + jnp.exp(-gate)) * up).astype(BF16))
    grad_down = dot_rows(cot_all, act).astype(BF16)
    d_act = dot(after(cot_all, grad_down), full_down)
    sg = 1.0 / (1.0 + jnp.exp(-gate))
    d_gate = (d_act * up * sg * (1.0 + gate * (1.0 - sg))).astype(BF16)
    d_up = (d_act * gate * sg).astype(BF16)
    d_h2_part = (dot_cols(d_gate, full_gate) + dot_cols(d_up, full_up)).astype(BF16)
    lows, highs = return_rows(d_h2_part, 2)
    h2_late, act_late = after((h2, act), d_h2_part)
    grad_gate = dot_rows(h2_late, d_gate).astype(BF16)
    grad_up = dot_rows(h2_late, d_up).astype(BF16)
    y_part = dot_cols(act_late, full_down).astype(BF16)
    lows[0] = after(lows[0], (grad_gate, grad_up, y_part))
    d_x2, d_x2_low, gain_mlp = row_pass(
        functools.partial(back_kernel, len(lows), len(highs), None),
        (cot_own, x2, gain_mlp_row, *lows, *highs),
        (row_f32, row_bf16, gain_shape),
        "middle_back",
    )
    branch = gather_rows(d_x2_low, ways)
    rows_down = scatter_weight(grad_down, 2)
    rows_gate = scatter_weight(after(grad_gate, rows_down), 2)
    grad_output = after(dot_rows(branch, mixed).astype(BF16), rows_gate)
    rows_output = scatter_weight(grad_output, ways)
    d_att = dot(branch, full_output).astype(BF16).reshape(q.shape)

    lows, highs = return_rows(after(y_part, branch), 2)
    out_tokens = row_pass(
        functools.partial(result_kernel, len(lows), len(highs), ctx_count),
        (x2, *lows, *highs),
        row_bf16,
        "result",
    ).reshape(tokens.shape)

    d_q, d_kv = attend_back(info, q, d_att, heads, lse, full_kv, count, ways)
    d_kv = after(d_kv.reshape(-1, kv_width), rows_output)
    d_kv = ctx_scatter(d_kv, ways).astype(F32)
    shard_down = own_rows(rows_down, pair, 2)
    shard_gate = own_rows(rows_gate, pair, 2)
    shard_output = own_rows(rows_output, pair, ways)
    d_kv = after(d_kv, (out_tokens, shard_down, shard_gate, shard_output))
    d_qp, gain_q_sum = head_prep_back(
        d_q.reshape(-1, q_width), raw, cos, sin, gain_q, 0, False
    )
    d_kvp, gain_k_sum = head_prep_back(d_kv, raw, cos, sin, gain_k, q_width // kv_width, True)
    d_h1 = (
        dot_cols(d_qp, full_qkv[:, :q_width]) + dot_cols(d_kvp, full_qkv[:, q_width:])
    ).astype(BF16)
    lows, highs = return_rows(d_h1, ways)
    d_raw = jnp.concatenate([d_qp, d_kvp], axis=1)
    grad_qkv = dot_rows(after(h1, d_h1), d_raw).astype(BF16)

    rows_up = scatter_weight(grad_up, 2)
    rows_qkv = scatter_weight(grad_qkv, ways)
    grad_tokens, gain_attn = row_pass(
        functools.partial(back_kernel, len(lows), len(highs), ctx_count),
        (d_x2, inputs, gain_attn_row, *lows, *highs),
        (row_f32, gain_shape),
        "entry_back",
    )
    rows_up, rows_qkv = after((rows_up, rows_qkv), gain_attn)
    shard_up = own_rows(rows_up, pair, 2)
    shard_query = own_rows(rows_qkv[:, :q_width], pair, ways)
    shard_kv = own_rows(rows_qkv[:, q_width:], pair, ways)
    shard_kv = shard_kv.reshape(shard_kv.shape[0], -1, 2, HD)
    grad_tokens = grad_tokens.reshape(tokens.shape)
    gains = butterfly_sum(
        jnp.concatenate([gain_attn[0], gain_mlp[0], gain_q_sum[0], gain_k_sum[0]])
    )
    return (
        out_tokens,
        grad_tokens,
        shard_query,
        shard_kv[:, :, 0].reshape(key_weight_matrix.shape),
        shard_kv[:, :, 1].reshape(value_weight_matrix.shape),
        shard_output,
        shard_gate,
        shard_up,
        shard_down,
        swap_blocks(gains[None, :width], ctx_count, 1)[0],
        swap_blocks(gains[None, width : 2 * width], ctx_count, 1)[0],
        gains[2 * width : 2 * width + HD],
        gains[2 * width + HD :],
    )


def solution(mesh):
    block = P("fsdp", "ctx", None, None, None)
    weight = P("ctx", "fsdp")
    return jax.shard_map(
        local,
        mesh=mesh,
        in_specs=(block, block, P()) + (weight,) * 7 + (P(),) * 4,
        out_specs=(block, block) + (weight,) * 7 + (P(),) * 4,
        check_vma=False,
    )
```

```python
import functools
import math

import jax
import jax.numpy as jnp
from jax import lax
from jax.experimental import pallas as pl
from jax.experimental.pallas import tpu as pltpu
from jax.sharding import PartitionSpec as P

QUERY_HEADS = 16
KEY_VALUE_HEADS = 8
HD = 128
DOCS = 4
CHUNK = 256
eps = 1e-06
rope_base = 1000000.0
SCALE = HD ** (-0.5)
EXP2_SCALE = SCALE * math.log2(math.e)
F32 = jnp.float32
BF16 = jnp.bfloat16


def xor_send(value, axis, step):
    count = lax.axis_size(axis)
    return lax.ppermute(value, axis, [(i, i ^ step) for i in range(count)])


def exchange_rows(rows, axis):
    return [rows] + [xor_send(rows, axis, r) for r in range(1, lax.axis_size(axis))]


def scatter_rows(partial, axis):
    count = lax.axis_size(axis)
    rows = partial.shape[0] // count
    total = partial[:rows].astype(F32)
    for r in range(1, count):
        total = total + xor_send(partial[r * rows : (r + 1) * rows], axis, r).astype(F32)
    return total


def pair_groups(count):
    return [[i for i in range(count) if (i >> 1) & 1 == bit] for bit in (0, 1)]


def swap_blocks(x, count, axis):
    shape = x.shape
    split = x.reshape(shape[:axis] + (count // 4, 2, 2, shape[axis] // count) + shape[axis + 1 :])
    return split.swapaxes(axis + 1, axis + 2).reshape(shape)


def assemble_kernel(plan, *refs):
    out_ref = refs[-1]
    place = 0
    for index, start, number in plan:
        out_ref[place : place + number, :] = refs[index][start : start + number, :]
        place += number


def assemble(arrays, plan):
    width = arrays[0].shape[1]
    rows = sum(number for _, _, number in plan)
    return pl.pallas_call(
        functools.partial(assemble_kernel, plan),
        out_shape=jax.ShapeDtypeStruct((rows, width), arrays[0].dtype),
        compiler_params=vmem_limit(32),
        cost_estimate=pl.CostEstimate(
            flops=0, bytes_accessed=4 * rows * width, transcendentals=0
        ),
        name="assemble",
    )(*arrays)


def gather_rows(rows, ways):
    count = lax.axis_size("fsdp")
    total = rows.shape[0]
    if ways == 1:
        return assemble(exchange_rows(rows, "fsdp"), [(r, 0, total) for r in range(count)])
    block = total // 2
    low = rows[:block]
    lows = exchange_rows(low, "fsdp")
    high = jnp.concatenate([rows[block:], xor_send(rows[block:], "ctx", 2)], axis=0)
    highs = exchange_rows(high, "fsdp")
    others = xor_send(jnp.concatenate(lows, axis=0), "ctx", 2)
    plan = []
    for r in range(count):
        plan += [(1 + r, 0, block), (0, r * block, block), (1 + count + r, 0, 2 * block)]
    return assemble([others] + lows + highs, plan)


def return_rows(partial, ways, filler=None):
    count = lax.axis_size("fsdp")
    if ways == 1:
        rows = partial.shape[0] // count
        terms = [partial[:rows]] + [
            xor_send(partial[r * rows : (r + 1) * rows], "fsdp", r) for r in range(1, count)
        ]
        return [t[: rows // 2] for t in terms], [t[rows // 2 :] for t in terms]
    block = partial.shape[0] // (4 * count)

    def rows(start, number):
        return partial[start * block : (start + number) * block]

    sent = jnp.concatenate([rows(4 * r + 1, 1) for r in range(count)], axis=0)
    pairs = [xor_send(rows(4 * r + 2, 2), "fsdp", r) for r in range(1, count)]
    other = xor_send(sent, "ctx", 2)
    if filler is not None:
        other = after(other, filler)
    first = [
        (rows(4 * r, 1).astype(F32) + other[r * block : (r + 1) * block].astype(F32)).astype(BF16)
        for r in range(count)
    ]
    second = rows(2, 2).astype(F32)
    for term in pairs:
        second = second + term.astype(F32)
    second = second.astype(BF16)
    lows = [first[0]] + [xor_send(first[r], "fsdp", r) for r in range(1, count)]
    return lows, [second[:block], xor_send(second[block:], "ctx", 2)]


def natural_columns(x, count):
    width = x.shape[1] // count
    order = [(i & ~3) | ((i & 1) << 1) | ((i >> 1) & 1) for i in range(count)]
    return jnp.concatenate([x[:, i * width : (i + 1) * width] for i in order], axis=1)


ROWS = 16


def over_rows(number, body, carry=None):
    def step(i, carry):
        return body(pl.multiple_of(i * ROWS, ROWS), carry)

    return lax.fori_loop(0, number // ROWS, step, carry)


def row_scale(x):
    return lax.rsqrt(jnp.mean(x * x, axis=-1, keepdims=True) + eps)


def entry_kernel(count, tok_ref, cot_ref, gain_ref, h_ref, x_ref, c_ref):
    def body(at, carry):
        rows = pl.ds(at, ROWS)
        x = natural_columns(tok_ref[rows, :], count)
        x_ref[rows, :] = x
        wide = x.astype(F32)
        h_ref[rows, :] = (wide * row_scale(wide) * gain_ref[...]).astype(BF16)
        c_ref[rows, :] = natural_columns(cot_ref[rows, :], count)
        return carry

    over_rows(tok_ref.shape[0], body, 0)


def sum_terms(refs, rows):
    total = refs[0][rows, :].astype(F32)
    for ref in refs[1:]:
        total = total + ref[rows, :].astype(F32)
    return total


def middle_kernel(lows, highs, *refs):
    x_ref, gain_ref, x2_ref, h_ref = refs[0], refs[1], refs[-2], refs[-1]
    block = x_ref.shape[0] // 2
    for half, terms in ((0, refs[2 : 2 + lows]), (1, refs[2 + lows : 2 + lows + highs])):

        def body(at, carry):
            rows = pl.ds(half * block + at, ROWS)
            x2 = x_ref[rows, :].astype(F32) + sum_terms(terms, pl.ds(at, ROWS))
            x2_ref[rows, :] = x2
            h_ref[rows, :] = (x2 * row_scale(x2) * gain_ref[...]).astype(BF16)
            return carry

        over_rows(block, body, 0)


def result_kernel(lows, highs, count, *refs):
    x_ref, out_ref = refs[0], refs[-1]
    block = x_ref.shape[0] // 2
    for half, terms in ((0, refs[1 : 1 + lows]), (1, refs[1 + lows : 1 + lows + highs])):

        def body(at, carry):
            rows = pl.ds(half * block + at, ROWS)
            total = x_ref[rows, :] + sum_terms(terms, pl.ds(at, ROWS))
            out_ref[rows, :] = natural_columns(total, count).astype(BF16)
            return carry

        over_rows(block, body, 0)


def back_kernel(lows, highs, count, *refs):
    base_ref, x_ref, gain_ref = refs[:3]
    wide_ref, gain_out = refs[3 + lows + highs], refs[-1]
    low_ref = refs[4 + lows + highs] if count is None else None
    block = x_ref.shape[0] // 2
    total = jnp.zeros((ROWS, x_ref.shape[1]), F32)
    for half, terms in ((0, refs[3 : 3 + lows]), (1, refs[3 + lows : 3 + lows + highs])):

        def body(at, carry):
            rows = pl.ds(half * block + at, ROWS)
            grad = sum_terms(terms, pl.ds(at, ROWS))
            x = x_ref[rows, :].astype(F32)
            scale = row_scale(x)
            unit = x * scale
            scaled = grad * gain_ref[...]
            out = base_ref[rows, :].astype(F32) + scale * (
                scaled - unit * jnp.mean(scaled * unit, axis=-1, keepdims=True)
            )
            if count is None:
                wide_ref[rows, :] = out
                low_ref[rows, :] = out.astype(BF16)
            else:
                wide_ref[rows, :] = natural_columns(out, count)
            return carry + grad * unit

        total = over_rows(block, body, total)
    gain_out[...] = jnp.sum(total, axis=0, keepdims=True)


def row_pass(kernel, args, outs, name):
    return pl.pallas_call(
        kernel,
        out_shape=outs,
        compiler_params=vmem_limit(40),
        cost_estimate=pl.CostEstimate(
            flops=10 * args[0].size, bytes_accessed=10 * args[0].size, transcendentals=0
        ),
        name=name,
    )(*args)


def pair_columns(weights, pair, ways):
    shares = []
    for place in (pair, 1 - pair):
        parts = []
        for weight in weights:
            columns = weight.shape[1] // ways
            parts.append(lax.dynamic_slice_in_dim(weight, place * columns, columns, 1))
        shares.append(jnp.concatenate(parts, axis=1))
    return shares


def swap_shards(mine, theirs, pair):
    theirs = xor_send(theirs, "ctx", 2)
    return jnp.concatenate(
        [jnp.where(pair == 0, mine, theirs), jnp.where(pair == 0, theirs, mine)], axis=0
    )


def ctx_gather(rows, ways):
    groups = pair_groups(lax.axis_size("ctx")) if ways == 2 else None
    return lax.all_gather(rows, "ctx", axis=0, tiled=True, axis_index_groups=groups)


def ctx_scatter(rows, ways):
    groups = pair_groups(lax.axis_size("ctx")) if ways == 2 else None
    return lax.psum_scatter(
        rows, "ctx", scatter_dimension=0, tiled=True, axis_index_groups=groups
    )


def gather_weight(shard, ways):
    full = ctx_gather(shard, ways)
    return swap_blocks(full, lax.axis_size("ctx"), 0) if ways == 1 else full


def scatter_weight(grad, ways):
    if ways == 1:
        grad = swap_blocks(grad, lax.axis_size("ctx"), 0)
    return ctx_scatter(grad, ways)


def own_kernel(plan, pair_ref, both_ref, other_ref, *outs):
    pair = pair_ref[0]
    rows, width = other_ref.shape
    mine = pl.ds(pl.multiple_of(pair * rows, rows), rows)
    for source, columns, target, place in plan:
        half = outs[target].shape[1] // 2
        for ref, at, which in ((both_ref, mine, pair), (other_ref, slice(None), 1 - pair)):
            start = pl.multiple_of(which * half + place, HD)
            outs[target][:, pl.ds(start, columns)] = ref[at, source : source + columns].astype(F32)


def own_rows(both, pair, ways, plan, widths):
    if ways == 1:
        return [
            jnp.concatenate([both[:, s : s + n] for s, n, t, _ in plan if t == i], axis=1).astype(F32)
            for i in range(len(widths))
        ]
    rows = both.shape[0] // 2
    other = xor_send(lax.dynamic_slice_in_dim(both, (1 - pair) * rows, rows, 0), "ctx", 2)
    shapes = tuple(jax.ShapeDtypeStruct((rows, 2 * width), F32) for width in widths)
    whole = [pl.BlockSpec(t.shape, lambda i, m: (0, 0)) for t in (both, other) + shapes]
    return pl.pallas_call(
        functools.partial(own_kernel, plan),
        out_shape=shapes,
        grid_spec=pltpu.PrefetchScalarGridSpec(
            num_scalar_prefetch=1,
            grid=(1,),
            in_specs=whole[:2],
            out_specs=tuple(whole[2:]),
        ),
        cost_estimate=pl.CostEstimate(flops=0, bytes_accessed=8 * both.size, transcendentals=0),
        name="own_rows",
    )(pair.reshape(1), both, other)


def butterfly_sum(value):
    for axis in ("ctx", "fsdp"):
        step = 1
        while step < lax.axis_size(axis):
            value = value + xor_send(value, axis, step)
            step *= 2
    return value


def dot(left, right):
    return jnp.dot(left, right, preferred_element_type=F32)


def dot_rows(left, right):
    return lax.dot_general(left, right, (((0,), (0,)), ((), ())), preferred_element_type=F32)


def dot_cols(left, right):
    return lax.dot_general(left, right, (((1,), (1,)), ((), ())), preferred_element_type=F32)


def vmem_limit(mib):
    return pltpu.CompilerParams(vmem_limit_bytes=mib * 1024 * 1024)


def prep_kernel(query_heads, groups, raw_ref, cos_ref, sin_ref, gq_ref, gk_ref, q_ref, kv_ref):
    cos = cos_ref[...]
    sin = sin_ref[...]

    def rotate_norm(x, gain):
        scale = lax.rsqrt(jnp.mean(x * x, axis=-1, keepdims=True) + eps)
        u = x * scale * gain
        return u * cos + pltpu.roll(u, HD // 2, 1) * sin

    for h in range(query_heads):
        cols = slice(h * HD, (h + 1) * HD)
        q_ref[:, cols] = rotate_norm(raw_ref[:, cols], gq_ref[...]).astype(BF16)
    for h in range(2 * groups):
        x = raw_ref[:, (query_heads + h) * HD : (query_heads + h + 1) * HD]
        if h % 2 == 0:
            x = rotate_norm(x, gk_ref[...])
        kv_ref[:, h * HD : (h + 1) * HD] = x.astype(BF16)


def head_prep(raw, cos, sin, gq, gk, query_heads, groups):
    rows, width = raw.shape
    tile = 256
    vec = pl.BlockSpec((1, HD), lambda i: (0, 0))
    tab = pl.BlockSpec((tile, HD), lambda i: (i, 0))
    return pl.pallas_call(
        functools.partial(prep_kernel, query_heads, groups),
        out_shape=(
            jax.ShapeDtypeStruct((rows, query_heads * HD), BF16),
            jax.ShapeDtypeStruct((rows, 2 * groups * HD), BF16),
        ),
        grid=(rows // tile,),
        in_specs=[pl.BlockSpec((tile, width), lambda i: (i, 0)), tab, tab, vec, vec],
        out_specs=(
            pl.BlockSpec((tile, query_heads * HD), lambda i: (i, 0)),
            pl.BlockSpec((tile, 2 * groups * HD), lambda i: (i, 0)),
        ),
        cost_estimate=pl.CostEstimate(
            flops=20 * raw.size, bytes_accessed=6 * raw.size, transcendentals=0
        ),
        name="head_prep",
    )(raw, cos, sin, gq, gk)


def prep_back_kernel(heads, plain, d_ref, raw_ref, cos_ref, sin_ref, g_ref, out_ref, gain_ref):
    cos = cos_ref[...]
    sin = sin_ref[...]
    gain = g_ref[...]
    gain_sum = jnp.zeros((1, HD), F32)
    for h in range(heads):
        cols = slice(h * HD, (h + 1) * HD)
        d = d_ref[:, cols].astype(F32)
        if plain and h % 2 == 1:
            out_ref[:, cols] = d.astype(BF16)
            continue
        x = raw_ref[:, cols]
        t = d * cos - pltpu.roll(d, HD // 2, 1) * sin
        scale = lax.rsqrt(jnp.mean(x * x, axis=-1, keepdims=True) + eps)
        n = x * scale
        gain_sum = gain_sum + jnp.sum(t * n, axis=0, keepdims=True)
        e = t * gain
        out_ref[:, cols] = (scale * (e - n * jnp.mean(e * n, axis=-1, keepdims=True))).astype(BF16)

    @pl.when(pl.program_id(0) == 0)
    def _():
        gain_ref[...] = jnp.zeros_like(gain_ref)

    gain_ref[...] += gain_sum


def head_prep_back(grad, raw, cos, sin, gain, raw_block, plain):
    rows, width = grad.shape
    tile = 256
    tab = pl.BlockSpec((tile, HD), lambda i: (i, 0))
    return pl.pallas_call(
        functools.partial(prep_back_kernel, width // HD, plain),
        out_shape=(
            jax.ShapeDtypeStruct((rows, width), BF16),
            jax.ShapeDtypeStruct((1, HD), F32),
        ),
        grid=(rows // tile,),
        in_specs=[
            pl.BlockSpec((tile, width), lambda i: (i, 0)),
            pl.BlockSpec((tile, width), lambda i: (i, raw_block)),
            tab,
            tab,
            pl.BlockSpec((1, HD), lambda i: (0, 0)),
        ],
        out_specs=(
            pl.BlockSpec((tile, width), lambda i: (i, 0)),
            pl.BlockSpec((1, HD), lambda i: (0, 0)),
        ),
        cost_estimate=pl.CostEstimate(
            flops=20 * rows * width, bytes_accessed=10 * rows * width, transcendentals=0
        ),
        name="head_prep_back",
    )(grad, raw, cos, sin, gain)


def block_place(pair, shard, place, ways, count):
    owner = shard
    if ways == 2:
        other = (pair + place % 2) % 2 if isinstance(pair, int) else lax.rem(pair + place % 2, 2)
        owner = (shard // 2) * 4 + 2 * other + shard % 2
    return owner if place < ways else 2 * count - 1 - owner


def load_sequence(pair, ways, kv_ref, keys, values):
    shards, _, _, block, _ = kv_ref.shape
    for shard in range(shards):
        for place in range(2 * ways):
            index = block_place(pair, shard, place, ways, shards * ways)
            rows = pl.ds(pl.multiple_of(index * block, block), block)
            keys[rows, :] = kv_ref[shard, 0, place, :, :HD]
            values[rows, :] = kv_ref[shard, 0, place, :, HD:]


def stack_heads(tile, count):
    return jnp.concatenate([tile[:, h * HD : (h + 1) * HD] for h in range(count)], axis=0)


def row_positions(info_ref, place, block, count):
    base = pl.program_id(0) * (info_ref.shape[0] // pl.num_programs(0)) + 1 + 3 * place
    first = info_ref[base]
    lane = lax.broadcasted_iota(jnp.int32, (1, count * block), 1)
    position = first + lax.rem(lane, block)
    start_first, start_last = info_ref[base + 1], info_ref[base + 2]
    start = jnp.where(position >= start_last, start_last, start_first)
    return position, start, start_first // CHUNK, (first + block - 1) // CHUNK + 1


def valid_tile(chunk, position, start, shape):
    key_index = chunk * CHUNK + lax.broadcasted_iota(jnp.int32, shape, 0)
    return (key_index <= position) & (key_index >= start)


def forward_kernel(ways, count, info_ref, q_ref, kv_ref, o_ref, lse_ref, keys, values):
    load_sequence(info_ref[0], ways, kv_ref, keys, values)
    block = q_ref.shape[2]
    columns = count * block
    for place in range(2 * ways):
        queries = stack_heads(q_ref[0, place], count)
        position, start, low, high = row_positions(info_ref, place, block, count)

        def body(chunk, carry):
            total, norm = carry
            rows = pl.ds(pl.multiple_of(chunk * CHUNK, CHUNK), CHUNK)
            score = dot_cols(keys[rows, :], queries)
            weight = jnp.where(
                valid_tile(chunk, position, start, score.shape), jnp.exp2(score * EXP2_SCALE), 0.0
            )
            norm = norm + jnp.sum(weight, axis=0, keepdims=True)
            total = total + dot_rows(values[rows, :], weight.astype(BF16))
            return total, norm

        total, norm = lax.fori_loop(
            low, high, body, (jnp.zeros((HD, columns), F32), jnp.zeros((1, columns), F32))
        )
        out = (total / norm).T.astype(BF16)
        for h in range(count):
            o_ref[0, place, :, h * HD : (h + 1) * HD] = out[h * block : (h + 1) * block]
        lse_ref[0, 0, place] = jnp.log2(norm)


def backward_kernel(
    ways, count, info_ref, q_ref, do_ref, o_ref, lse_ref, kv_ref,
    dq_ref, dkv_ref, keys, values, grad_k, grad_v,
):
    pair = info_ref[0]
    load_sequence(pair, ways, kv_ref, keys, values)
    block = q_ref.shape[2]
    columns = count * block
    grad_k[...] = jnp.zeros_like(grad_k)
    grad_v[...] = jnp.zeros_like(grad_v)
    for place in range(2 * ways):
        queries = stack_heads(q_ref[0, place], count)
        grads = stack_heads(do_ref[0, place], count)
        outs = stack_heads(o_ref[0, place], count)
        delta = jnp.sum((grads.astype(F32) * outs.astype(F32)).T, axis=0, keepdims=True)
        lse = lse_ref[0, 0, place]
        position, start, low, high = row_positions(info_ref, place, block, count)

        def body(chunk, total):
            rows = pl.ds(pl.multiple_of(chunk * CHUNK, CHUNK), CHUNK)
            key_rows = keys[rows, :]
            score = dot_cols(key_rows, queries)
            prob = jnp.where(
                valid_tile(chunk, position, start, score.shape),
                jnp.exp2(score * EXP2_SCALE - lse),
                0.0,
            )
            grad_prob = dot_cols(values[rows, :], grads)
            grad_score = (prob * (grad_prob - delta)).astype(BF16)
            grad_v[rows, :] += dot(prob.astype(BF16), grads)
            grad_k[rows, :] += dot(grad_score, queries)
            return total + dot_rows(key_rows, grad_score)

        total = lax.fori_loop(low, high, body, jnp.zeros((HD, columns), F32))
        out = total.T * SCALE
        for h in range(count):
            dq_ref[0, place, :, h * HD : (h + 1) * HD] = out[h * block : (h + 1) * block]
    shards = dkv_ref.shape[0]
    for shard in range(shards):
        for place in range(2 * ways):
            index = block_place(pair, shard, place, ways, shards * ways)
            rows = pl.ds(pl.multiple_of(index * block, block), block)
            dkv_ref[shard, 0, place, :, :HD] = (grad_k[rows, :] * SCALE).astype(BF16)
            dkv_ref[shard, 0, place, :, HD:] = grad_v[rows, :].astype(BF16)


def attention_specs(q, kv, count):
    shards, sequences, places, block, width = kv.shape
    row = pl.BlockSpec((1, places, block, count * HD), lambda s, n, i: (s, 0, 0, n))
    part = pl.BlockSpec((shards, 1, places, block, 2 * HD), lambda s, n, i: (0, s, 0, 0, n))
    sums = pl.BlockSpec((1, 1, places, 1, count * block), lambda s, n, i: (s, n, 0, 0, 0))
    sums_shape = (sequences, width // (2 * HD), places, 1, count * block)
    return row, part, sums, sums_shape, shards * places * block


def attend(info, q, kv, count, ways):
    row, part, sums, sums_shape, length = attention_specs(q, kv, count)
    return pl.pallas_call(
        functools.partial(forward_kernel, ways, count),
        out_shape=(
            jax.ShapeDtypeStruct(q.shape, BF16),
            jax.ShapeDtypeStruct(sums_shape, F32),
        ),
        grid_spec=pltpu.PrefetchScalarGridSpec(
            num_scalar_prefetch=1,
            grid=sums_shape[:2],
            in_specs=[row, part],
            out_specs=(row, sums),
            scratch_shapes=[pltpu.VMEM((length, HD), BF16)] * 2,
        ),
        compiler_params=vmem_limit(48),
        cost_estimate=pl.CostEstimate(
            flops=4 * 8 * CHUNK * q.size, bytes_accessed=2 * kv.size, transcendentals=0
        ),
        name="attend",
    )(info, q, kv)


def attend_back(info, q, grad, out, lse, kv, count, ways):
    row, part, sums, sums_shape, length = attention_specs(q, kv, count)
    return pl.pallas_call(
        functools.partial(backward_kernel, ways, count),
        out_shape=(
            jax.ShapeDtypeStruct(q.shape, F32),
            jax.ShapeDtypeStruct(kv.shape, BF16),
        ),
        grid_spec=pltpu.PrefetchScalarGridSpec(
            num_scalar_prefetch=1,
            grid=sums_shape[:2],
            in_specs=[row, row, row, sums, part],
            out_specs=(row, part),
            scratch_shapes=[pltpu.VMEM((length, HD), BF16)] * 2
            + [pltpu.VMEM((length, HD), F32)] * 2,
        ),
        compiler_params=vmem_limit(56),
        cost_estimate=pl.CostEstimate(
            flops=10 * 8 * CHUNK * q.size, bytes_accessed=4 * kv.size, transcendentals=0
        ),
        name="attend_back",
    )(info, q, grad, out, lse, kv)


def interleave_heads(first, second):
    rows, width = first.shape
    heads = width // HD
    both = jnp.stack([first.reshape(rows, heads, HD), second.reshape(rows, heads, HD)], axis=2)
    return both.reshape(rows, 2 * width)


def after(value, earlier):
    return lax.optimization_barrier((value, earlier))[0]


def local(
    tokens,
    grad_out,
    segments,
    w_query,
    key_weight_matrix,
    value_weight_matrix,
    w_output,
    w_gate,
    w_up,
    w_down,
    norm_attn,
    norm_mlp,
    norm_query,
    norm_key,
):
    ctx_count = lax.axis_size("ctx")
    seq_count = lax.axis_size("fsdp")
    me = lax.axis_index("ctx").astype(jnp.int32)
    my_seq = lax.axis_index("fsdp").astype(jnp.int32)
    pair = lax.rem(me // 2, 2)
    block = tokens.shape[3]
    width = tokens.shape[4]
    own = 2 * block
    ways = 2 if (key_weight_matrix.shape[1] // HD) % 2 == 0 else 1
    query_heads = w_query.shape[1] // HD // ways
    groups = key_weight_matrix.shape[1] // HD // ways
    count = query_heads // groups
    q_width, kv_width = query_heads * HD, 2 * groups * HD
    hidden = w_gate.shape[1] // 2

    w_kv = interleave_heads(key_weight_matrix, value_weight_matrix)
    gain_attn_row = swap_blocks(norm_attn[None], ctx_count, 1)
    gain_mlp_row = swap_blocks(norm_mlp[None], ctx_count, 1)

    qkv_width = q_width + kv_width
    if ways == 2:
        early = swap_shards(*pair_columns([w_query, w_kv, w_output], pair, 2), pair)
        qkv_shard, output_shard = early[:, :qkv_width], early[:, qkv_width:]
    else:
        qkv_shard, output_shard = jnp.concatenate([w_query, w_kv], axis=1), w_output
    full_qkv = gather_weight(qkv_shard, ways)
    full_output = gather_weight(output_shard, ways)

    row_bf16 = jax.ShapeDtypeStruct((own, width), BF16)
    row_f32 = jax.ShapeDtypeStruct((own, width), F32)
    gain_shape = jax.ShapeDtypeStruct((1, width), F32)
    h1_own, inputs, cot_own = row_pass(
        functools.partial(entry_kernel, ctx_count),
        (tokens.reshape(own, width), grad_out.reshape(own, width), gain_attn_row),
        (row_bf16, row_bf16, row_bf16),
        "entry",
    )
    h1 = gather_rows(h1_own, ways)

    offsets = jnp.arange(block, dtype=jnp.int32)
    owners = [me, me + 2 - 4 * pair][:ways]
    firsts = [o * block for o in owners + [2 * ctx_count - 1 - o for o in owners]]
    freq = jnp.exp(jnp.arange(HD // 2, dtype=F32) * (-2.0 * math.log(rope_base) / HD))
    infos, positions = [], []
    for r in range(seq_count):
        line = lax.dynamic_index_in_dim(
            segments, lax.bitwise_xor(my_seq, jnp.int32(r)), 0, keepdims=False
        )
        doc_first = [jnp.sum((line < d).astype(jnp.int32)) for d in range(DOCS)]
        scalars = [pair]
        for first in firsts:
            mine = lax.dynamic_slice_in_dim(line, first, block)
            start = sum(jnp.where(mine == d, doc_first[d], 0) for d in range(DOCS))
            scalars += [first, start[0], start[block - 1]]
            positions.append(first + offsets - start)
        infos += scalars
    info = jnp.stack(infos)
    angle = jnp.concatenate(positions).astype(F32)[:, None] * freq
    cos, sin = jnp.cos(angle), jnp.sin(angle)
    cos, sin = jnp.concatenate([cos, cos], 1), jnp.concatenate([-sin, sin], 1)
    gain_q, gain_k = norm_query.reshape(1, HD), norm_key.reshape(1, HD)

    raw = dot(h1, full_qkv)
    q, kv = head_prep(raw, cos, sin, gain_q, gain_k, query_heads, groups)
    q = q.reshape(seq_count, 2 * ways, block, q_width)

    mine, theirs = pair_columns([w_gate, w_up, w_down], pair, 2)
    shards = swap_shards(mine, after(theirs, h1), pair)
    full_kv = ctx_gather(after(kv, full_output), ways).reshape(-1, seq_count, 2 * ways, block, kv_width)
    shards = after(shards, kv)
    full_gate, full_up, full_down = (
        gather_weight(shards[:, i * hidden : (i + 1) * hidden], 2) for i in range(3)
    )
    cot_all = gather_rows(after(cot_own, shards), 2)

    q = after(q, cot_all)
    heads, lse = attend(info, q, full_kv, count, ways)
    mixed = heads.reshape(-1, q_width)
    lows, highs = return_rows(dot_cols(mixed, full_output).astype(BF16), ways)
    x2, h2_own = row_pass(
        functools.partial(middle_kernel, len(lows), len(highs)),
        (inputs, gain_mlp_row, *lows, *highs),
        (row_f32, row_bf16),
        "middle",
    )
    h2 = gather_rows(h2_own, 2)

    gate = dot(h2, full_gate)
    up = dot(h2, full_up)
    act = lax.optimization_barrier((gate / (1.0 + jnp.exp(-gate)) * up).astype(BF16))
    grad_down = dot_rows(cot_all, act).astype(BF16)
    d_act = dot(after(cot_all, grad_down), full_down)
    sg = 1.0 / (1.0 + jnp.exp(-gate))
    d_gate = (d_act * up * sg * (1.0 + gate * (1.0 - sg))).astype(BF16)
    d_up = (d_act * gate * sg).astype(BF16)
    d_h2_part = (dot_cols(d_gate, full_gate) + dot_cols(d_up, full_up)).astype(BF16)
    h2_late = after(h2, d_h2_part)
    grad_gate = dot_rows(h2_late, d_gate).astype(BF16)
    grad_up = dot_rows(h2_late, d_up).astype(BF16)
    lows, highs = return_rows(d_h2_part, 2, (grad_gate, grad_up))
    returned = lows + highs
    d_x2, d_x2_low, gain_mlp = row_pass(
        functools.partial(back_kernel, len(lows), len(highs), None),
        (cot_own, x2, gain_mlp_row, *lows, *highs),
        (row_f32, row_bf16, gain_shape),
        "middle_back",
    )
    y_part = dot_cols(after(act, d_x2_low), full_down).astype(BF16)
    branch = gather_rows(d_x2_low, ways)
    rows_down = scatter_weight(grad_down, 2)
    rows_gate = scatter_weight(after(grad_gate, (rows_down, returned)), 2)
    d_att = dot(branch, full_output).astype(BF16).reshape(q.shape)
    rows_up = scatter_weight(after(grad_up, (rows_gate, d_att)), 2)
    grad_output = dot_rows(branch, mixed).astype(BF16)

    def one(both, split):
        return own_rows(both, pair, split, [(0, both.shape[1], 0, 0)], [both.shape[1]])[0]

    shard_down = one(rows_down, 2)
    shard_gate = one(rows_gate, 2)
    d_q, d_kv = attend_back(info, q, d_att, heads, lse, full_kv, count, ways)
    d_qp, gain_q_sum = head_prep_back(
        d_q.reshape(-1, q_width), raw, cos, sin, gain_q, 0, False
    )
    d_h1_query = dot_cols(d_qp, full_qkv[:, :q_width])
    d_kv = after(
        d_kv.reshape(-1, kv_width),
        (rows_up, d_h1_query, grad_output, y_part, shard_down, shard_gate),
    )
    d_kv = ctx_scatter(d_kv, ways)
    rows_output = scatter_weight(after(grad_output, d_kv), ways)
    d_kvp, gain_k_sum = head_prep_back(d_kv, raw, cos, sin, gain_k, q_width // kv_width, True)
    d_h1 = (
        d_h1_query + dot_cols(d_kvp, full_qkv[:, q_width:])
    ).astype(BF16)
    lows, highs = return_rows(after(y_part, branch), 2)
    out_tokens = row_pass(
        functools.partial(result_kernel, len(lows), len(highs), ctx_count),
        (after(x2, d_h1), *lows, *highs),
        row_bf16,
        "result",
    ).reshape(tokens.shape)
    lows, highs = return_rows(d_h1, ways)
    d_raw = jnp.concatenate([d_qp, d_kvp], axis=1)
    grad_qkv = dot_rows(after(h1, d_h1), d_raw).astype(BF16)

    rows_qkv = scatter_weight(grad_qkv, ways)
    grad_tokens, gain_attn = row_pass(
        functools.partial(back_kernel, len(lows), len(highs), ctx_count),
        (d_x2, inputs, gain_attn_row, *lows, *highs),
        (row_f32, gain_shape),
        "entry_back",
    )
    rows_output, rows_up, rows_qkv = after((rows_output, rows_up, rows_qkv), gain_attn)
    shard_output = one(rows_output, ways)
    shard_up = one(rows_up, 2)
    plan = [(0, q_width, 0, 0)]
    for h in range(groups):
        for t in (0, 1):
            plan.append((q_width + (2 * h + t) * HD, HD, 1 + t, h * HD))
    shard_query, shard_key, shard_value = own_rows(
        rows_qkv, pair, ways, plan, [q_width, groups * HD, groups * HD]
    )
    grad_tokens = grad_tokens.reshape(tokens.shape)
    gains = butterfly_sum(
        jnp.concatenate([gain_attn[0], gain_mlp[0], gain_q_sum[0], gain_k_sum[0]])
    )
    return (
        out_tokens,
        grad_tokens,
        shard_query,
        shard_key,
        shard_value,
        shard_output,
        shard_gate,
        shard_up,
        shard_down,
        swap_blocks(gains[None, :width], ctx_count, 1)[0],
        swap_blocks(gains[None, width : 2 * width], ctx_count, 1)[0],
        gains[2 * width : 2 * width + HD],
        gains[2 * width + HD :],
    )


def solution(mesh):
    block = P("fsdp", "ctx", None, None, None)
    weight = P("ctx", "fsdp")
    return jax.shard_map(
        local,
        mesh=mesh,
        in_specs=(block, block, P()) + (weight,) * 7 + (P(),) * 4,
        out_specs=(block, block) + (weight,) * 7 + (P(),) * 4,
        check_vma=False,
    )
```

```python
import functools
import math

import jax
import jax.numpy as jnp
from jax import lax
from jax.experimental import pallas as pl
from jax.experimental.pallas import tpu as pltpu
from jax.sharding import PartitionSpec as P

QUERY_HEADS = 16
KEY_VALUE_HEADS = 8
HD = 128
DOCS = 4
CHUNK = 256
eps = 1e-06
rope_base = 1000000.0
SCALE = HD ** (-0.5)
EXP2_SCALE = SCALE * math.log2(math.e)
F32 = jnp.float32
BF16 = jnp.bfloat16


def xor_send(value, axis, step):
    count = lax.axis_size(axis)
    return lax.ppermute(value, axis, [(i, i ^ step) for i in range(count)])


def exchange_rows(rows, axis):
    return [rows] + [xor_send(rows, axis, r) for r in range(1, lax.axis_size(axis))]


def scatter_rows(partial, axis):
    count = lax.axis_size(axis)
    rows = partial.shape[0] // count
    total = partial[:rows].astype(F32)
    for r in range(1, count):
        total = total + xor_send(partial[r * rows : (r + 1) * rows], axis, r).astype(F32)
    return total


def pair_groups(count):
    return [[i for i in range(count) if (i >> 1) & 1 == bit] for bit in (0, 1)]


def swap_blocks(x, count, axis):
    shape = x.shape
    split = x.reshape(shape[:axis] + (count // 4, 2, 2, shape[axis] // count) + shape[axis + 1 :])
    return split.swapaxes(axis + 1, axis + 2).reshape(shape)


def assemble_kernel(plan, *refs):
    out_ref = refs[-1]
    place = 0
    for index, start, number in plan:
        out_ref[place : place + number, :] = refs[index][start : start + number, :]
        place += number


def assemble(arrays, plan):
    width = arrays[0].shape[1]
    rows = sum(number for _, _, number in plan)
    return pl.pallas_call(
        functools.partial(assemble_kernel, plan),
        out_shape=jax.ShapeDtypeStruct((rows, width), arrays[0].dtype),
        compiler_params=vmem_limit(32),
        cost_estimate=pl.CostEstimate(
            flops=0, bytes_accessed=4 * rows * width, transcendentals=0
        ),
        name="assemble",
    )(*arrays)


def gather_rows(rows, ways):
    count = lax.axis_size("fsdp")
    total = rows.shape[0]
    if ways == 1:
        return assemble(exchange_rows(rows, "fsdp"), [(r, 0, total) for r in range(count)])
    block = total // 2
    low = rows[:block]
    lows = exchange_rows(low, "fsdp")
    high = jnp.concatenate([rows[block:], xor_send(rows[block:], "ctx", 2)], axis=0)
    highs = exchange_rows(high, "fsdp")
    others = xor_send(jnp.concatenate(lows, axis=0), "ctx", 2)
    plan = []
    for r in range(count):
        plan += [(1 + r, 0, block), (0, r * block, block), (1 + count + r, 0, 2 * block)]
    return assemble([others] + lows + highs, plan)


def return_rows(partial, ways, filler=None):
    count = lax.axis_size("fsdp")
    if ways == 1:
        rows = partial.shape[0] // count
        terms = [partial[:rows]] + [
            xor_send(partial[r * rows : (r + 1) * rows], "fsdp", r) for r in range(1, count)
        ]
        return [t[: rows // 2] for t in terms], [t[rows // 2 :] for t in terms]
    block = partial.shape[0] // (4 * count)

    def rows(start, number):
        return partial[start * block : (start + number) * block]

    sent = jnp.concatenate([rows(4 * r + 1, 1) for r in range(count)], axis=0)
    pairs = [xor_send(rows(4 * r + 2, 2), "fsdp", r) for r in range(1, count)]
    other = xor_send(sent, "ctx", 2)
    if filler is not None:
        other = after(other, filler)
    first = [
        (rows(4 * r, 1).astype(F32) + other[r * block : (r + 1) * block].astype(F32)).astype(BF16)
        for r in range(count)
    ]
    second = rows(2, 2).astype(F32)
    for term in pairs:
        second = second + term.astype(F32)
    second = second.astype(BF16)
    lows = [first[0]] + [xor_send(first[r], "fsdp", r) for r in range(1, count)]
    return lows, [second[:block], xor_send(second[block:], "ctx", 2)]


def natural_columns(x, count):
    width = x.shape[1] // count
    order = [(i & ~3) | ((i & 1) << 1) | ((i >> 1) & 1) for i in range(count)]
    return jnp.concatenate([x[:, i * width : (i + 1) * width] for i in order], axis=1)


ROWS = 16


def over_rows(number, body, carry=None):
    def step(i, carry):
        return body(pl.multiple_of(i * ROWS, ROWS), carry)

    return lax.fori_loop(0, number // ROWS, step, carry)


def row_scale(x):
    return lax.rsqrt(jnp.mean(x * x, axis=-1, keepdims=True) + eps)


def entry_kernel(count, tok_ref, cot_ref, gain_ref, h_ref, x_ref, c_ref):
    def body(at, carry):
        rows = pl.ds(at, ROWS)
        x = natural_columns(tok_ref[rows, :], count)
        x_ref[rows, :] = x
        wide = x.astype(F32)
        h_ref[rows, :] = (wide * row_scale(wide) * gain_ref[...]).astype(BF16)
        c_ref[rows, :] = natural_columns(cot_ref[rows, :], count)
        return carry

    over_rows(tok_ref.shape[0], body, 0)


def sum_terms(refs, rows):
    total = refs[0][rows, :].astype(F32)
    for ref in refs[1:]:
        total = total + ref[rows, :].astype(F32)
    return total


def middle_kernel(lows, highs, *refs):
    x_ref, gain_ref, x2_ref, h_ref = refs[0], refs[1], refs[-2], refs[-1]
    block = x_ref.shape[0] // 2
    for half, terms in ((0, refs[2 : 2 + lows]), (1, refs[2 + lows : 2 + lows + highs])):

        def body(at, carry):
            rows = pl.ds(half * block + at, ROWS)
            x2 = x_ref[rows, :].astype(F32) + sum_terms(terms, pl.ds(at, ROWS))
            x2_ref[rows, :] = x2
            h_ref[rows, :] = (x2 * row_scale(x2) * gain_ref[...]).astype(BF16)
            return carry

        over_rows(block, body, 0)


def result_kernel(lows, highs, count, *refs):
    x_ref, out_ref = refs[0], refs[-1]
    block = x_ref.shape[0] // 2
    for half, terms in ((0, refs[1 : 1 + lows]), (1, refs[1 + lows : 1 + lows + highs])):

        def body(at, carry):
            rows = pl.ds(half * block + at, ROWS)
            total = x_ref[rows, :] + sum_terms(terms, pl.ds(at, ROWS))
            out_ref[rows, :] = natural_columns(total, count).astype(BF16)
            return carry

        over_rows(block, body, 0)


def back_kernel(lows, highs, count, *refs):
    base_ref, x_ref, gain_ref = refs[:3]
    wide_ref, gain_out = refs[3 + lows + highs], refs[-1]
    low_ref = refs[4 + lows + highs] if count is None else None
    block = x_ref.shape[0] // 2
    total = jnp.zeros((ROWS, x_ref.shape[1]), F32)
    for half, terms in ((0, refs[3 : 3 + lows]), (1, refs[3 + lows : 3 + lows + highs])):

        def body(at, carry):
            rows = pl.ds(half * block + at, ROWS)
            grad = sum_terms(terms, pl.ds(at, ROWS))
            x = x_ref[rows, :].astype(F32)
            scale = row_scale(x)
            unit = x * scale
            scaled = grad * gain_ref[...]
            out = base_ref[rows, :].astype(F32) + scale * (
                scaled - unit * jnp.mean(scaled * unit, axis=-1, keepdims=True)
            )
            if count is None:
                wide_ref[rows, :] = out
                low_ref[rows, :] = out.astype(BF16)
            else:
                wide_ref[rows, :] = natural_columns(out, count)
            return carry + grad * unit

        total = over_rows(block, body, total)
    gain_out[...] = jnp.sum(total, axis=0, keepdims=True)


def row_pass(kernel, args, outs, name):
    return pl.pallas_call(
        kernel,
        out_shape=outs,
        compiler_params=vmem_limit(40),
        cost_estimate=pl.CostEstimate(
            flops=10 * args[0].size, bytes_accessed=10 * args[0].size, transcendentals=0
        ),
        name=name,
    )(*args)


def pair_columns(weights, pair, ways):
    shares = []
    for place in (pair, 1 - pair):
        parts = []
        for weight in weights:
            columns = weight.shape[1] // ways
            parts.append(lax.dynamic_slice_in_dim(weight, place * columns, columns, 1))
        shares.append(jnp.concatenate(parts, axis=1))
    return shares


def swap_shards(mine, theirs, pair):
    theirs = xor_send(theirs, "ctx", 2)
    return jnp.concatenate(
        [jnp.where(pair == 0, mine, theirs), jnp.where(pair == 0, theirs, mine)], axis=0
    )


def ctx_gather(rows, ways):
    groups = pair_groups(lax.axis_size("ctx")) if ways == 2 else None
    return lax.all_gather(rows, "ctx", axis=0, tiled=True, axis_index_groups=groups)


def ctx_scatter(rows, ways):
    groups = pair_groups(lax.axis_size("ctx")) if ways == 2 else None
    return lax.psum_scatter(
        rows, "ctx", scatter_dimension=0, tiled=True, axis_index_groups=groups
    )


def gather_weight(shard, ways):
    full = ctx_gather(shard, ways)
    return swap_blocks(full, lax.axis_size("ctx"), 0) if ways == 1 else full


def scatter_weight(grad, ways):
    if ways == 1:
        grad = swap_blocks(grad, lax.axis_size("ctx"), 0)
    return ctx_scatter(grad, ways)


def own_kernel(plan, pair_ref, both_ref, other_ref, *outs):
    pair = pair_ref[0]
    rows, width = other_ref.shape
    mine = pl.ds(pl.multiple_of(pair * rows, rows), rows)
    for source, columns, target, place in plan:
        half = outs[target].shape[1] // 2
        for ref, at, which in ((both_ref, mine, pair), (other_ref, slice(None), 1 - pair)):
            start = pl.multiple_of(which * half + place, HD)
            outs[target][:, pl.ds(start, columns)] = ref[at, source : source + columns].astype(F32)


def own_rows(both, pair, ways, plan, widths):
    if ways == 1:
        return [
            jnp.concatenate([both[:, s : s + n] for s, n, t, _ in plan if t == i], axis=1).astype(F32)
            for i in range(len(widths))
        ]
    rows = both.shape[0] // 2
    other = xor_send(lax.dynamic_slice_in_dim(both, (1 - pair) * rows, rows, 0), "ctx", 2)
    shapes = tuple(jax.ShapeDtypeStruct((rows, 2 * width), F32) for width in widths)
    whole = [pl.BlockSpec(t.shape, lambda i, m: (0, 0)) for t in (both, other) + shapes]
    return pl.pallas_call(
        functools.partial(own_kernel, plan),
        out_shape=shapes,
        grid_spec=pltpu.PrefetchScalarGridSpec(
            num_scalar_prefetch=1,
            grid=(1,),
            in_specs=whole[:2],
            out_specs=tuple(whole[2:]),
        ),
        cost_estimate=pl.CostEstimate(flops=0, bytes_accessed=8 * both.size, transcendentals=0),
        name="own_rows",
    )(pair.reshape(1), both, other)


def butterfly_sum(value):
    for axis in ("ctx", "fsdp"):
        step = 1
        while step < lax.axis_size(axis):
            value = value + xor_send(value, axis, step)
            step *= 2
    return value


def dot(left, right):
    return jnp.dot(left, right, preferred_element_type=F32)


def dot_rows(left, right):
    return lax.dot_general(left, right, (((0,), (0,)), ((), ())), preferred_element_type=F32)


def dot_cols(left, right):
    return lax.dot_general(left, right, (((1,), (1,)), ((), ())), preferred_element_type=F32)


def vmem_limit(mib):
    return pltpu.CompilerParams(vmem_limit_bytes=mib * 1024 * 1024)


def prep_kernel(query_heads, groups, raw_ref, cos_ref, sin_ref, gq_ref, gk_ref, q_ref, kv_ref):
    cos = cos_ref[...]
    sin = sin_ref[...]

    def rotate_norm(x, gain):
        scale = lax.rsqrt(jnp.mean(x * x, axis=-1, keepdims=True) + eps)
        u = x * scale * gain
        return u * cos + pltpu.roll(u, HD // 2, 1) * sin

    for h in range(query_heads):
        cols = slice(h * HD, (h + 1) * HD)
        q_ref[:, cols] = rotate_norm(raw_ref[:, cols], gq_ref[...]).astype(BF16)
    for h in range(2 * groups):
        x = raw_ref[:, (query_heads + h) * HD : (query_heads + h + 1) * HD]
        if h % 2 == 0:
            x = rotate_norm(x, gk_ref[...])
        kv_ref[:, h * HD : (h + 1) * HD] = x.astype(BF16)


def head_prep(raw, cos, sin, gq, gk, query_heads, groups):
    rows, width = raw.shape
    tile = 256
    vec = pl.BlockSpec((1, HD), lambda i: (0, 0))
    tab = pl.BlockSpec((tile, HD), lambda i: (i, 0))
    return pl.pallas_call(
        functools.partial(prep_kernel, query_heads, groups),
        out_shape=(
            jax.ShapeDtypeStruct((rows, query_heads * HD), BF16),
            jax.ShapeDtypeStruct((rows, 2 * groups * HD), BF16),
        ),
        grid=(rows // tile,),
        in_specs=[pl.BlockSpec((tile, width), lambda i: (i, 0)), tab, tab, vec, vec],
        out_specs=(
            pl.BlockSpec((tile, query_heads * HD), lambda i: (i, 0)),
            pl.BlockSpec((tile, 2 * groups * HD), lambda i: (i, 0)),
        ),
        cost_estimate=pl.CostEstimate(
            flops=20 * raw.size, bytes_accessed=6 * raw.size, transcendentals=0
        ),
        name="head_prep",
    )(raw, cos, sin, gq, gk)


def prep_back_kernel(heads, plain, d_ref, raw_ref, cos_ref, sin_ref, g_ref, out_ref, gain_ref):
    cos = cos_ref[...]
    sin = sin_ref[...]
    gain = g_ref[...]
    gain_sum = jnp.zeros((1, HD), F32)
    for h in range(heads):
        cols = slice(h * HD, (h + 1) * HD)
        d = d_ref[:, cols].astype(F32)
        if plain and h % 2 == 1:
            out_ref[:, cols] = d.astype(BF16)
            continue
        x = raw_ref[:, cols]
        t = d * cos - pltpu.roll(d, HD // 2, 1) * sin
        scale = lax.rsqrt(jnp.mean(x * x, axis=-1, keepdims=True) + eps)
        n = x * scale
        gain_sum = gain_sum + jnp.sum(t * n, axis=0, keepdims=True)
        e = t * gain
        out_ref[:, cols] = (scale * (e - n * jnp.mean(e * n, axis=-1, keepdims=True))).astype(BF16)

    @pl.when(pl.program_id(0) == 0)
    def _():
        gain_ref[...] = jnp.zeros_like(gain_ref)

    gain_ref[...] += gain_sum


def head_prep_back(grad, raw, cos, sin, gain, raw_block, plain):
    rows, width = grad.shape
    tile = 256
    tab = pl.BlockSpec((tile, HD), lambda i: (i, 0))
    return pl.pallas_call(
        functools.partial(prep_back_kernel, width // HD, plain),
        out_shape=(
            jax.ShapeDtypeStruct((rows, width), BF16),
            jax.ShapeDtypeStruct((1, HD), F32),
        ),
        grid=(rows // tile,),
        in_specs=[
            pl.BlockSpec((tile, width), lambda i: (i, 0)),
            pl.BlockSpec((tile, width), lambda i: (i, raw_block)),
            tab,
            tab,
            pl.BlockSpec((1, HD), lambda i: (0, 0)),
        ],
        out_specs=(
            pl.BlockSpec((tile, width), lambda i: (i, 0)),
            pl.BlockSpec((1, HD), lambda i: (0, 0)),
        ),
        cost_estimate=pl.CostEstimate(
            flops=20 * rows * width, bytes_accessed=10 * rows * width, transcendentals=0
        ),
        name="head_prep_back",
    )(grad, raw, cos, sin, gain)


def block_place(pair, shard, place, ways, count):
    owner = shard
    if ways == 2:
        other = (pair + place % 2) % 2 if isinstance(pair, int) else lax.rem(pair + place % 2, 2)
        owner = (shard // 2) * 4 + 2 * other + shard % 2
    return owner if place < ways else 2 * count - 1 - owner


def load_sequence(pair, ways, kv_ref, keys, values):
    shards, _, _, block, _ = kv_ref.shape
    for shard in range(shards):
        for place in range(2 * ways):
            index = block_place(pair, shard, place, ways, shards * ways)
            rows = pl.ds(pl.multiple_of(index * block, block), block)
            keys[rows, :] = kv_ref[shard, 0, place, :, :HD]
            values[rows, :] = kv_ref[shard, 0, place, :, HD:]


def stack_heads(tile, count):
    return jnp.concatenate([tile[:, h * HD : (h + 1) * HD] for h in range(count)], axis=0)


def row_positions(info_ref, place, block, count):
    base = pl.program_id(0) * (info_ref.shape[0] // pl.num_programs(0)) + 1 + 3 * place
    first = info_ref[base]
    lane = lax.broadcasted_iota(jnp.int32, (1, count * block), 1)
    position = first + lax.rem(lane, block)
    start_first, start_last = info_ref[base + 1], info_ref[base + 2]
    start = jnp.where(position >= start_last, start_last, start_first)
    return position, start, start_first // CHUNK, (first + block - 1) // CHUNK + 1


def valid_tile(chunk, position, start, shape):
    key_index = chunk * CHUNK + lax.broadcasted_iota(jnp.int32, shape, 0)
    return (key_index <= position) & (key_index >= start)


def forward_kernel(ways, count, info_ref, q_ref, kv_ref, o_ref, lse_ref, keys, values):
    load_sequence(info_ref[0], ways, kv_ref, keys, values)
    block = q_ref.shape[2]
    columns = count * block
    for place in range(2 * ways):
        queries = stack_heads(q_ref[0, place], count)
        position, start, low, high = row_positions(info_ref, place, block, count)

        def body(chunk, carry):
            total, norm = carry
            rows = pl.ds(pl.multiple_of(chunk * CHUNK, CHUNK), CHUNK)
            score = dot_cols(keys[rows, :], queries)
            weight = jnp.where(
                valid_tile(chunk, position, start, score.shape), jnp.exp2(score * EXP2_SCALE), 0.0
            )
            norm = norm + jnp.sum(weight, axis=0, keepdims=True)
            total = total + dot_rows(values[rows, :], weight.astype(BF16))
            return total, norm

        total, norm = lax.fori_loop(
            low, high, body, (jnp.zeros((HD, columns), F32), jnp.zeros((1, columns), F32))
        )
        out = (total / norm).T.astype(BF16)
        for h in range(count):
            o_ref[0, place, :, h * HD : (h + 1) * HD] = out[h * block : (h + 1) * block]
        lse_ref[0, 0, place] = jnp.log2(norm)


def backward_kernel(
    ways, count, info_ref, q_ref, do_ref, o_ref, lse_ref, kv_ref,
    dq_ref, dkv_ref, keys, values, grad_k, grad_v,
):
    pair = info_ref[0]
    load_sequence(pair, ways, kv_ref, keys, values)
    block = q_ref.shape[2]
    columns = count * block
    grad_k[...] = jnp.zeros_like(grad_k)
    grad_v[...] = jnp.zeros_like(grad_v)
    for place in range(2 * ways):
        queries = stack_heads(q_ref[0, place], count)
        grads = stack_heads(do_ref[0, place], count)
        outs = stack_heads(o_ref[0, place], count)
        delta = jnp.sum((grads.astype(F32) * outs.astype(F32)).T, axis=0, keepdims=True)
        lse = lse_ref[0, 0, place]
        position, start, low, high = row_positions(info_ref, place, block, count)

        def body(chunk, total):
            rows = pl.ds(pl.multiple_of(chunk * CHUNK, CHUNK), CHUNK)
            key_rows = keys[rows, :]
            score = dot_cols(key_rows, queries)
            prob = jnp.where(
                valid_tile(chunk, position, start, score.shape),
                jnp.exp2(score * EXP2_SCALE - lse),
                0.0,
            )
            grad_prob = dot_cols(values[rows, :], grads)
            grad_score = (prob * (grad_prob - delta)).astype(BF16)
            grad_v[rows, :] += dot(prob.astype(BF16), grads)
            grad_k[rows, :] += dot(grad_score, queries)
            return total + dot_rows(key_rows, grad_score)

        total = lax.fori_loop(low, high, body, jnp.zeros((HD, columns), F32))
        out = total.T * SCALE
        for h in range(count):
            dq_ref[0, place, :, h * HD : (h + 1) * HD] = out[h * block : (h + 1) * block]
    shards = dkv_ref.shape[0]
    for shard in range(shards):
        for place in range(2 * ways):
            index = block_place(pair, shard, place, ways, shards * ways)
            rows = pl.ds(pl.multiple_of(index * block, block), block)
            dkv_ref[shard, 0, place, :, :HD] = (grad_k[rows, :] * SCALE).astype(BF16)
            dkv_ref[shard, 0, place, :, HD:] = grad_v[rows, :].astype(BF16)


def attention_specs(q, kv, count):
    shards, sequences, places, block, width = kv.shape
    row = pl.BlockSpec((1, places, block, count * HD), lambda s, n, i: (s, 0, 0, n))
    part = pl.BlockSpec((shards, 1, places, block, 2 * HD), lambda s, n, i: (0, s, 0, 0, n))
    sums = pl.BlockSpec((1, 1, places, 1, count * block), lambda s, n, i: (s, n, 0, 0, 0))
    sums_shape = (sequences, width // (2 * HD), places, 1, count * block)
    return row, part, sums, sums_shape, shards * places * block


def attend(info, q, kv, count, ways):
    row, part, sums, sums_shape, length = attention_specs(q, kv, count)
    return pl.pallas_call(
        functools.partial(forward_kernel, ways, count),
        out_shape=(
            jax.ShapeDtypeStruct(q.shape, BF16),
            jax.ShapeDtypeStruct(sums_shape, F32),
        ),
        grid_spec=pltpu.PrefetchScalarGridSpec(
            num_scalar_prefetch=1,
            grid=sums_shape[:2],
            in_specs=[row, part],
            out_specs=(row, sums),
            scratch_shapes=[pltpu.VMEM((length, HD), BF16)] * 2,
        ),
        compiler_params=vmem_limit(48),
        cost_estimate=pl.CostEstimate(
            flops=4 * 8 * CHUNK * q.size, bytes_accessed=2 * kv.size, transcendentals=0
        ),
        name="attend",
    )(info, q, kv)


def attend_back(info, q, grad, out, lse, kv, count, ways):
    row, part, sums, sums_shape, length = attention_specs(q, kv, count)
    return pl.pallas_call(
        functools.partial(backward_kernel, ways, count),
        out_shape=(
            jax.ShapeDtypeStruct(q.shape, F32),
            jax.ShapeDtypeStruct(kv.shape, BF16),
        ),
        grid_spec=pltpu.PrefetchScalarGridSpec(
            num_scalar_prefetch=1,
            grid=sums_shape[:2],
            in_specs=[row, row, row, sums, part],
            out_specs=(row, part),
            scratch_shapes=[pltpu.VMEM((length, HD), BF16)] * 2
            + [pltpu.VMEM((length, HD), F32)] * 2,
        ),
        compiler_params=vmem_limit(56),
        cost_estimate=pl.CostEstimate(
            flops=10 * 8 * CHUNK * q.size, bytes_accessed=4 * kv.size, transcendentals=0
        ),
        name="attend_back",
    )(info, q, grad, out, lse, kv)


def interleave_heads(first, second):
    rows, width = first.shape
    heads = width // HD
    both = jnp.stack([first.reshape(rows, heads, HD), second.reshape(rows, heads, HD)], axis=2)
    return both.reshape(rows, 2 * width)


def after(value, earlier):
    return lax.optimization_barrier((value, earlier))[0]


def local(
    tokens,
    grad_out,
    segments,
    w_query,
    key_weight_matrix,
    value_weight_matrix,
    w_output,
    w_gate,
    w_up,
    w_down,
    norm_attn,
    norm_mlp,
    norm_query,
    norm_key,
):
    ctx_count = lax.axis_size("ctx")
    seq_count = lax.axis_size("fsdp")
    me = lax.axis_index("ctx").astype(jnp.int32)
    my_seq = lax.axis_index("fsdp").astype(jnp.int32)
    pair = lax.rem(me // 2, 2)
    block = tokens.shape[3]
    width = tokens.shape[4]
    own = 2 * block
    ways = 2 if (key_weight_matrix.shape[1] // HD) % 2 == 0 else 1
    query_heads = w_query.shape[1] // HD // ways
    groups = key_weight_matrix.shape[1] // HD // ways
    count = query_heads // groups
    q_width, kv_width = query_heads * HD, 2 * groups * HD
    hidden = w_gate.shape[1] // 2

    w_kv = interleave_heads(key_weight_matrix, value_weight_matrix)
    gain_attn_row = swap_blocks(norm_attn[None], ctx_count, 1)
    gain_mlp_row = swap_blocks(norm_mlp[None], ctx_count, 1)

    qkv_width = q_width + kv_width
    if ways == 2:
        early = swap_shards(*pair_columns([w_query, w_kv, w_output], pair, 2), pair)
        qkv_shard, output_shard = early[:, :qkv_width], early[:, qkv_width:]
    else:
        qkv_shard, output_shard = jnp.concatenate([w_query, w_kv], axis=1), w_output
    full_qkv = gather_weight(qkv_shard, ways)
    full_output = gather_weight(output_shard, ways)

    row_bf16 = jax.ShapeDtypeStruct((own, width), BF16)
    row_f32 = jax.ShapeDtypeStruct((own, width), F32)
    gain_shape = jax.ShapeDtypeStruct((1, width), F32)
    h1_own, inputs, cot_own = row_pass(
        functools.partial(entry_kernel, ctx_count),
        (tokens.reshape(own, width), grad_out.reshape(own, width), gain_attn_row),
        (row_bf16, row_bf16, row_bf16),
        "entry",
    )
    h1 = gather_rows(h1_own, ways)

    offsets = jnp.arange(block, dtype=jnp.int32)
    owners = [me, me + 2 - 4 * pair][:ways]
    firsts = [o * block for o in owners + [2 * ctx_count - 1 - o for o in owners]]
    freq = jnp.exp(jnp.arange(HD // 2, dtype=F32) * (-2.0 * math.log(rope_base) / HD))
    infos, positions = [], []
    for r in range(seq_count):
        line = lax.dynamic_index_in_dim(
            segments, lax.bitwise_xor(my_seq, jnp.int32(r)), 0, keepdims=False
        )
        doc_first = [jnp.sum((line < d).astype(jnp.int32)) for d in range(DOCS)]
        scalars = [pair]
        for first in firsts:
            mine = lax.dynamic_slice_in_dim(line, first, block)
            start = sum(jnp.where(mine == d, doc_first[d], 0) for d in range(DOCS))
            scalars += [first, start[0], start[block - 1]]
            positions.append(first + offsets - start)
        infos += scalars
    info = jnp.stack(infos)
    angle = jnp.concatenate(positions).astype(F32)[:, None] * freq
    cos, sin = jnp.cos(angle), jnp.sin(angle)
    cos, sin = jnp.concatenate([cos, cos], 1), jnp.concatenate([-sin, sin], 1)
    gain_q, gain_k = norm_query.reshape(1, HD), norm_key.reshape(1, HD)

    raw = dot(h1, full_qkv)
    q, kv = head_prep(raw, cos, sin, gain_q, gain_k, query_heads, groups)
    q = q.reshape(seq_count, 2 * ways, block, q_width)

    mine, theirs = pair_columns([w_gate, w_up, w_down], pair, 2)
    shards = swap_shards(mine, after(theirs, h1), pair)
    full_kv = ctx_gather(after(kv, full_output), ways).reshape(-1, seq_count, 2 * ways, block, kv_width)
    shards = after(shards, kv)
    full_gate, full_up, full_down = (
        gather_weight(shards[:, i * hidden : (i + 1) * hidden], 2) for i in range(3)
    )
    cot_all = gather_rows(after(cot_own, shards), 2)

    q = after(q, cot_all)
    heads, lse = attend(info, q, full_kv, count, ways)
    mixed = heads.reshape(-1, q_width)
    lows, highs = return_rows(dot_cols(mixed, full_output).astype(BF16), ways)
    x2, h2_own = row_pass(
        functools.partial(middle_kernel, len(lows), len(highs)),
        (inputs, gain_mlp_row, *lows, *highs),
        (row_f32, row_bf16),
        "middle",
    )
    h2 = gather_rows(h2_own, 2)

    gate = dot(h2, full_gate)
    up = dot(h2, full_up)
    act = lax.optimization_barrier((gate / (1.0 + jnp.exp(-gate)) * up).astype(BF16))
    grad_down = dot_rows(cot_all, act).astype(BF16)
    d_act = dot(after(cot_all, grad_down), full_down)
    sg = 1.0 / (1.0 + jnp.exp(-gate))
    d_gate = (d_act * up * sg * (1.0 + gate * (1.0 - sg))).astype(BF16)
    d_up = (d_act * gate * sg).astype(BF16)
    d_h2_part = (dot_cols(d_gate, full_gate) + dot_cols(d_up, full_up)).astype(BF16)
    h2_late = after(h2, d_h2_part)
    grad_gate = dot_rows(h2_late, d_gate).astype(BF16)
    grad_up = dot_rows(h2_late, d_up).astype(BF16)
    lows, highs = return_rows(d_h2_part, 2, (grad_gate, grad_up))
    returned = (lows[0], highs[0])
    d_x2, d_x2_low, gain_mlp = row_pass(
        functools.partial(back_kernel, len(lows), len(highs), None),
        (cot_own, x2, gain_mlp_row, *lows, *highs),
        (row_f32, row_bf16, gain_shape),
        "middle_back",
    )
    y_part = dot_cols(after(act, d_x2_low), full_down).astype(BF16)
    branch = after(gather_rows(d_x2_low, ways), y_part)
    y_lows, y_highs = return_rows(after(y_part, branch), 2)
    out_tokens = row_pass(
        functools.partial(result_kernel, len(y_lows), len(y_highs), ctx_count),
        (x2, *y_lows, *y_highs),
        row_bf16,
        "result",
    ).reshape(tokens.shape)
    rows_down = scatter_weight(grad_down, 2)
    rows_gate = scatter_weight(after(grad_gate, (rows_down, returned)), 2)
    d_att = dot(branch, full_output).astype(BF16).reshape(q.shape)
    rows_up = scatter_weight(after(grad_up, (rows_gate, d_att)), 2)
    grad_output = dot_rows(branch, mixed).astype(BF16)

    def one(both, split):
        return own_rows(both, pair, split, [(0, both.shape[1], 0, 0)], [both.shape[1]])[0]

    shard_down = one(rows_down, 2)
    shard_gate = one(rows_gate, 2)
    d_q, d_kv = attend_back(info, q, d_att, heads, lse, full_kv, count, ways)
    d_qp, gain_q_sum = head_prep_back(
        d_q.reshape(-1, q_width), raw, cos, sin, gain_q, 0, False
    )
    d_h1_query = dot_cols(d_qp, full_qkv[:, :q_width])
    d_kv = after(
        d_kv.reshape(-1, kv_width),
        (rows_up, d_h1_query, out_tokens, shard_down, shard_gate),
    )
    d_kv = ctx_scatter(d_kv, ways)
    rows_output = scatter_weight(after(grad_output, d_kv), ways)
    d_kvp, gain_k_sum = head_prep_back(d_kv, raw, cos, sin, gain_k, q_width // kv_width, True)
    d_h1 = (
        d_h1_query + dot_cols(d_kvp, full_qkv[:, q_width:])
    ).astype(BF16)
    lows, highs = return_rows(d_h1, ways)
    d_raw = jnp.concatenate([d_qp, d_kvp], axis=1)
    grad_qkv = dot_rows(after(h1, d_h1), d_raw).astype(BF16)

    rows_qkv = scatter_weight(grad_qkv, ways)
    grad_tokens, gain_attn = row_pass(
        functools.partial(back_kernel, len(lows), len(highs), ctx_count),
        (d_x2, inputs, gain_attn_row, *lows, *highs),
        (row_f32, gain_shape),
        "entry_back",
    )
    rows_output, rows_up, rows_qkv = after((rows_output, rows_up, rows_qkv), (lows, highs))
    shard_output = one(rows_output, ways)
    shard_up = one(rows_up, 2)
    plan = [(0, q_width, 0, 0)]
    for h in range(groups):
        for t in (0, 1):
            plan.append((q_width + (2 * h + t) * HD, HD, 1 + t, h * HD))
    shard_query, shard_key, shard_value = own_rows(
        rows_qkv, pair, ways, plan, [q_width, groups * HD, groups * HD]
    )
    grad_tokens = grad_tokens.reshape(tokens.shape)
    gains = butterfly_sum(
        jnp.concatenate([gain_attn[0], gain_mlp[0], gain_q_sum[0], gain_k_sum[0]])
    )
    return (
        out_tokens,
        grad_tokens,
        shard_query,
        shard_key,
        shard_value,
        shard_output,
        shard_gate,
        shard_up,
        shard_down,
        swap_blocks(gains[None, :width], ctx_count, 1)[0],
        swap_blocks(gains[None, width : 2 * width], ctx_count, 1)[0],
        gains[2 * width : 2 * width + HD],
        gains[2 * width + HD :],
    )


def solution(mesh):
    block = P("fsdp", "ctx", None, None, None)
    weight = P("ctx", "fsdp")
    return jax.shard_map(
        local,
        mesh=mesh,
        in_specs=(block, block, P()) + (weight,) * 7 + (P(),) * 4,
        out_specs=(block, block) + (weight,) * 7 + (P(),) * 4,
        check_vma=False,
    )
```

```python
import functools
import math

import jax
import jax.numpy as jnp
from jax import lax
from jax.experimental import pallas as pl
from jax.experimental.pallas import tpu as pltpu
from jax.sharding import PartitionSpec as P

QUERY_HEADS = 16
KEY_VALUE_HEADS = 8
HD = 128
DOCS = 4
CHUNK = 256
eps = 1e-06
rope_base = 1000000.0
SCALE = HD ** (-0.5)
EXP2_SCALE = SCALE * math.log2(math.e)
F32 = jnp.float32
BF16 = jnp.bfloat16


def xor_send(value, axis, step):
    count = lax.axis_size(axis)
    return lax.ppermute(value, axis, [(i, i ^ step) for i in range(count)])


def exchange_rows(rows, axis):
    return [rows] + [xor_send(rows, axis, r) for r in range(1, lax.axis_size(axis))]


def scatter_rows(partial, axis):
    count = lax.axis_size(axis)
    rows = partial.shape[0] // count
    total = partial[:rows].astype(F32)
    for r in range(1, count):
        total = total + xor_send(partial[r * rows : (r + 1) * rows], axis, r).astype(F32)
    return total


def pair_groups(count):
    return [[i for i in range(count) if (i >> 1) & 1 == bit] for bit in (0, 1)]


def swap_blocks(x, count, axis):
    shape = x.shape
    split = x.reshape(shape[:axis] + (count // 4, 2, 2, shape[axis] // count) + shape[axis + 1 :])
    return split.swapaxes(axis + 1, axis + 2).reshape(shape)


def assemble_kernel(plan, *refs):
    out_ref = refs[-1]
    place = 0
    for index, start, number in plan:
        out_ref[place : place + number, :] = refs[index][start : start + number, :]
        place += number


def assemble(arrays, plan):
    width = arrays[0].shape[1]
    rows = sum(number for _, _, number in plan)
    return pl.pallas_call(
        functools.partial(assemble_kernel, plan),
        out_shape=jax.ShapeDtypeStruct((rows, width), arrays[0].dtype),
        compiler_params=vmem_limit(32),
        cost_estimate=pl.CostEstimate(
            flops=0, bytes_accessed=4 * rows * width, transcendentals=0
        ),
        name="assemble",
    )(*arrays)


def gather_rows(rows, ways):
    count = lax.axis_size("fsdp")
    total = rows.shape[0]
    if ways == 1:
        return assemble(exchange_rows(rows, "fsdp"), [(r, 0, total) for r in range(count)])
    block = total // 2
    low = rows[:block]
    lows = exchange_rows(low, "fsdp")
    high = jnp.concatenate([rows[block:], xor_send(rows[block:], "ctx", 2)], axis=0)
    highs = exchange_rows(high, "fsdp")
    others = xor_send(jnp.concatenate(lows, axis=0), "ctx", 2)
    plan = []
    for r in range(count):
        plan += [(1 + r, 0, block), (0, r * block, block), (1 + count + r, 0, 2 * block)]
    return assemble([others] + lows + highs, plan)


def return_rows(partial, ways, filler=None):
    count = lax.axis_size("fsdp")
    if ways == 1:
        rows = partial.shape[0] // count
        terms = [partial[:rows]] + [
            xor_send(partial[r * rows : (r + 1) * rows], "fsdp", r) for r in range(1, count)
        ]
        return [t[: rows // 2] for t in terms], [t[rows // 2 :] for t in terms]
    block = partial.shape[0] // (4 * count)

    def rows(start, number):
        return partial[start * block : (start + number) * block]

    sent = jnp.concatenate([rows(4 * r + 1, 1) for r in range(count)], axis=0)
    pairs = [xor_send(rows(4 * r + 2, 2), "fsdp", r) for r in range(1, count)]
    other = xor_send(sent, "ctx", 2)
    if filler is not None:
        other, pairs = after((other, pairs), filler)
    first = [
        (rows(4 * r, 1).astype(F32) + other[r * block : (r + 1) * block].astype(F32)).astype(BF16)
        for r in range(count)
    ]
    second = rows(2, 2).astype(F32)
    for term in pairs:
        second = second + term.astype(F32)
    second = second.astype(BF16)
    lows = [first[0]] + [xor_send(first[r], "fsdp", r) for r in range(1, count)]
    return lows, [second[:block], xor_send(second[block:], "ctx", 2)]


def natural_columns(x, count):
    width = x.shape[1] // count
    order = [(i & ~3) | ((i & 1) << 1) | ((i >> 1) & 1) for i in range(count)]
    return jnp.concatenate([x[:, i * width : (i + 1) * width] for i in order], axis=1)


ROWS = 16


def over_rows(number, body, carry=None):
    def step(i, carry):
        return body(pl.multiple_of(i * ROWS, ROWS), carry)

    return lax.fori_loop(0, number // ROWS, step, carry)


def row_scale(x):
    return lax.rsqrt(jnp.mean(x * x, axis=-1, keepdims=True) + eps)


def entry_kernel(count, tok_ref, cot_ref, gain_ref, h_ref, x_ref, c_ref):
    def body(at, carry):
        rows = pl.ds(at, ROWS)
        x = natural_columns(tok_ref[rows, :], count)
        x_ref[rows, :] = x
        wide = x.astype(F32)
        h_ref[rows, :] = (wide * row_scale(wide) * gain_ref[...]).astype(BF16)
        c_ref[rows, :] = natural_columns(cot_ref[rows, :], count)
        return carry

    over_rows(tok_ref.shape[0], body, 0)


def sum_terms(refs, rows):
    total = refs[0][rows, :].astype(F32)
    for ref in refs[1:]:
        total = total + ref[rows, :].astype(F32)
    return total


def middle_kernel(lows, highs, *refs):
    x_ref, gain_ref, x2_ref, h_ref = refs[0], refs[1], refs[-2], refs[-1]
    block = x_ref.shape[0] // 2
    for half, terms in ((0, refs[2 : 2 + lows]), (1, refs[2 + lows : 2 + lows + highs])):

        def body(at, carry):
            rows = pl.ds(half * block + at, ROWS)
            x2 = x_ref[rows, :].astype(F32) + sum_terms(terms, pl.ds(at, ROWS))
            x2_ref[rows, :] = x2
            h_ref[rows, :] = (x2 * row_scale(x2) * gain_ref[...]).astype(BF16)
            return carry

        over_rows(block, body, 0)


def result_kernel(lows, highs, count, *refs):
    x_ref, out_ref = refs[0], refs[-1]
    block = x_ref.shape[0] // 2
    for half, terms in ((0, refs[1 : 1 + lows]), (1, refs[1 + lows : 1 + lows + highs])):

        def body(at, carry):
            rows = pl.ds(half * block + at, ROWS)
            total = x_ref[rows, :] + sum_terms(terms, pl.ds(at, ROWS))
            out_ref[rows, :] = natural_columns(total, count).astype(BF16)
            return carry

        over_rows(block, body, 0)


def back_kernel(lows, highs, count, *refs):
    base_ref, x_ref, gain_ref = refs[:3]
    wide_ref, gain_out = refs[3 + lows + highs], refs[-1]
    low_ref = refs[4 + lows + highs] if count is None else None
    block = x_ref.shape[0] // 2
    total = jnp.zeros((ROWS, x_ref.shape[1]), F32)
    for half, terms in ((0, refs[3 : 3 + lows]), (1, refs[3 + lows : 3 + lows + highs])):

        def body(at, carry):
            rows = pl.ds(half * block + at, ROWS)
            grad = sum_terms(terms, pl.ds(at, ROWS))
            x = x_ref[rows, :].astype(F32)
            scale = row_scale(x)
            unit = x * scale
            scaled = grad * gain_ref[...]
            out = base_ref[rows, :].astype(F32) + scale * (
                scaled - unit * jnp.mean(scaled * unit, axis=-1, keepdims=True)
            )
            if count is None:
                wide_ref[rows, :] = out
                low_ref[rows, :] = out.astype(BF16)
            else:
                wide_ref[rows, :] = natural_columns(out, count)
            return carry + grad * unit

        total = over_rows(block, body, total)
    gain_out[...] = jnp.sum(total, axis=0, keepdims=True)


def row_pass(kernel, args, outs, name):
    return pl.pallas_call(
        kernel,
        out_shape=outs,
        compiler_params=vmem_limit(40),
        cost_estimate=pl.CostEstimate(
            flops=10 * args[0].size, bytes_accessed=10 * args[0].size, transcendentals=0
        ),
        name=name,
    )(*args)


def pair_columns(weights, pair, ways):
    shares = []
    for place in (pair, 1 - pair):
        parts = []
        for weight in weights:
            columns = weight.shape[1] // ways
            parts.append(lax.dynamic_slice_in_dim(weight, place * columns, columns, 1))
        shares.append(jnp.concatenate(parts, axis=1))
    return shares


def swap_shards(mine, theirs, pair):
    theirs = xor_send(theirs, "ctx", 2)
    return jnp.concatenate(
        [jnp.where(pair == 0, mine, theirs), jnp.where(pair == 0, theirs, mine)], axis=0
    )


def ctx_gather(rows, ways):
    groups = pair_groups(lax.axis_size("ctx")) if ways == 2 else None
    return lax.all_gather(rows, "ctx", axis=0, tiled=True, axis_index_groups=groups)


def ctx_scatter(rows, ways):
    groups = pair_groups(lax.axis_size("ctx")) if ways == 2 else None
    return lax.psum_scatter(
        rows, "ctx", scatter_dimension=0, tiled=True, axis_index_groups=groups
    )


def gather_weight(shard, ways):
    full = ctx_gather(shard, ways)
    return swap_blocks(full, lax.axis_size("ctx"), 0) if ways == 1 else full


def scatter_weight(grad, ways):
    if ways == 1:
        grad = swap_blocks(grad, lax.axis_size("ctx"), 0)
    return ctx_scatter(grad, ways)


def own_kernel(plan, pair_ref, both_ref, other_ref, *outs):
    pair = pair_ref[0]
    rows, width = other_ref.shape
    mine = pl.ds(pl.multiple_of(pair * rows, rows), rows)
    for source, columns, target, place in plan:
        half = outs[target].shape[1] // 2
        for ref, at, which in ((both_ref, mine, pair), (other_ref, slice(None), 1 - pair)):
            start = pl.multiple_of(which * half + place, HD)
            outs[target][:, pl.ds(start, columns)] = ref[at, source : source + columns].astype(F32)


def own_rows(both, pair, ways, plan, widths):
    if ways == 1:
        return [
            jnp.concatenate([both[:, s : s + n] for s, n, t, _ in plan if t == i], axis=1).astype(F32)
            for i in range(len(widths))
        ]
    rows = both.shape[0] // 2
    other = xor_send(lax.dynamic_slice_in_dim(both, (1 - pair) * rows, rows, 0), "ctx", 2)
    shapes = tuple(jax.ShapeDtypeStruct((rows, 2 * width), F32) for width in widths)
    whole = [pl.BlockSpec(t.shape, lambda i, m: (0, 0)) for t in (both, other) + shapes]
    return pl.pallas_call(
        functools.partial(own_kernel, plan),
        out_shape=shapes,
        grid_spec=pltpu.PrefetchScalarGridSpec(
            num_scalar_prefetch=1,
            grid=(1,),
            in_specs=whole[:2],
            out_specs=tuple(whole[2:]),
        ),
        cost_estimate=pl.CostEstimate(flops=0, bytes_accessed=8 * both.size, transcendentals=0),
        name="own_rows",
    )(pair.reshape(1), both, other)


def butterfly_sum(value):
    for axis in ("ctx", "fsdp"):
        step = 1
        while step < lax.axis_size(axis):
            value = value + xor_send(value, axis, step)
            step *= 2
    return value


def dot(left, right):
    return jnp.dot(left, right, preferred_element_type=F32)


def dot_rows(left, right):
    return lax.dot_general(left, right, (((0,), (0,)), ((), ())), preferred_element_type=F32)


def dot_cols(left, right):
    return lax.dot_general(left, right, (((1,), (1,)), ((), ())), preferred_element_type=F32)


def vmem_limit(mib):
    return pltpu.CompilerParams(vmem_limit_bytes=mib * 1024 * 1024)


def prep_kernel(query_heads, groups, raw_ref, cos_ref, sin_ref, gq_ref, gk_ref, q_ref, kv_ref):
    cos = cos_ref[...]
    sin = sin_ref[...]

    def rotate_norm(x, gain):
        scale = lax.rsqrt(jnp.mean(x * x, axis=-1, keepdims=True) + eps)
        u = x * scale * gain
        return u * cos + pltpu.roll(u, HD // 2, 1) * sin

    for h in range(query_heads):
        cols = slice(h * HD, (h + 1) * HD)
        q_ref[:, cols] = rotate_norm(raw_ref[:, cols], gq_ref[...]).astype(BF16)
    for h in range(2 * groups):
        x = raw_ref[:, (query_heads + h) * HD : (query_heads + h + 1) * HD]
        if h % 2 == 0:
            x = rotate_norm(x, gk_ref[...])
        kv_ref[:, h * HD : (h + 1) * HD] = x.astype(BF16)


def head_prep(raw, cos, sin, gq, gk, query_heads, groups):
    rows, width = raw.shape
    tile = 256
    vec = pl.BlockSpec((1, HD), lambda i: (0, 0))
    tab = pl.BlockSpec((tile, HD), lambda i: (i, 0))
    return pl.pallas_call(
        functools.partial(prep_kernel, query_heads, groups),
        out_shape=(
            jax.ShapeDtypeStruct((rows, query_heads * HD), BF16),
            jax.ShapeDtypeStruct((rows, 2 * groups * HD), BF16),
        ),
        grid=(rows // tile,),
        in_specs=[pl.BlockSpec((tile, width), lambda i: (i, 0)), tab, tab, vec, vec],
        out_specs=(
            pl.BlockSpec((tile, query_heads * HD), lambda i: (i, 0)),
            pl.BlockSpec((tile, 2 * groups * HD), lambda i: (i, 0)),
        ),
        cost_estimate=pl.CostEstimate(
            flops=20 * raw.size, bytes_accessed=6 * raw.size, transcendentals=0
        ),
        name="head_prep",
    )(raw, cos, sin, gq, gk)


def prep_back_kernel(heads, plain, d_ref, raw_ref, cos_ref, sin_ref, g_ref, out_ref, gain_ref):
    cos = cos_ref[...]
    sin = sin_ref[...]
    gain = g_ref[...]
    gain_sum = jnp.zeros((1, HD), F32)
    for h in range(heads):
        cols = slice(h * HD, (h + 1) * HD)
        d = d_ref[:, cols].astype(F32)
        if plain and h % 2 == 1:
            out_ref[:, cols] = d.astype(BF16)
            continue
        x = raw_ref[:, cols]
        t = d * cos - pltpu.roll(d, HD // 2, 1) * sin
        scale = lax.rsqrt(jnp.mean(x * x, axis=-1, keepdims=True) + eps)
        n = x * scale
        gain_sum = gain_sum + jnp.sum(t * n, axis=0, keepdims=True)
        e = t * gain
        out_ref[:, cols] = (scale * (e - n * jnp.mean(e * n, axis=-1, keepdims=True))).astype(BF16)

    @pl.when(pl.program_id(0) == 0)
    def _():
        gain_ref[...] = jnp.zeros_like(gain_ref)

    gain_ref[...] += gain_sum


def head_prep_back(grad, raw, cos, sin, gain, raw_block, plain):
    rows, width = grad.shape
    tile = 256
    tab = pl.BlockSpec((tile, HD), lambda i: (i, 0))
    return pl.pallas_call(
        functools.partial(prep_back_kernel, width // HD, plain),
        out_shape=(
            jax.ShapeDtypeStruct((rows, width), BF16),
            jax.ShapeDtypeStruct((1, HD), F32),
        ),
        grid=(rows // tile,),
        in_specs=[
            pl.BlockSpec((tile, width), lambda i: (i, 0)),
            pl.BlockSpec((tile, width), lambda i: (i, raw_block)),
            tab,
            tab,
            pl.BlockSpec((1, HD), lambda i: (0, 0)),
        ],
        out_specs=(
            pl.BlockSpec((tile, width), lambda i: (i, 0)),
            pl.BlockSpec((1, HD), lambda i: (0, 0)),
        ),
        cost_estimate=pl.CostEstimate(
            flops=20 * rows * width, bytes_accessed=10 * rows * width, transcendentals=0
        ),
        name="head_prep_back",
    )(grad, raw, cos, sin, gain)


def block_place(pair, shard, place, ways, count):
    owner = shard
    if ways == 2:
        other = (pair + place % 2) % 2 if isinstance(pair, int) else lax.rem(pair + place % 2, 2)
        owner = (shard // 2) * 4 + 2 * other + shard % 2
    return owner if place < ways else 2 * count - 1 - owner


def load_sequence(pair, ways, kv_ref, keys, values):
    shards, _, _, block, _ = kv_ref.shape
    for shard in range(shards):
        for place in range(2 * ways):
            index = block_place(pair, shard, place, ways, shards * ways)
            rows = pl.ds(pl.multiple_of(index * block, block), block)
            keys[rows, :] = kv_ref[shard, 0, place, :, :HD]
            values[rows, :] = kv_ref[shard, 0, place, :, HD:]


def stack_heads(tile, count):
    return jnp.concatenate([tile[:, h * HD : (h + 1) * HD] for h in range(count)], axis=0)


def row_positions(info_ref, place, block, count):
    base = pl.program_id(0) * (info_ref.shape[0] // pl.num_programs(0)) + 1 + 3 * place
    first = info_ref[base]
    lane = lax.broadcasted_iota(jnp.int32, (1, count * block), 1)
    position = first + lax.rem(lane, block)
    start_first, start_last = info_ref[base + 1], info_ref[base + 2]
    start = jnp.where(position >= start_last, start_last, start_first)
    return position, start, start_first // CHUNK, (first + block - 1) // CHUNK + 1


def valid_tile(chunk, position, start, shape):
    key_index = chunk * CHUNK + lax.broadcasted_iota(jnp.int32, shape, 0)
    return (key_index <= position) & (key_index >= start)


def forward_kernel(ways, count, info_ref, q_ref, kv_ref, o_ref, lse_ref, keys, values):
    load_sequence(info_ref[0], ways, kv_ref, keys, values)
    block = q_ref.shape[2]
    columns = count * block
    for place in range(2 * ways):
        queries = stack_heads(q_ref[0, place], count)
        position, start, low, high = row_positions(info_ref, place, block, count)

        def body(chunk, carry):
            total, norm = carry
            rows = pl.ds(pl.multiple_of(chunk * CHUNK, CHUNK), CHUNK)
            score = dot_cols(keys[rows, :], queries)
            weight = jnp.where(
                valid_tile(chunk, position, start, score.shape), jnp.exp2(score * EXP2_SCALE), 0.0
            )
            norm = norm + jnp.sum(weight, axis=0, keepdims=True)
            total = total + dot_rows(values[rows, :], weight.astype(BF16))
            return total, norm

        total, norm = lax.fori_loop(
            low, high, body, (jnp.zeros((HD, columns), F32), jnp.zeros((1, columns), F32))
        )
        out = (total / norm).T.astype(BF16)
        for h in range(count):
            o_ref[0, place, :, h * HD : (h + 1) * HD] = out[h * block : (h + 1) * block]
        lse_ref[0, 0, place] = jnp.log2(norm)


def backward_kernel(
    ways, count, info_ref, q_ref, do_ref, o_ref, lse_ref, kv_ref,
    dq_ref, dkv_ref, keys, values, grad_k, grad_v,
):
    pair = info_ref[0]
    load_sequence(pair, ways, kv_ref, keys, values)
    block = q_ref.shape[2]
    columns = count * block
    grad_k[...] = jnp.zeros_like(grad_k)
    grad_v[...] = jnp.zeros_like(grad_v)
    for place in range(2 * ways):
        queries = stack_heads(q_ref[0, place], count)
        grads = stack_heads(do_ref[0, place], count)
        outs = stack_heads(o_ref[0, place], count)
        delta = jnp.sum((grads.astype(F32) * outs.astype(F32)).T, axis=0, keepdims=True)
        lse = lse_ref[0, 0, place]
        position, start, low, high = row_positions(info_ref, place, block, count)

        def body(chunk, total):
            rows = pl.ds(pl.multiple_of(chunk * CHUNK, CHUNK), CHUNK)
            key_rows = keys[rows, :]
            score = dot_cols(key_rows, queries)
            prob = jnp.where(
                valid_tile(chunk, position, start, score.shape),
                jnp.exp2(score * EXP2_SCALE - lse),
                0.0,
            )
            grad_prob = dot_cols(values[rows, :], grads)
            grad_score = (prob * (grad_prob - delta)).astype(BF16)
            grad_v[rows, :] += dot(prob.astype(BF16), grads)
            grad_k[rows, :] += dot(grad_score, queries)
            return total + dot_rows(key_rows, grad_score)

        total = lax.fori_loop(low, high, body, jnp.zeros((HD, columns), F32))
        out = total.T * SCALE
        for h in range(count):
            dq_ref[0, place, :, h * HD : (h + 1) * HD] = out[h * block : (h + 1) * block]
    shards = dkv_ref.shape[0]
    for shard in range(shards):
        for place in range(2 * ways):
            index = block_place(pair, shard, place, ways, shards * ways)
            rows = pl.ds(pl.multiple_of(index * block, block), block)
            dkv_ref[shard, 0, place, :, :HD] = (grad_k[rows, :] * SCALE).astype(BF16)
            dkv_ref[shard, 0, place, :, HD:] = grad_v[rows, :].astype(BF16)


def attention_specs(q, kv, count):
    shards, sequences, places, block, width = kv.shape
    row = pl.BlockSpec((1, places, block, count * HD), lambda s, n, i: (s, 0, 0, n))
    part = pl.BlockSpec((shards, 1, places, block, 2 * HD), lambda s, n, i: (0, s, 0, 0, n))
    sums = pl.BlockSpec((1, 1, places, 1, count * block), lambda s, n, i: (s, n, 0, 0, 0))
    sums_shape = (sequences, width // (2 * HD), places, 1, count * block)
    return row, part, sums, sums_shape, shards * places * block


def attend(info, q, kv, count, ways):
    row, part, sums, sums_shape, length = attention_specs(q, kv, count)
    return pl.pallas_call(
        functools.partial(forward_kernel, ways, count),
        out_shape=(
            jax.ShapeDtypeStruct(q.shape, BF16),
            jax.ShapeDtypeStruct(sums_shape, F32),
        ),
        grid_spec=pltpu.PrefetchScalarGridSpec(
            num_scalar_prefetch=1,
            grid=sums_shape[:2],
            in_specs=[row, part],
            out_specs=(row, sums),
            scratch_shapes=[pltpu.VMEM((length, HD), BF16)] * 2,
        ),
        compiler_params=vmem_limit(48),
        cost_estimate=pl.CostEstimate(
            flops=4 * 8 * CHUNK * q.size, bytes_accessed=2 * kv.size, transcendentals=0
        ),
        name="attend",
    )(info, q, kv)


def attend_back(info, q, grad, out, lse, kv, count, ways):
    row, part, sums, sums_shape, length = attention_specs(q, kv, count)
    return pl.pallas_call(
        functools.partial(backward_kernel, ways, count),
        out_shape=(
            jax.ShapeDtypeStruct(q.shape, F32),
            jax.ShapeDtypeStruct(kv.shape, BF16),
        ),
        grid_spec=pltpu.PrefetchScalarGridSpec(
            num_scalar_prefetch=1,
            grid=sums_shape[:2],
            in_specs=[row, row, row, sums, part],
            out_specs=(row, part),
            scratch_shapes=[pltpu.VMEM((length, HD), BF16)] * 2
            + [pltpu.VMEM((length, HD), F32)] * 2,
        ),
        compiler_params=vmem_limit(56),
        cost_estimate=pl.CostEstimate(
            flops=10 * 8 * CHUNK * q.size, bytes_accessed=4 * kv.size, transcendentals=0
        ),
        name="attend_back",
    )(info, q, grad, out, lse, kv)


def interleave_heads(first, second):
    rows, width = first.shape
    heads = width // HD
    both = jnp.stack([first.reshape(rows, heads, HD), second.reshape(rows, heads, HD)], axis=2)
    return both.reshape(rows, 2 * width)


def after(value, earlier):
    return lax.optimization_barrier((value, earlier))[0]


def local(
    tokens,
    grad_out,
    segments,
    w_query,
    key_weight_matrix,
    value_weight_matrix,
    w_output,
    w_gate,
    w_up,
    w_down,
    norm_attn,
    norm_mlp,
    norm_query,
    norm_key,
):
    ctx_count = lax.axis_size("ctx")
    seq_count = lax.axis_size("fsdp")
    me = lax.axis_index("ctx").astype(jnp.int32)
    my_seq = lax.axis_index("fsdp").astype(jnp.int32)
    pair = lax.rem(me // 2, 2)
    block = tokens.shape[3]
    width = tokens.shape[4]
    own = 2 * block
    ways = 2 if (key_weight_matrix.shape[1] // HD) % 2 == 0 else 1
    query_heads = w_query.shape[1] // HD // ways
    groups = key_weight_matrix.shape[1] // HD // ways
    count = query_heads // groups
    q_width, kv_width = query_heads * HD, 2 * groups * HD
    hidden = w_gate.shape[1] // 2

    w_kv = interleave_heads(key_weight_matrix, value_weight_matrix)
    gain_attn_row = swap_blocks(norm_attn[None], ctx_count, 1)
    gain_mlp_row = swap_blocks(norm_mlp[None], ctx_count, 1)

    if ways == 2:
        qkv_shard = swap_shards(*pair_columns([w_query, w_kv], pair, 2), pair)
        output_shard = swap_shards(*pair_columns([w_output], pair, 2), pair)
    else:
        qkv_shard, output_shard = jnp.concatenate([w_query, w_kv], axis=1), w_output
    full_qkv = gather_weight(qkv_shard, ways)
    full_output = gather_weight(output_shard, ways)

    row_bf16 = jax.ShapeDtypeStruct((own, width), BF16)
    row_f32 = jax.ShapeDtypeStruct((own, width), F32)
    gain_shape = jax.ShapeDtypeStruct((1, width), F32)
    h1_own, inputs, cot_own = row_pass(
        functools.partial(entry_kernel, ctx_count),
        (tokens.reshape(own, width), grad_out.reshape(own, width), gain_attn_row),
        (row_bf16, row_bf16, row_bf16),
        "entry",
    )
    h1 = gather_rows(h1_own, ways)

    offsets = jnp.arange(block, dtype=jnp.int32)
    owners = [me, me + 2 - 4 * pair][:ways]
    firsts = [o * block for o in owners + [2 * ctx_count - 1 - o for o in owners]]
    freq = jnp.exp(jnp.arange(HD // 2, dtype=F32) * (-2.0 * math.log(rope_base) / HD))
    infos, positions = [], []
    for r in range(seq_count):
        line = lax.dynamic_index_in_dim(
            segments, lax.bitwise_xor(my_seq, jnp.int32(r)), 0, keepdims=False
        )
        doc_first = [jnp.sum((line < d).astype(jnp.int32)) for d in range(DOCS)]
        scalars = [pair]
        for first in firsts:
            mine = lax.dynamic_slice_in_dim(line, first, block)
            start = sum(jnp.where(mine == d, doc_first[d], 0) for d in range(DOCS))
            scalars += [first, start[0], start[block - 1]]
            positions.append(first + offsets - start)
        infos += scalars
    info = jnp.stack(infos)
    angle = jnp.concatenate(positions).astype(F32)[:, None] * freq
    cos, sin = jnp.cos(angle), jnp.sin(angle)
    cos, sin = jnp.concatenate([cos, cos], 1), jnp.concatenate([-sin, sin], 1)
    gain_q, gain_k = norm_query.reshape(1, HD), norm_key.reshape(1, HD)

    raw = dot(h1, full_qkv)
    q, kv = head_prep(raw, cos, sin, gain_q, gain_k, query_heads, groups)
    q = q.reshape(seq_count, 2 * ways, block, q_width)

    mine, theirs = pair_columns([w_gate, w_up, w_down], pair, 2)
    shards = swap_shards(mine, after(theirs, h1), pair)
    full_kv = ctx_gather(after(kv, full_output), ways).reshape(-1, seq_count, 2 * ways, block, kv_width)
    shards = after(shards, kv)
    full_gate, full_up, full_down = (
        gather_weight(shards[:, i * hidden : (i + 1) * hidden], 2) for i in range(3)
    )
    cot_all = gather_rows(after(cot_own, shards), 2)

    q = after(q, cot_all)
    heads, lse = attend(info, q, full_kv, count, ways)
    mixed = heads.reshape(-1, q_width)
    lows, highs = return_rows(dot_cols(mixed, full_output).astype(BF16), ways)
    x2, h2_own = row_pass(
        functools.partial(middle_kernel, len(lows), len(highs)),
        (inputs, gain_mlp_row, *lows, *highs),
        (row_f32, row_bf16),
        "middle",
    )
    h2 = gather_rows(h2_own, 2)

    gate = dot(h2, full_gate)
    up = dot(h2, full_up)
    act = lax.optimization_barrier((gate / (1.0 + jnp.exp(-gate)) * up).astype(BF16))
    grad_down = dot_rows(cot_all, act).astype(BF16)
    d_act = dot(after(cot_all, grad_down), full_down)
    sg = 1.0 / (1.0 + jnp.exp(-gate))
    d_gate = (d_act * up * sg * (1.0 + gate * (1.0 - sg))).astype(BF16)
    d_up = (d_act * gate * sg).astype(BF16)
    d_h2_part = (dot_cols(d_gate, full_gate) + dot_cols(d_up, full_up)).astype(BF16)
    h2_late = after(h2, d_h2_part)
    grad_gate = dot_rows(h2_late, d_gate).astype(BF16)
    grad_up = dot_rows(h2_late, d_up).astype(BF16)
    lows, highs = return_rows(d_h2_part, 2, (grad_gate, grad_up))
    returned = (lows[0], highs[0])
    d_x2, d_x2_low, gain_mlp = row_pass(
        functools.partial(back_kernel, len(lows), len(highs), None),
        (cot_own, x2, gain_mlp_row, *lows, *highs),
        (row_f32, row_bf16, gain_shape),
        "middle_back",
    )
    y_part = dot_cols(after(act, d_x2_low), full_down).astype(BF16)
    branch = after(gather_rows(d_x2_low, ways), y_part)
    rows_down = scatter_weight(grad_down, 2)
    rows_gate = scatter_weight(after(grad_gate, (rows_down, returned)), 2)
    def one(both, split):
        return own_rows(both, pair, split, [(0, both.shape[1], 0, 0)], [both.shape[1]])[0]

    d_att = dot(branch, full_output).astype(BF16).reshape(q.shape)
    rows_up = scatter_weight(after(grad_up, (rows_gate, d_att)), 2)
    grad_output = dot_rows(branch, mixed).astype(BF16)
    rows_output = scatter_weight(after(grad_output, rows_gate), ways)
    shard_down = one(rows_down, 2)
    shard_gate = one(rows_gate, 2)
    shard_up = one(rows_up, 2)
    d_q, d_kv = attend_back(info, q, d_att, heads, lse, full_kv, count, ways)
    y_lows, y_highs = return_rows(after(y_part, branch), 2, d_q)
    out_tokens = row_pass(
        functools.partial(result_kernel, len(y_lows), len(y_highs), ctx_count),
        (x2, *y_lows, *y_highs),
        row_bf16,
        "result",
    ).reshape(tokens.shape)
    d_qp, gain_q_sum = head_prep_back(
        d_q.reshape(-1, q_width), raw, cos, sin, gain_q, 0, False
    )
    d_h1_query = dot_cols(d_qp, full_qkv[:, :q_width])
    d_kv = after(
        d_kv.reshape(-1, kv_width),
        (rows_output, d_h1_query, out_tokens, shard_down, shard_gate, shard_up),
    )
    d_kv = ctx_scatter(d_kv, ways)
    d_kvp, gain_k_sum = head_prep_back(d_kv, raw, cos, sin, gain_k, q_width // kv_width, True)
    d_h1 = (
        d_h1_query + dot_cols(d_kvp, full_qkv[:, q_width:])
    ).astype(BF16)
    lows, highs = return_rows(d_h1, ways)
    d_raw = jnp.concatenate([d_qp, d_kvp], axis=1)
    grad_qkv = dot_rows(after(h1, d_h1), d_raw).astype(BF16)

    rows_qkv = scatter_weight(grad_qkv, ways)
    grad_tokens, gain_attn = row_pass(
        functools.partial(back_kernel, len(lows), len(highs), ctx_count),
        (d_x2, inputs, gain_attn_row, *lows, *highs),
        (row_f32, gain_shape),
        "entry_back",
    )
    rows_output, rows_qkv = after((rows_output, rows_qkv), (lows, highs))
    shard_output = one(rows_output, ways)
    plan = [(0, q_width, 0, 0)]
    for h in range(groups):
        for t in (0, 1):
            plan.append((q_width + (2 * h + t) * HD, HD, 1 + t, h * HD))
    shard_query, shard_key, shard_value = own_rows(
        rows_qkv, pair, ways, plan, [q_width, groups * HD, groups * HD]
    )
    grad_tokens = grad_tokens.reshape(tokens.shape)
    gains = butterfly_sum(
        jnp.concatenate([gain_attn[0], gain_mlp[0], gain_q_sum[0], gain_k_sum[0]])
    )
    return (
        out_tokens,
        grad_tokens,
        shard_query,
        shard_key,
        shard_value,
        shard_output,
        shard_gate,
        shard_up,
        shard_down,
        swap_blocks(gains[None, :width], ctx_count, 1)[0],
        swap_blocks(gains[None, width : 2 * width], ctx_count, 1)[0],
        gains[2 * width : 2 * width + HD],
        gains[2 * width + HD :],
    )


def solution(mesh):
    block = P("fsdp", "ctx", None, None, None)
    weight = P("ctx", "fsdp")
    return jax.shard_map(
        local,
        mesh=mesh,
        in_specs=(block, block, P()) + (weight,) * 7 + (P(),) * 4,
        out_specs=(block, block) + (weight,) * 7 + (P(),) * 4,
        check_vma=False,
    )
```

```python
import functools
import math

import jax
import jax.numpy as jnp
from jax import lax
from jax.experimental import pallas as pl
from jax.experimental.pallas import tpu as pltpu
from jax.sharding import PartitionSpec as P

QUERY_HEADS = 16
KEY_VALUE_HEADS = 8
HD = 128
DOCS = 4
CHUNK = 256
eps = 1e-06
rope_base = 1000000.0
SCALE = HD ** (-0.5)
EXP2_SCALE = SCALE * math.log2(math.e)
F32 = jnp.float32
BF16 = jnp.bfloat16


def xor_send(value, axis, step):
    count = lax.axis_size(axis)
    return lax.ppermute(value, axis, [(i, i ^ step) for i in range(count)])


def exchange_rows(rows, axis):
    return [rows] + [xor_send(rows, axis, r) for r in range(1, lax.axis_size(axis))]


def scatter_rows(partial, axis):
    count = lax.axis_size(axis)
    rows = partial.shape[0] // count
    total = partial[:rows].astype(F32)
    for r in range(1, count):
        total = total + xor_send(partial[r * rows : (r + 1) * rows], axis, r).astype(F32)
    return total


def pair_groups(count):
    return [[i for i in range(count) if (i >> 1) & 1 == bit] for bit in (0, 1)]


def swap_blocks(x, count, axis):
    shape = x.shape
    split = x.reshape(shape[:axis] + (count // 4, 2, 2, shape[axis] // count) + shape[axis + 1 :])
    return split.swapaxes(axis + 1, axis + 2).reshape(shape)


def assemble_kernel(plan, *refs):
    out_ref = refs[-1]
    place = 0
    for index, start, number in plan:
        out_ref[place : place + number, :] = refs[index][start : start + number, :]
        place += number


def assemble(arrays, plan):
    width = arrays[0].shape[1]
    rows = sum(number for _, _, number in plan)
    return pl.pallas_call(
        functools.partial(assemble_kernel, plan),
        out_shape=jax.ShapeDtypeStruct((rows, width), arrays[0].dtype),
        compiler_params=vmem_limit(32),
        cost_estimate=pl.CostEstimate(
            flops=0, bytes_accessed=4 * rows * width, transcendentals=0
        ),
        name="assemble",
    )(*arrays)


def gather_rows(rows, ways):
    count = lax.axis_size("fsdp")
    total = rows.shape[0]
    if ways == 1:
        return assemble(exchange_rows(rows, "fsdp"), [(r, 0, total) for r in range(count)])
    block = total // 2
    low = rows[:block]
    lows = exchange_rows(low, "fsdp")
    high = jnp.concatenate([rows[block:], xor_send(rows[block:], "ctx", 2)], axis=0)
    highs = exchange_rows(high, "fsdp")
    others = xor_send(jnp.concatenate(lows, axis=0), "ctx", 2)
    plan = []
    for r in range(count):
        plan += [(1 + r, 0, block), (0, r * block, block), (1 + count + r, 0, 2 * block)]
    return assemble([others] + lows + highs, plan)


def return_rows(partial, ways, filler=None):
    count = lax.axis_size("fsdp")
    if ways == 1:
        rows = partial.shape[0] // count
        terms = [partial[:rows]] + [
            xor_send(partial[r * rows : (r + 1) * rows], "fsdp", r) for r in range(1, count)
        ]
        return [t[: rows // 2] for t in terms], [t[rows // 2 :] for t in terms]
    block = partial.shape[0] // (4 * count)

    def rows(start, number):
        return partial[start * block : (start + number) * block]

    sent = jnp.concatenate([rows(4 * r + 1, 1) for r in range(count)], axis=0)
    pairs = [xor_send(rows(4 * r + 2, 2), "fsdp", r) for r in range(1, count)]
    other = xor_send(sent, "ctx", 2)
    if filler is not None:
        other, pairs = after((other, pairs), filler)
    first = [
        (rows(4 * r, 1).astype(F32) + other[r * block : (r + 1) * block].astype(F32)).astype(BF16)
        for r in range(count)
    ]
    second = rows(2, 2).astype(F32)
    for term in pairs:
        second = second + term.astype(F32)
    second = second.astype(BF16)
    lows = [first[0]] + [xor_send(first[r], "fsdp", r) for r in range(1, count)]
    return lows, [second[:block], xor_send(second[block:], "ctx", 2)]


def natural_columns(x, count):
    width = x.shape[1] // count
    order = [(i & ~3) | ((i & 1) << 1) | ((i >> 1) & 1) for i in range(count)]
    return jnp.concatenate([x[:, i * width : (i + 1) * width] for i in order], axis=1)


ROWS = 16


def over_rows(number, body, carry=None):
    def step(i, carry):
        return body(pl.multiple_of(i * ROWS, ROWS), carry)

    return lax.fori_loop(0, number // ROWS, step, carry)


def row_scale(x):
    return lax.rsqrt(jnp.mean(x * x, axis=-1, keepdims=True) + eps)


def entry_kernel(count, tok_ref, cot_ref, gain_ref, h_ref, x_ref, c_ref):
    def body(at, carry):
        rows = pl.ds(at, ROWS)
        x = natural_columns(tok_ref[rows, :], count)
        x_ref[rows, :] = x
        wide = x.astype(F32)
        h_ref[rows, :] = (wide * row_scale(wide) * gain_ref[...]).astype(BF16)
        c_ref[rows, :] = natural_columns(cot_ref[rows, :], count)
        return carry

    over_rows(tok_ref.shape[0], body, 0)


def sum_terms(refs, rows):
    total = refs[0][rows, :].astype(F32)
    for ref in refs[1:]:
        total = total + ref[rows, :].astype(F32)
    return total


def middle_kernel(lows, highs, *refs):
    x_ref, gain_ref, x2_ref, h_ref = refs[0], refs[1], refs[-2], refs[-1]
    block = x_ref.shape[0] // 2
    for half, terms in ((0, refs[2 : 2 + lows]), (1, refs[2 + lows : 2 + lows + highs])):

        def body(at, carry):
            rows = pl.ds(half * block + at, ROWS)
            x2 = x_ref[rows, :].astype(F32) + sum_terms(terms, pl.ds(at, ROWS))
            x2_ref[rows, :] = x2
            h_ref[rows, :] = (x2 * row_scale(x2) * gain_ref[...]).astype(BF16)
            return carry

        over_rows(block, body, 0)


def result_kernel(lows, highs, count, *refs):
    x_ref, out_ref = refs[0], refs[-1]
    block = x_ref.shape[0] // 2
    for half, terms in ((0, refs[1 : 1 + lows]), (1, refs[1 + lows : 1 + lows + highs])):

        def body(at, carry):
            rows = pl.ds(half * block + at, ROWS)
            total = x_ref[rows, :] + sum_terms(terms, pl.ds(at, ROWS))
            out_ref[rows, :] = natural_columns(total, count).astype(BF16)
            return carry

        over_rows(block, body, 0)


def back_kernel(lows, highs, count, *refs):
    base_ref, x_ref, gain_ref = refs[:3]
    wide_ref, gain_out = refs[3 + lows + highs], refs[-1]
    low_ref = refs[4 + lows + highs] if count is None else None
    block = x_ref.shape[0] // 2
    total = jnp.zeros((ROWS, x_ref.shape[1]), F32) if count is None else 0
    for half, terms in ((0, refs[3 : 3 + lows]), (1, refs[3 + lows : 3 + lows + highs])):

        def body(at, carry):
            rows = pl.ds(half * block + at, ROWS)
            grad = sum_terms(terms, pl.ds(at, ROWS))
            x = x_ref[rows, :].astype(F32)
            scale = row_scale(x)
            unit = x * scale
            scaled = grad * gain_ref[...]
            out = base_ref[rows, :].astype(F32) + scale * (
                scaled - unit * jnp.mean(scaled * unit, axis=-1, keepdims=True)
            )
            if count is None:
                wide_ref[rows, :] = out
                low_ref[rows, :] = out.astype(BF16)
            else:
                wide_ref[rows, :] = natural_columns(out, count)
            return carry + grad * unit if count is None else carry

        total = over_rows(block, body, total)
    if count is None:
        gain_out[...] = jnp.sum(total, axis=0, keepdims=True)


def row_pass(kernel, args, outs, name):
    return pl.pallas_call(
        kernel,
        out_shape=outs,
        compiler_params=vmem_limit(40),
        cost_estimate=pl.CostEstimate(
            flops=10 * args[0].size, bytes_accessed=10 * args[0].size, transcendentals=0
        ),
        name=name,
    )(*args)


def pair_columns(weights, pair, ways):
    shares = []
    for place in (pair, 1 - pair):
        parts = []
        for weight in weights:
            columns = weight.shape[1] // ways
            parts.append(lax.dynamic_slice_in_dim(weight, place * columns, columns, 1))
        shares.append(jnp.concatenate(parts, axis=1))
    return shares


def swap_shards(mine, theirs, pair):
    theirs = xor_send(theirs, "ctx", 2)
    return jnp.concatenate(
        [jnp.where(pair == 0, mine, theirs), jnp.where(pair == 0, theirs, mine)], axis=0
    )


def ctx_gather(rows, ways):
    groups = pair_groups(lax.axis_size("ctx")) if ways == 2 else None
    return lax.all_gather(rows, "ctx", axis=0, tiled=True, axis_index_groups=groups)


def ctx_scatter(rows, ways):
    groups = pair_groups(lax.axis_size("ctx")) if ways == 2 else None
    return lax.psum_scatter(
        rows, "ctx", scatter_dimension=0, tiled=True, axis_index_groups=groups
    )


def gather_weight(shard, ways):
    full = ctx_gather(shard, ways)
    return swap_blocks(full, lax.axis_size("ctx"), 0) if ways == 1 else full


def scatter_weight(grad, ways):
    if ways == 1:
        grad = swap_blocks(grad, lax.axis_size("ctx"), 0)
    return ctx_scatter(grad, ways)


def own_kernel(plan, pair_ref, both_ref, other_ref, *outs):
    pair = pair_ref[0]
    rows, width = other_ref.shape
    mine = pl.ds(pl.multiple_of(pair * rows, rows), rows)
    for source, columns, target, place in plan:
        half = outs[target].shape[1] // 2
        for ref, at, which in ((both_ref, mine, pair), (other_ref, slice(None), 1 - pair)):
            start = pl.multiple_of(which * half + place, HD)
            outs[target][:, pl.ds(start, columns)] = ref[at, source : source + columns].astype(F32)


def own_rows(both, pair, ways, plan, widths):
    if ways == 1:
        return [
            jnp.concatenate([both[:, s : s + n] for s, n, t, _ in plan if t == i], axis=1).astype(F32)
            for i in range(len(widths))
        ]
    rows = both.shape[0] // 2
    other = xor_send(lax.dynamic_slice_in_dim(both, (1 - pair) * rows, rows, 0), "ctx", 2)
    shapes = tuple(jax.ShapeDtypeStruct((rows, 2 * width), F32) for width in widths)
    whole = [pl.BlockSpec(t.shape, lambda i, m: (0, 0)) for t in (both, other) + shapes]
    return pl.pallas_call(
        functools.partial(own_kernel, plan),
        out_shape=shapes,
        grid_spec=pltpu.PrefetchScalarGridSpec(
            num_scalar_prefetch=1,
            grid=(1,),
            in_specs=whole[:2],
            out_specs=tuple(whole[2:]),
        ),
        cost_estimate=pl.CostEstimate(flops=0, bytes_accessed=8 * both.size, transcendentals=0),
        name="own_rows",
    )(pair.reshape(1), both, other)


def butterfly_sum(value):
    for axis in ("ctx", "fsdp"):
        step = 1
        while step < lax.axis_size(axis):
            value = value + xor_send(value, axis, step)
            step *= 2
    return value


def dot(left, right):
    return jnp.dot(left, right, preferred_element_type=F32)


def dot_rows(left, right):
    return lax.dot_general(left, right, (((0,), (0,)), ((), ())), preferred_element_type=F32)


def dot_cols(left, right):
    return lax.dot_general(left, right, (((1,), (1,)), ((), ())), preferred_element_type=F32)


def vmem_limit(mib):
    return pltpu.CompilerParams(vmem_limit_bytes=mib * 1024 * 1024)


def prep_kernel(query_heads, groups, raw_ref, cos_ref, sin_ref, gq_ref, gk_ref, q_ref, kv_ref):
    cos = cos_ref[...]
    sin = sin_ref[...]

    def rotate_norm(x, gain):
        scale = lax.rsqrt(jnp.mean(x * x, axis=-1, keepdims=True) + eps)
        u = x * scale * gain
        return u * cos + pltpu.roll(u, HD // 2, 1) * sin

    for h in range(query_heads):
        cols = slice(h * HD, (h + 1) * HD)
        q_ref[:, cols] = rotate_norm(raw_ref[:, cols], gq_ref[...]).astype(BF16)
    for h in range(2 * groups):
        x = raw_ref[:, (query_heads + h) * HD : (query_heads + h + 1) * HD]
        if h % 2 == 0:
            x = rotate_norm(x, gk_ref[...])
        kv_ref[:, h * HD : (h + 1) * HD] = x.astype(BF16)


def head_prep(raw, cos, sin, gq, gk, query_heads, groups):
    rows, width = raw.shape
    tile = 256
    vec = pl.BlockSpec((1, HD), lambda i: (0, 0))
    tab = pl.BlockSpec((tile, HD), lambda i: (i, 0))
    return pl.pallas_call(
        functools.partial(prep_kernel, query_heads, groups),
        out_shape=(
            jax.ShapeDtypeStruct((rows, query_heads * HD), BF16),
            jax.ShapeDtypeStruct((rows, 2 * groups * HD), BF16),
        ),
        grid=(rows // tile,),
        in_specs=[pl.BlockSpec((tile, width), lambda i: (i, 0)), tab, tab, vec, vec],
        out_specs=(
            pl.BlockSpec((tile, query_heads * HD), lambda i: (i, 0)),
            pl.BlockSpec((tile, 2 * groups * HD), lambda i: (i, 0)),
        ),
        cost_estimate=pl.CostEstimate(
            flops=20 * raw.size, bytes_accessed=6 * raw.size, transcendentals=0
        ),
        name="head_prep",
    )(raw, cos, sin, gq, gk)


def prep_back_kernel(heads, plain, d_ref, raw_ref, cos_ref, sin_ref, g_ref, out_ref, gain_ref):
    cos = cos_ref[...]
    sin = sin_ref[...]
    gain = g_ref[...]
    gain_sum = jnp.zeros((1, HD), F32)
    for h in range(heads):
        cols = slice(h * HD, (h + 1) * HD)
        d = d_ref[:, cols].astype(F32)
        if plain and h % 2 == 1:
            out_ref[:, cols] = d.astype(BF16)
            continue
        x = raw_ref[:, cols]
        t = d * cos - pltpu.roll(d, HD // 2, 1) * sin
        scale = lax.rsqrt(jnp.mean(x * x, axis=-1, keepdims=True) + eps)
        n = x * scale
        gain_sum = gain_sum + jnp.sum(t * n, axis=0, keepdims=True)
        e = t * gain
        out_ref[:, cols] = (scale * (e - n * jnp.mean(e * n, axis=-1, keepdims=True))).astype(BF16)

    @pl.when(pl.program_id(0) == 0)
    def _():
        gain_ref[...] = jnp.zeros_like(gain_ref)

    gain_ref[...] += gain_sum


def head_prep_back(grad, raw, cos, sin, gain, raw_block, plain):
    rows, width = grad.shape
    tile = 256
    tab = pl.BlockSpec((tile, HD), lambda i: (i, 0))
    return pl.pallas_call(
        functools.partial(prep_back_kernel, width // HD, plain),
        out_shape=(
            jax.ShapeDtypeStruct((rows, width), BF16),
            jax.ShapeDtypeStruct((1, HD), F32),
        ),
        grid=(rows // tile,),
        in_specs=[
            pl.BlockSpec((tile, width), lambda i: (i, 0)),
            pl.BlockSpec((tile, width), lambda i: (i, raw_block)),
            tab,
            tab,
            pl.BlockSpec((1, HD), lambda i: (0, 0)),
        ],
        out_specs=(
            pl.BlockSpec((tile, width), lambda i: (i, 0)),
            pl.BlockSpec((1, HD), lambda i: (0, 0)),
        ),
        cost_estimate=pl.CostEstimate(
            flops=20 * rows * width, bytes_accessed=10 * rows * width, transcendentals=0
        ),
        name="head_prep_back",
    )(grad, raw, cos, sin, gain)


def block_place(pair, shard, place, ways, count):
    owner = shard
    if ways == 2:
        other = (pair + place % 2) % 2 if isinstance(pair, int) else lax.rem(pair + place % 2, 2)
        owner = (shard // 2) * 4 + 2 * other + shard % 2
    return owner if place < ways else 2 * count - 1 - owner


def load_sequence(pair, ways, kv_ref, keys, values):
    shards, _, _, block, _ = kv_ref.shape
    for shard in range(shards):
        for place in range(2 * ways):
            index = block_place(pair, shard, place, ways, shards * ways)
            rows = pl.ds(pl.multiple_of(index * block, block), block)
            keys[rows, :] = kv_ref[shard, 0, place, :, :HD]
            values[rows, :] = kv_ref[shard, 0, place, :, HD:]


def stack_heads(tile, count):
    return jnp.concatenate([tile[:, h * HD : (h + 1) * HD] for h in range(count)], axis=0)


def row_positions(info_ref, place, block, count):
    base = pl.program_id(0) * (info_ref.shape[0] // pl.num_programs(0)) + 1 + 3 * place
    first = info_ref[base]
    lane = lax.broadcasted_iota(jnp.int32, (1, count * block), 1)
    position = first + lax.rem(lane, block)
    start_first, start_last = info_ref[base + 1], info_ref[base + 2]
    start = jnp.where(position >= start_last, start_last, start_first)
    return position, start, start_first // CHUNK, (first + block - 1) // CHUNK + 1


def valid_tile(chunk, position, start, shape):
    key_index = chunk * CHUNK + lax.broadcasted_iota(jnp.int32, shape, 0)
    return (key_index <= position) & (key_index >= start)


def forward_kernel(ways, count, info_ref, q_ref, kv_ref, o_ref, lse_ref, keys, values):
    load_sequence(info_ref[0], ways, kv_ref, keys, values)
    block = q_ref.shape[2]
    columns = count * block
    for place in range(2 * ways):
        queries = stack_heads(q_ref[0, place], count)
        position, start, low, high = row_positions(info_ref, place, block, count)

        def body(chunk, carry):
            total, norm = carry
            rows = pl.ds(pl.multiple_of(chunk * CHUNK, CHUNK), CHUNK)
            score = dot_cols(keys[rows, :], queries)
            weight = jnp.where(
                valid_tile(chunk, position, start, score.shape), jnp.exp2(score * EXP2_SCALE), 0.0
            )
            norm = norm + jnp.sum(weight, axis=0, keepdims=True)
            total = total + dot_rows(values[rows, :], weight.astype(BF16))
            return total, norm

        total, norm = lax.fori_loop(
            low, high, body, (jnp.zeros((HD, columns), F32), jnp.zeros((1, columns), F32))
        )
        out = (total / norm).T.astype(BF16)
        for h in range(count):
            o_ref[0, place, :, h * HD : (h + 1) * HD] = out[h * block : (h + 1) * block]
        lse_ref[0, 0, place] = jnp.log2(norm)


def backward_kernel(
    ways, count, info_ref, q_ref, do_ref, o_ref, lse_ref, kv_ref,
    dq_ref, dkv_ref, keys, values, grad_k, grad_v,
):
    pair = info_ref[0]
    load_sequence(pair, ways, kv_ref, keys, values)
    block = q_ref.shape[2]
    columns = count * block
    grad_k[...] = jnp.zeros_like(grad_k)
    grad_v[...] = jnp.zeros_like(grad_v)
    for place in range(2 * ways):
        queries = stack_heads(q_ref[0, place], count)
        grads = stack_heads(do_ref[0, place], count)
        outs = stack_heads(o_ref[0, place], count)
        delta = jnp.sum((grads.astype(F32) * outs.astype(F32)).T, axis=0, keepdims=True)
        lse = lse_ref[0, 0, place]
        position, start, low, high = row_positions(info_ref, place, block, count)

        def body(chunk, total):
            rows = pl.ds(pl.multiple_of(chunk * CHUNK, CHUNK), CHUNK)
            key_rows = keys[rows, :]
            score = dot_cols(key_rows, queries)
            prob = jnp.where(
                valid_tile(chunk, position, start, score.shape),
                jnp.exp2(score * EXP2_SCALE - lse),
                0.0,
            )
            grad_prob = dot_cols(values[rows, :], grads)
            grad_score = (prob * (grad_prob - delta)).astype(BF16)
            grad_v[rows, :] += dot(prob.astype(BF16), grads)
            grad_k[rows, :] += dot(grad_score, queries)
            return total + dot_rows(key_rows, grad_score)

        total = lax.fori_loop(low, high, body, jnp.zeros((HD, columns), F32))
        out = total.T * SCALE
        for h in range(count):
            dq_ref[0, place, :, h * HD : (h + 1) * HD] = out[h * block : (h + 1) * block]
    shards = dkv_ref.shape[0]
    for shard in range(shards):
        for place in range(2 * ways):
            index = block_place(pair, shard, place, ways, shards * ways)
            rows = pl.ds(pl.multiple_of(index * block, block), block)
            dkv_ref[shard, 0, place, :, :HD] = (grad_k[rows, :] * SCALE).astype(BF16)
            dkv_ref[shard, 0, place, :, HD:] = grad_v[rows, :].astype(BF16)


def attention_specs(q, kv, count):
    shards, sequences, places, block, width = kv.shape
    row = pl.BlockSpec((1, places, block, count * HD), lambda s, n, i: (s, 0, 0, n))
    part = pl.BlockSpec((shards, 1, places, block, 2 * HD), lambda s, n, i: (0, s, 0, 0, n))
    sums = pl.BlockSpec((1, 1, places, 1, count * block), lambda s, n, i: (s, n, 0, 0, 0))
    sums_shape = (sequences, width // (2 * HD), places, 1, count * block)
    return row, part, sums, sums_shape, shards * places * block


def attend(info, q, kv, count, ways):
    row, part, sums, sums_shape, length = attention_specs(q, kv, count)
    return pl.pallas_call(
        functools.partial(forward_kernel, ways, count),
        out_shape=(
            jax.ShapeDtypeStruct(q.shape, BF16),
            jax.ShapeDtypeStruct(sums_shape, F32),
        ),
        grid_spec=pltpu.PrefetchScalarGridSpec(
            num_scalar_prefetch=1,
            grid=sums_shape[:2],
            in_specs=[row, part],
            out_specs=(row, sums),
            scratch_shapes=[pltpu.VMEM((length, HD), BF16)] * 2,
        ),
        compiler_params=vmem_limit(48),
        cost_estimate=pl.CostEstimate(
            flops=4 * 8 * CHUNK * q.size, bytes_accessed=2 * kv.size, transcendentals=0
        ),
        name="attend",
    )(info, q, kv)


def attend_back(info, q, grad, out, lse, kv, count, ways):
    row, part, sums, sums_shape, length = attention_specs(q, kv, count)
    return pl.pallas_call(
        functools.partial(backward_kernel, ways, count),
        out_shape=(
            jax.ShapeDtypeStruct(q.shape, F32),
            jax.ShapeDtypeStruct(kv.shape, BF16),
        ),
        grid_spec=pltpu.PrefetchScalarGridSpec(
            num_scalar_prefetch=1,
            grid=sums_shape[:2],
            in_specs=[row, row, row, sums, part],
            out_specs=(row, part),
            scratch_shapes=[pltpu.VMEM((length, HD), BF16)] * 2
            + [pltpu.VMEM((length, HD), F32)] * 2,
        ),
        compiler_params=vmem_limit(56),
        cost_estimate=pl.CostEstimate(
            flops=10 * 8 * CHUNK * q.size, bytes_accessed=4 * kv.size, transcendentals=0
        ),
        name="attend_back",
    )(info, q, grad, out, lse, kv)


def interleave_heads(first, second):
    rows, width = first.shape
    heads = width // HD
    both = jnp.stack([first.reshape(rows, heads, HD), second.reshape(rows, heads, HD)], axis=2)
    return both.reshape(rows, 2 * width)


def after(value, earlier):
    return lax.optimization_barrier((value, earlier))[0]


def local(
    tokens,
    grad_out,
    segments,
    w_query,
    key_weight_matrix,
    value_weight_matrix,
    w_output,
    w_gate,
    w_up,
    w_down,
    norm_attn,
    norm_mlp,
    norm_query,
    norm_key,
):
    ctx_count = lax.axis_size("ctx")
    seq_count = lax.axis_size("fsdp")
    me = lax.axis_index("ctx").astype(jnp.int32)
    my_seq = lax.axis_index("fsdp").astype(jnp.int32)
    pair = lax.rem(me // 2, 2)
    block = tokens.shape[3]
    width = tokens.shape[4]
    own = 2 * block
    ways = 2 if (key_weight_matrix.shape[1] // HD) % 2 == 0 else 1
    query_heads = w_query.shape[1] // HD // ways
    groups = key_weight_matrix.shape[1] // HD // ways
    count = query_heads // groups
    q_width, kv_width = query_heads * HD, 2 * groups * HD
    hidden = w_gate.shape[1] // 2

    w_kv = interleave_heads(key_weight_matrix, value_weight_matrix)
    gain_attn_row = swap_blocks(norm_attn[None], ctx_count, 1)
    gain_mlp_row = swap_blocks(norm_mlp[None], ctx_count, 1)

    if ways == 2:
        qkv_shard = swap_shards(*pair_columns([w_query, w_kv], pair, 2), pair)
        output_shard = swap_shards(*pair_columns([w_output], pair, 2), pair)
    else:
        qkv_shard, output_shard = jnp.concatenate([w_query, w_kv], axis=1), w_output
    full_qkv = gather_weight(qkv_shard, ways)
    full_output = gather_weight(output_shard, ways)

    row_bf16 = jax.ShapeDtypeStruct((own, width), BF16)
    row_f32 = jax.ShapeDtypeStruct((own, width), F32)
    gain_shape = jax.ShapeDtypeStruct((1, width), F32)
    h1_own, inputs, cot_own = row_pass(
        functools.partial(entry_kernel, ctx_count),
        (tokens.reshape(own, width), grad_out.reshape(own, width), gain_attn_row),
        (row_bf16, row_bf16, row_bf16),
        "entry",
    )
    h1 = gather_rows(h1_own, ways)

    offsets = jnp.arange(block, dtype=jnp.int32)
    owners = [me, me + 2 - 4 * pair][:ways]
    firsts = [o * block for o in owners + [2 * ctx_count - 1 - o for o in owners]]
    freq = jnp.exp(jnp.arange(HD // 2, dtype=F32) * (-2.0 * math.log(rope_base) / HD))
    infos, positions = [], []
    for r in range(seq_count):
        line = lax.dynamic_index_in_dim(
            segments, lax.bitwise_xor(my_seq, jnp.int32(r)), 0, keepdims=False
        )
        doc_first = [jnp.sum((line < d).astype(jnp.int32)) for d in range(DOCS)]
        scalars = [pair]
        for first in firsts:
            mine = lax.dynamic_slice_in_dim(line, first, block)
            start = sum(jnp.where(mine == d, doc_first[d], 0) for d in range(DOCS))
            scalars += [first, start[0], start[block - 1]]
            positions.append(first + offsets - start)
        infos += scalars
    info = jnp.stack(infos)
    angle = jnp.concatenate(positions).astype(F32)[:, None] * freq
    cos, sin = jnp.cos(angle), jnp.sin(angle)
    cos, sin = jnp.concatenate([cos, cos], 1), jnp.concatenate([-sin, sin], 1)
    gain_q, gain_k = norm_query.reshape(1, HD), norm_key.reshape(1, HD)

    raw = dot(h1, full_qkv)
    q, kv = head_prep(raw, cos, sin, gain_q, gain_k, query_heads, groups)
    q = q.reshape(seq_count, 2 * ways, block, q_width)

    mine, theirs = pair_columns([w_gate, w_up, w_down], pair, 2)
    shards = swap_shards(mine, after(theirs, h1), pair)
    full_kv = ctx_gather(after(kv, full_output), ways).reshape(-1, seq_count, 2 * ways, block, kv_width)
    shards = after(shards, kv)
    full_gate, full_up, full_down = (
        gather_weight(shards[:, i * hidden : (i + 1) * hidden], 2) for i in range(3)
    )
    cot_all = gather_rows(after(cot_own, shards), 2)

    q = after(q, cot_all)
    heads, lse = attend(info, q, full_kv, count, ways)
    mixed = heads.reshape(-1, q_width)
    lows, highs = return_rows(dot_cols(mixed, full_output).astype(BF16), ways)
    x2, h2_own = row_pass(
        functools.partial(middle_kernel, len(lows), len(highs)),
        (inputs, gain_mlp_row, *lows, *highs),
        (row_f32, row_bf16),
        "middle",
    )
    h2 = gather_rows(h2_own, 2)

    gate = dot(h2, full_gate)
    up = dot(h2, full_up)
    act = lax.optimization_barrier((gate / (1.0 + jnp.exp(-gate)) * up).astype(BF16))
    grad_down = dot_rows(cot_all, act).astype(BF16)
    d_act = dot(after(cot_all, grad_down), full_down)
    sg = 1.0 / (1.0 + jnp.exp(-gate))
    d_gate = (d_act * up * sg * (1.0 + gate * (1.0 - sg))).astype(BF16)
    d_up = (d_act * gate * sg).astype(BF16)
    d_h2_part = (dot_cols(d_gate, full_gate) + dot_cols(d_up, full_up)).astype(BF16)
    h2_late = after(h2, d_h2_part)
    grad_gate = dot_rows(h2_late, d_gate).astype(BF16)
    grad_up = dot_rows(h2_late, d_up).astype(BF16)
    lows, highs = return_rows(d_h2_part, 2, (grad_gate, grad_up))
    returned = (lows[0], highs[0])
    d_x2, d_x2_low, gain_mlp = row_pass(
        functools.partial(back_kernel, len(lows), len(highs), None),
        (cot_own, x2, gain_mlp_row, *lows, *highs),
        (row_f32, row_bf16, gain_shape),
        "middle_back",
    )
    y_part = dot_cols(after(act, d_x2_low), full_down).astype(BF16)
    branch = after(gather_rows(d_x2_low, ways), y_part)
    rows_down = scatter_weight(grad_down, 2)
    rows_gate = scatter_weight(after(grad_gate, (rows_down, returned)), 2)
    def one(both, split):
        return own_rows(both, pair, split, [(0, both.shape[1], 0, 0)], [both.shape[1]])[0]

    d_att = dot(branch, full_output).astype(BF16).reshape(q.shape)
    rows_up = scatter_weight(after(grad_up, (rows_gate, d_att)), 2)
    grad_output = dot_rows(branch, mixed).astype(BF16)
    rows_output = scatter_weight(after(grad_output, rows_gate), ways)
    shard_down = one(rows_down, 2)
    shard_gate = one(rows_gate, 2)
    shard_up = one(rows_up, 2)
    d_q, d_kv = attend_back(info, q, d_att, heads, lse, full_kv, count, ways)
    y_lows, y_highs = return_rows(after(y_part, branch), 2, d_q)
    out_tokens = row_pass(
        functools.partial(result_kernel, len(y_lows), len(y_highs), ctx_count),
        (x2, *y_lows, *y_highs),
        row_bf16,
        "result",
    ).reshape(tokens.shape)
    d_qp, gain_q_sum = head_prep_back(
        d_q.reshape(-1, q_width), raw, cos, sin, gain_q, 0, False
    )
    d_h1_query = dot_cols(d_qp, full_qkv[:, :q_width])
    d_kv = after(
        d_kv.reshape(-1, kv_width),
        (rows_output, d_h1_query, out_tokens, shard_down, shard_gate, shard_up),
    )
    d_kv = ctx_scatter(d_kv, ways)
    grad_query = dot_rows(h1, d_qp).astype(BF16)
    rows_query = scatter_weight(after(grad_query, d_kv), ways)
    d_kvp, gain_k_sum = head_prep_back(d_kv, raw, cos, sin, gain_k, q_width // kv_width, True)
    grad_kv = dot_rows(h1, d_kvp).astype(BF16)
    rows_kv = scatter_weight(grad_kv, ways)
    d_h1 = (
        d_h1_query + dot_cols(after(d_kvp, grad_kv), full_qkv[:, q_width:])
    ).astype(BF16)
    gain_attn = jnp.sum(d_h1.astype(F32) * h1.astype(F32), axis=0) / gain_attn_row[0]
    gains = butterfly_sum(
        jnp.concatenate([gain_attn, gain_mlp[0], gain_q_sum[0], gain_k_sum[0]])
    )
    lows, highs = return_rows(d_h1, ways)
    lows[0] = after(lows[0], gains)
    grad_tokens = row_pass(
        functools.partial(back_kernel, len(lows), len(highs), ctx_count),
        (d_x2, inputs, gain_attn_row, *lows, *highs),
        row_f32,
        "entry_back",
    )
    rows_output, rows_query, rows_kv = after((rows_output, rows_query, rows_kv), (lows, highs))
    shard_output = one(rows_output, ways)
    shard_query = one(rows_query, ways)
    plan = []
    for h in range(groups):
        for t in (0, 1):
            plan.append(((2 * h + t) * HD, HD, t, h * HD))
    shard_key, shard_value = own_rows(rows_kv, pair, ways, plan, [groups * HD, groups * HD])
    grad_tokens = grad_tokens.reshape(tokens.shape)
    return (
        out_tokens,
        grad_tokens,
        shard_query,
        shard_key,
        shard_value,
        shard_output,
        shard_gate,
        shard_up,
        shard_down,
        swap_blocks(gains[None, :width], ctx_count, 1)[0],
        swap_blocks(gains[None, width : 2 * width], ctx_count, 1)[0],
        gains[2 * width : 2 * width + HD],
        gains[2 * width + HD :],
    )


def solution(mesh):
    block = P("fsdp", "ctx", None, None, None)
    weight = P("ctx", "fsdp")
    return jax.shard_map(
        local,
        mesh=mesh,
        in_specs=(block, block, P()) + (weight,) * 7 + (P(),) * 4,
        out_specs=(block, block) + (weight,) * 7 + (P(),) * 4,
        check_vma=False,
    )
```

```python
import functools
import math

import jax
import jax.numpy as jnp
from jax import lax
from jax.experimental import pallas as pl
from jax.experimental.pallas import tpu as pltpu
from jax.sharding import PartitionSpec as P

QUERY_HEADS = 16
KEY_VALUE_HEADS = 8
HD = 128
DOCS = 4
CHUNK = 256
eps = 1e-06
rope_base = 1000000.0
SCALE = HD ** (-0.5)
EXP2_SCALE = SCALE * math.log2(math.e)
F32 = jnp.float32
BF16 = jnp.bfloat16


def xor_send(value, axis, step):
    count = lax.axis_size(axis)
    return lax.ppermute(value, axis, [(i, i ^ step) for i in range(count)])


def exchange_rows(rows, axis):
    return [rows] + [xor_send(rows, axis, r) for r in range(1, lax.axis_size(axis))]


def scatter_rows(partial, axis):
    count = lax.axis_size(axis)
    rows = partial.shape[0] // count
    total = partial[:rows].astype(F32)
    for r in range(1, count):
        total = total + xor_send(partial[r * rows : (r + 1) * rows], axis, r).astype(F32)
    return total


def pair_groups(count):
    return [[i for i in range(count) if (i >> 1) & 1 == bit] for bit in (0, 1)]


def swap_blocks(x, count, axis):
    shape = x.shape
    split = x.reshape(shape[:axis] + (count // 4, 2, 2, shape[axis] // count) + shape[axis + 1 :])
    return split.swapaxes(axis + 1, axis + 2).reshape(shape)


def assemble_kernel(plan, *refs):
    out_ref = refs[-1]
    place = 0
    for index, start, number in plan:
        out_ref[place : place + number, :] = refs[index][start : start + number, :]
        place += number


def assemble(arrays, plan):
    width = arrays[0].shape[1]
    rows = sum(number for _, _, number in plan)
    return pl.pallas_call(
        functools.partial(assemble_kernel, plan),
        out_shape=jax.ShapeDtypeStruct((rows, width), arrays[0].dtype),
        compiler_params=vmem_limit(32),
        cost_estimate=pl.CostEstimate(
            flops=0, bytes_accessed=4 * rows * width, transcendentals=0
        ),
        name="assemble",
    )(*arrays)


def gather_rows(rows, ways):
    count = lax.axis_size("fsdp")
    total = rows.shape[0]
    if ways == 1:
        return assemble(exchange_rows(rows, "fsdp"), [(r, 0, total) for r in range(count)])
    block = total // 2
    low = rows[:block]
    lows = exchange_rows(low, "fsdp")
    high = jnp.concatenate([rows[block:], xor_send(rows[block:], "ctx", 2)], axis=0)
    highs = exchange_rows(high, "fsdp")
    others = xor_send(jnp.concatenate(lows, axis=0), "ctx", 2)
    plan = []
    for r in range(count):
        plan += [(1 + r, 0, block), (0, r * block, block), (1 + count + r, 0, 2 * block)]
    return assemble([others] + lows + highs, plan)


def return_rows(partial, ways, filler=None):
    count = lax.axis_size("fsdp")
    if ways == 1:
        rows = partial.shape[0] // count
        terms = [partial[:rows]] + [
            xor_send(partial[r * rows : (r + 1) * rows], "fsdp", r) for r in range(1, count)
        ]
        return [t[: rows // 2] for t in terms], [t[rows // 2 :] for t in terms]
    block = partial.shape[0] // (4 * count)

    def rows(start, number):
        return partial[start * block : (start + number) * block]

    sent = jnp.concatenate([rows(4 * r + 1, 1) for r in range(count)], axis=0)
    pairs = [xor_send(rows(4 * r + 2, 2), "fsdp", r) for r in range(1, count)]
    other = xor_send(sent, "ctx", 2)
    if filler is not None:
        other, pairs = after((other, pairs), filler)
    first = [
        (rows(4 * r, 1).astype(F32) + other[r * block : (r + 1) * block].astype(F32)).astype(BF16)
        for r in range(count)
    ]
    second = rows(2, 2).astype(F32)
    for term in pairs:
        second = second + term.astype(F32)
    second = second.astype(BF16)
    lows = [first[0]] + [xor_send(first[r], "fsdp", r) for r in range(1, count)]
    return lows, [second[:block], xor_send(second[block:], "ctx", 2)]


def natural_columns(x, count):
    width = x.shape[1] // count
    order = [(i & ~3) | ((i & 1) << 1) | ((i >> 1) & 1) for i in range(count)]
    return jnp.concatenate([x[:, i * width : (i + 1) * width] for i in order], axis=1)


ROWS = 16


def over_rows(number, body, carry=None):
    def step(i, carry):
        return body(pl.multiple_of(i * ROWS, ROWS), carry)

    return lax.fori_loop(0, number // ROWS, step, carry)


def row_scale(x):
    return lax.rsqrt(jnp.mean(x * x, axis=-1, keepdims=True) + eps)


def entry_kernel(count, tok_ref, cot_ref, gain_ref, h_ref, x_ref, c_ref):
    def body(at, carry):
        rows = pl.ds(at, ROWS)
        x = natural_columns(tok_ref[rows, :], count)
        x_ref[rows, :] = x
        wide = x.astype(F32)
        h_ref[rows, :] = (wide * row_scale(wide) * gain_ref[...]).astype(BF16)
        c_ref[rows, :] = natural_columns(cot_ref[rows, :], count)
        return carry

    over_rows(tok_ref.shape[0], body, 0)


def sum_terms(refs, rows):
    total = refs[0][rows, :].astype(F32)
    for ref in refs[1:]:
        total = total + ref[rows, :].astype(F32)
    return total


def middle_kernel(lows, highs, *refs):
    x_ref, gain_ref, x2_ref, h_ref = refs[0], refs[1], refs[-2], refs[-1]
    block = x_ref.shape[0] // 2
    for half, terms in ((0, refs[2 : 2 + lows]), (1, refs[2 + lows : 2 + lows + highs])):

        def body(at, carry):
            rows = pl.ds(half * block + at, ROWS)
            x2 = x_ref[rows, :].astype(F32) + sum_terms(terms, pl.ds(at, ROWS))
            x2_ref[rows, :] = x2
            h_ref[rows, :] = (x2 * row_scale(x2) * gain_ref[...]).astype(BF16)
            return carry

        over_rows(block, body, 0)


def result_kernel(lows, highs, count, *refs):
    x_ref, out_ref = refs[0], refs[-1]
    block = x_ref.shape[0] // 2
    for half, terms in ((0, refs[1 : 1 + lows]), (1, refs[1 + lows : 1 + lows + highs])):

        def body(at, carry):
            rows = pl.ds(half * block + at, ROWS)
            total = x_ref[rows, :] + sum_terms(terms, pl.ds(at, ROWS))
            out_ref[rows, :] = natural_columns(total, count).astype(BF16)
            return carry

        over_rows(block, body, 0)


def back_kernel(lows, highs, count, *refs):
    base_ref, x_ref, gain_ref = refs[:3]
    wide_ref, gain_out = refs[3 + lows + highs], refs[-1]
    low_ref = refs[4 + lows + highs] if count is None else None
    block = x_ref.shape[0] // 2
    total = jnp.zeros((ROWS, x_ref.shape[1]), F32) if count is None else 0
    for half, terms in ((0, refs[3 : 3 + lows]), (1, refs[3 + lows : 3 + lows + highs])):

        def body(at, carry):
            rows = pl.ds(half * block + at, ROWS)
            grad = sum_terms(terms, pl.ds(at, ROWS))
            x = x_ref[rows, :].astype(F32)
            scale = row_scale(x)
            unit = x * scale
            scaled = grad * gain_ref[...]
            out = base_ref[rows, :].astype(F32) + scale * (
                scaled - unit * jnp.mean(scaled * unit, axis=-1, keepdims=True)
            )
            if count is None:
                wide_ref[rows, :] = out
                low_ref[rows, :] = out.astype(BF16)
            else:
                wide_ref[rows, :] = natural_columns(out, count)
            return carry + grad * unit if count is None else carry

        total = over_rows(block, body, total)
    if count is None:
        gain_out[...] = jnp.sum(total, axis=0, keepdims=True)


def row_pass(kernel, args, outs, name):
    return pl.pallas_call(
        kernel,
        out_shape=outs,
        compiler_params=vmem_limit(40),
        cost_estimate=pl.CostEstimate(
            flops=10 * args[0].size, bytes_accessed=10 * args[0].size, transcendentals=0
        ),
        name=name,
    )(*args)


def pair_columns(weights, pair, ways):
    shares = []
    for place in (pair, 1 - pair):
        parts = []
        for weight in weights:
            columns = weight.shape[1] // ways
            parts.append(lax.dynamic_slice_in_dim(weight, place * columns, columns, 1))
        shares.append(jnp.concatenate(parts, axis=1))
    return shares


def swap_shards(mine, theirs, pair):
    theirs = xor_send(theirs, "ctx", 2)
    return jnp.concatenate(
        [jnp.where(pair == 0, mine, theirs), jnp.where(pair == 0, theirs, mine)], axis=0
    )


def ctx_gather(rows, ways):
    groups = pair_groups(lax.axis_size("ctx")) if ways == 2 else None
    return lax.all_gather(rows, "ctx", axis=0, tiled=True, axis_index_groups=groups)


def ctx_scatter(rows, ways):
    groups = pair_groups(lax.axis_size("ctx")) if ways == 2 else None
    return lax.psum_scatter(
        rows, "ctx", scatter_dimension=0, tiled=True, axis_index_groups=groups
    )


def gather_weight(shard, ways):
    full = ctx_gather(shard, ways)
    return swap_blocks(full, lax.axis_size("ctx"), 0) if ways == 1 else full


def scatter_weight(grad, ways):
    if ways == 1:
        grad = swap_blocks(grad, lax.axis_size("ctx"), 0)
    return ctx_scatter(grad, ways)


def own_kernel(plan, pair_ref, both_ref, other_ref, *outs):
    pair = pair_ref[0]
    rows, width = other_ref.shape
    mine = pl.ds(pl.multiple_of(pair * rows, rows), rows)
    for source, columns, target, place in plan:
        half = outs[target].shape[1] // 2
        for ref, at, which in ((both_ref, mine, pair), (other_ref, slice(None), 1 - pair)):
            start = pl.multiple_of(which * half + place, HD)
            outs[target][:, pl.ds(start, columns)] = ref[at, source : source + columns].astype(F32)


def own_rows(both, pair, ways, plan, widths):
    if ways == 1:
        return [
            jnp.concatenate([both[:, s : s + n] for s, n, t, _ in plan if t == i], axis=1).astype(F32)
            for i in range(len(widths))
        ]
    rows = both.shape[0] // 2
    other = xor_send(lax.dynamic_slice_in_dim(both, (1 - pair) * rows, rows, 0), "ctx", 2)
    shapes = tuple(jax.ShapeDtypeStruct((rows, 2 * width), F32) for width in widths)
    whole = [pl.BlockSpec(t.shape, lambda i, m: (0, 0)) for t in (both, other) + shapes]
    return pl.pallas_call(
        functools.partial(own_kernel, plan),
        out_shape=shapes,
        grid_spec=pltpu.PrefetchScalarGridSpec(
            num_scalar_prefetch=1,
            grid=(1,),
            in_specs=whole[:2],
            out_specs=tuple(whole[2:]),
        ),
        cost_estimate=pl.CostEstimate(flops=0, bytes_accessed=8 * both.size, transcendentals=0),
        name="own_rows",
    )(pair.reshape(1), both, other)


def butterfly_sum(value):
    for axis in ("ctx", "fsdp"):
        step = 1
        while step < lax.axis_size(axis):
            value = value + xor_send(value, axis, step)
            step *= 2
    return value


def dot(left, right):
    return jnp.dot(left, right, preferred_element_type=F32)


def dot_rows(left, right):
    return lax.dot_general(left, right, (((0,), (0,)), ((), ())), preferred_element_type=F32)


def dot_cols(left, right):
    return lax.dot_general(left, right, (((1,), (1,)), ((), ())), preferred_element_type=F32)


def vmem_limit(mib):
    return pltpu.CompilerParams(vmem_limit_bytes=mib * 1024 * 1024)


def prep_kernel(query_heads, groups, raw_ref, cos_ref, sin_ref, gq_ref, gk_ref, q_ref, kv_ref):
    cos = cos_ref[...]
    sin = sin_ref[...]

    def rotate_norm(x, gain):
        scale = lax.rsqrt(jnp.mean(x * x, axis=-1, keepdims=True) + eps)
        u = x * scale * gain
        return u * cos + pltpu.roll(u, HD // 2, 1) * sin

    for h in range(query_heads):
        cols = slice(h * HD, (h + 1) * HD)
        q_ref[:, cols] = rotate_norm(raw_ref[:, cols], gq_ref[...]).astype(BF16)
    for h in range(2 * groups):
        x = raw_ref[:, (query_heads + h) * HD : (query_heads + h + 1) * HD]
        if h % 2 == 0:
            x = rotate_norm(x, gk_ref[...])
        kv_ref[:, h * HD : (h + 1) * HD] = x.astype(BF16)


def head_prep(raw, cos, sin, gq, gk, query_heads, groups):
    rows, width = raw.shape
    tile = 256
    vec = pl.BlockSpec((1, HD), lambda i: (0, 0))
    tab = pl.BlockSpec((tile, HD), lambda i: (i, 0))
    return pl.pallas_call(
        functools.partial(prep_kernel, query_heads, groups),
        out_shape=(
            jax.ShapeDtypeStruct((rows, query_heads * HD), BF16),
            jax.ShapeDtypeStruct((rows, 2 * groups * HD), BF16),
        ),
        grid=(rows // tile,),
        in_specs=[pl.BlockSpec((tile, width), lambda i: (i, 0)), tab, tab, vec, vec],
        out_specs=(
            pl.BlockSpec((tile, query_heads * HD), lambda i: (i, 0)),
            pl.BlockSpec((tile, 2 * groups * HD), lambda i: (i, 0)),
        ),
        cost_estimate=pl.CostEstimate(
            flops=20 * raw.size, bytes_accessed=6 * raw.size, transcendentals=0
        ),
        name="head_prep",
    )(raw, cos, sin, gq, gk)


def prep_back_kernel(heads, plain, d_ref, raw_ref, cos_ref, sin_ref, g_ref, out_ref, gain_ref):
    cos = cos_ref[...]
    sin = sin_ref[...]
    gain = g_ref[...]
    gain_sum = jnp.zeros((1, HD), F32)
    for h in range(heads):
        cols = slice(h * HD, (h + 1) * HD)
        d = d_ref[:, cols].astype(F32)
        if plain and h % 2 == 1:
            out_ref[:, cols] = d.astype(BF16)
            continue
        x = raw_ref[:, cols]
        t = d * cos - pltpu.roll(d, HD // 2, 1) * sin
        scale = lax.rsqrt(jnp.mean(x * x, axis=-1, keepdims=True) + eps)
        n = x * scale
        gain_sum = gain_sum + jnp.sum(t * n, axis=0, keepdims=True)
        e = t * gain
        out_ref[:, cols] = (scale * (e - n * jnp.mean(e * n, axis=-1, keepdims=True))).astype(BF16)

    @pl.when(pl.program_id(0) == 0)
    def _():
        gain_ref[...] = jnp.zeros_like(gain_ref)

    gain_ref[...] += gain_sum


def head_prep_back(grad, raw, cos, sin, gain, raw_block, plain):
    rows, width = grad.shape
    tile = 256
    tab = pl.BlockSpec((tile, HD), lambda i: (i, 0))
    return pl.pallas_call(
        functools.partial(prep_back_kernel, width // HD, plain),
        out_shape=(
            jax.ShapeDtypeStruct((rows, width), BF16),
            jax.ShapeDtypeStruct((1, HD), F32),
        ),
        grid=(rows // tile,),
        in_specs=[
            pl.BlockSpec((tile, width), lambda i: (i, 0)),
            pl.BlockSpec((tile, width), lambda i: (i, raw_block)),
            tab,
            tab,
            pl.BlockSpec((1, HD), lambda i: (0, 0)),
        ],
        out_specs=(
            pl.BlockSpec((tile, width), lambda i: (i, 0)),
            pl.BlockSpec((1, HD), lambda i: (0, 0)),
        ),
        cost_estimate=pl.CostEstimate(
            flops=20 * rows * width, bytes_accessed=10 * rows * width, transcendentals=0
        ),
        name="head_prep_back",
    )(grad, raw, cos, sin, gain)


def block_place(pair, shard, place, ways, count):
    owner = shard
    if ways == 2:
        other = (pair + place % 2) % 2 if isinstance(pair, int) else lax.rem(pair + place % 2, 2)
        owner = (shard // 2) * 4 + 2 * other + shard % 2
    return owner if place < ways else 2 * count - 1 - owner


def load_sequence(pair, ways, kv_ref, keys, values):
    shards, _, _, block, _ = kv_ref.shape
    for shard in range(shards):
        for place in range(2 * ways):
            index = block_place(pair, shard, place, ways, shards * ways)
            rows = pl.ds(pl.multiple_of(index * block, block), block)
            keys[rows, :] = kv_ref[shard, 0, place, :, :HD]
            values[rows, :] = kv_ref[shard, 0, place, :, HD:]


def stack_heads(tile, count):
    return jnp.concatenate([tile[:, h * HD : (h + 1) * HD] for h in range(count)], axis=0)


def row_positions(info_ref, place, block, count):
    base = pl.program_id(0) * (info_ref.shape[0] // pl.num_programs(0)) + 1 + 3 * place
    first = info_ref[base]
    lane = lax.broadcasted_iota(jnp.int32, (1, count * block), 1)
    position = first + lax.rem(lane, block)
    start_first, start_last = info_ref[base + 1], info_ref[base + 2]
    start = jnp.where(position >= start_last, start_last, start_first)
    return position, start, start_first // CHUNK, (first + block - 1) // CHUNK + 1


def valid_tile(chunk, position, start, shape):
    key_index = chunk * CHUNK + lax.broadcasted_iota(jnp.int32, shape, 0)
    return (key_index <= position) & (key_index >= start)


def forward_kernel(ways, count, info_ref, q_ref, kv_ref, o_ref, lse_ref, keys, values):
    load_sequence(info_ref[0], ways, kv_ref, keys, values)
    block = q_ref.shape[2]
    columns = count * block
    for place in range(2 * ways):
        queries = stack_heads(q_ref[0, place], count)
        position, start, low, high = row_positions(info_ref, place, block, count)

        def body(chunk, carry):
            total, norm = carry
            rows = pl.ds(pl.multiple_of(chunk * CHUNK, CHUNK), CHUNK)
            score = dot_cols(keys[rows, :], queries)
            weight = jnp.where(
                valid_tile(chunk, position, start, score.shape), jnp.exp2(score * EXP2_SCALE), 0.0
            )
            norm = norm + jnp.sum(weight, axis=0, keepdims=True)
            total = total + dot_rows(values[rows, :], weight.astype(BF16))
            return total, norm

        total, norm = lax.fori_loop(
            low, high, body, (jnp.zeros((HD, columns), F32), jnp.zeros((1, columns), F32))
        )
        out = (total / norm).T.astype(BF16)
        for h in range(count):
            o_ref[0, place, :, h * HD : (h + 1) * HD] = out[h * block : (h + 1) * block]
        lse_ref[0, 0, place] = jnp.log2(norm)


def backward_kernel(
    ways, count, info_ref, q_ref, do_ref, o_ref, lse_ref, kv_ref,
    dq_ref, dkv_ref, keys, values, grad_k, grad_v,
):
    pair = info_ref[0]
    load_sequence(pair, ways, kv_ref, keys, values)
    block = q_ref.shape[2]
    columns = count * block
    grad_k[...] = jnp.zeros_like(grad_k)
    grad_v[...] = jnp.zeros_like(grad_v)
    for place in range(2 * ways):
        queries = stack_heads(q_ref[0, place], count)
        grads = stack_heads(do_ref[0, place], count)
        outs = stack_heads(o_ref[0, place], count)
        delta = jnp.sum((grads.astype(F32) * outs.astype(F32)).T, axis=0, keepdims=True)
        lse = lse_ref[0, 0, place]
        position, start, low, high = row_positions(info_ref, place, block, count)

        def body(chunk, total):
            rows = pl.ds(pl.multiple_of(chunk * CHUNK, CHUNK), CHUNK)
            key_rows = keys[rows, :]
            score = dot_cols(key_rows, queries)
            prob = jnp.where(
                valid_tile(chunk, position, start, score.shape),
                jnp.exp2(score * EXP2_SCALE - lse),
                0.0,
            )
            grad_prob = dot_cols(values[rows, :], grads)
            grad_score = (prob * (grad_prob - delta)).astype(BF16)
            grad_v[rows, :] += dot(prob.astype(BF16), grads)
            grad_k[rows, :] += dot(grad_score, queries)
            return total + dot_rows(key_rows, grad_score)

        total = lax.fori_loop(low, high, body, jnp.zeros((HD, columns), F32))
        out = total.T * SCALE
        for h in range(count):
            dq_ref[0, place, :, h * HD : (h + 1) * HD] = out[h * block : (h + 1) * block]
    shards = dkv_ref.shape[0]
    for shard in range(shards):
        for place in range(2 * ways):
            index = block_place(pair, shard, place, ways, shards * ways)
            rows = pl.ds(pl.multiple_of(index * block, block), block)
            dkv_ref[shard, 0, place, :, :HD] = (grad_k[rows, :] * SCALE).astype(BF16)
            dkv_ref[shard, 0, place, :, HD:] = grad_v[rows, :].astype(BF16)


def attention_specs(q, kv, count):
    shards, sequences, places, block, width = kv.shape
    row = pl.BlockSpec((1, places, block, count * HD), lambda s, n, i: (s, 0, 0, n))
    part = pl.BlockSpec((shards, 1, places, block, 2 * HD), lambda s, n, i: (0, s, 0, 0, n))
    sums = pl.BlockSpec((1, 1, places, 1, count * block), lambda s, n, i: (s, n, 0, 0, 0))
    sums_shape = (sequences, width // (2 * HD), places, 1, count * block)
    return row, part, sums, sums_shape, shards * places * block


def attend(info, q, kv, count, ways):
    row, part, sums, sums_shape, length = attention_specs(q, kv, count)
    return pl.pallas_call(
        functools.partial(forward_kernel, ways, count),
        out_shape=(
            jax.ShapeDtypeStruct(q.shape, BF16),
            jax.ShapeDtypeStruct(sums_shape, F32),
        ),
        grid_spec=pltpu.PrefetchScalarGridSpec(
            num_scalar_prefetch=1,
            grid=sums_shape[:2],
            in_specs=[row, part],
            out_specs=(row, sums),
            scratch_shapes=[pltpu.VMEM((length, HD), BF16)] * 2,
        ),
        compiler_params=vmem_limit(48),
        cost_estimate=pl.CostEstimate(
            flops=4 * 8 * CHUNK * q.size, bytes_accessed=2 * kv.size, transcendentals=0
        ),
        name="attend",
    )(info, q, kv)


def attend_back(info, q, grad, out, lse, kv, count, ways):
    row, part, sums, sums_shape, length = attention_specs(q, kv, count)
    return pl.pallas_call(
        functools.partial(backward_kernel, ways, count),
        out_shape=(
            jax.ShapeDtypeStruct(q.shape, F32),
            jax.ShapeDtypeStruct(kv.shape, BF16),
        ),
        grid_spec=pltpu.PrefetchScalarGridSpec(
            num_scalar_prefetch=1,
            grid=sums_shape[:2],
            in_specs=[row, row, row, sums, part],
            out_specs=(row, part),
            scratch_shapes=[pltpu.VMEM((length, HD), BF16)] * 2
            + [pltpu.VMEM((length, HD), F32)] * 2,
        ),
        compiler_params=vmem_limit(56),
        cost_estimate=pl.CostEstimate(
            flops=10 * 8 * CHUNK * q.size, bytes_accessed=4 * kv.size, transcendentals=0
        ),
        name="attend_back",
    )(info, q, grad, out, lse, kv)


def interleave_heads(first, second):
    rows, width = first.shape
    heads = width // HD
    both = jnp.stack([first.reshape(rows, heads, HD), second.reshape(rows, heads, HD)], axis=2)
    return both.reshape(rows, 2 * width)


def after(value, earlier):
    return lax.optimization_barrier((value, earlier))[0]


def local(
    tokens,
    grad_out,
    segments,
    w_query,
    key_weight_matrix,
    value_weight_matrix,
    w_output,
    w_gate,
    w_up,
    w_down,
    norm_attn,
    norm_mlp,
    norm_query,
    norm_key,
):
    ctx_count = lax.axis_size("ctx")
    seq_count = lax.axis_size("fsdp")
    me = lax.axis_index("ctx").astype(jnp.int32)
    my_seq = lax.axis_index("fsdp").astype(jnp.int32)
    pair = lax.rem(me // 2, 2)
    block = tokens.shape[3]
    width = tokens.shape[4]
    own = 2 * block
    ways = 2 if (key_weight_matrix.shape[1] // HD) % 2 == 0 else 1
    query_heads = w_query.shape[1] // HD // ways
    groups = key_weight_matrix.shape[1] // HD // ways
    count = query_heads // groups
    q_width, kv_width = query_heads * HD, 2 * groups * HD
    hidden = w_gate.shape[1] // 2

    w_kv = interleave_heads(key_weight_matrix, value_weight_matrix)
    gain_attn_row = swap_blocks(norm_attn[None], ctx_count, 1)
    gain_mlp_row = swap_blocks(norm_mlp[None], ctx_count, 1)

    if ways == 2:
        qkv_shard = swap_shards(*pair_columns([w_query, w_kv], pair, 2), pair)
        output_shard = swap_shards(*pair_columns([w_output], pair, 2), pair)
    else:
        qkv_shard, output_shard = jnp.concatenate([w_query, w_kv], axis=1), w_output
    full_qkv = gather_weight(qkv_shard, ways)
    full_output = gather_weight(output_shard, ways)

    row_bf16 = jax.ShapeDtypeStruct((own, width), BF16)
    row_f32 = jax.ShapeDtypeStruct((own, width), F32)
    gain_shape = jax.ShapeDtypeStruct((1, width), F32)
    h1_own, inputs, cot_own = row_pass(
        functools.partial(entry_kernel, ctx_count),
        (tokens.reshape(own, width), grad_out.reshape(own, width), gain_attn_row),
        (row_bf16, row_bf16, row_bf16),
        "entry",
    )
    h1 = gather_rows(h1_own, ways)

    offsets = jnp.arange(block, dtype=jnp.int32)
    owners = [me, me + 2 - 4 * pair][:ways]
    firsts = [o * block for o in owners + [2 * ctx_count - 1 - o for o in owners]]
    freq = jnp.exp(jnp.arange(HD // 2, dtype=F32) * (-2.0 * math.log(rope_base) / HD))
    infos, positions = [], []
    for r in range(seq_count):
        line = lax.dynamic_index_in_dim(
            segments, lax.bitwise_xor(my_seq, jnp.int32(r)), 0, keepdims=False
        )
        doc_first = [jnp.sum((line < d).astype(jnp.int32)) for d in range(DOCS)]
        scalars = [pair]
        for first in firsts:
            mine = lax.dynamic_slice_in_dim(line, first, block)
            start = sum(jnp.where(mine == d, doc_first[d], 0) for d in range(DOCS))
            scalars += [first, start[0], start[block - 1]]
            positions.append(first + offsets - start)
        infos += scalars
    info = jnp.stack(infos)
    angle = jnp.concatenate(positions).astype(F32)[:, None] * freq
    cos, sin = jnp.cos(angle), jnp.sin(angle)
    cos, sin = jnp.concatenate([cos, cos], 1), jnp.concatenate([-sin, sin], 1)
    gain_q, gain_k = norm_query.reshape(1, HD), norm_key.reshape(1, HD)

    raw = dot(h1, full_qkv)
    q, kv = head_prep(raw, cos, sin, gain_q, gain_k, query_heads, groups)
    q = q.reshape(seq_count, 2 * ways, block, q_width)

    mine, theirs = pair_columns([w_gate, w_up, w_down], pair, 2)
    shards = swap_shards(mine, after(theirs, h1), pair)
    full_kv = ctx_gather(after(kv, full_output), ways).reshape(-1, seq_count, 2 * ways, block, kv_width)
    shards = after(shards, kv)
    full_gate, full_up, full_down = (
        gather_weight(shards[:, i * hidden : (i + 1) * hidden], 2) for i in range(3)
    )
    cot_all = gather_rows(after(cot_own, shards), 2)

    q = after(q, cot_all)
    heads, lse = attend(info, q, full_kv, count, ways)
    mixed = heads.reshape(-1, q_width)
    lows, highs = return_rows(dot_cols(mixed, full_output).astype(BF16), ways)
    x2, h2_own = row_pass(
        functools.partial(middle_kernel, len(lows), len(highs)),
        (inputs, gain_mlp_row, *lows, *highs),
        (row_f32, row_bf16),
        "middle",
    )
    h2 = gather_rows(h2_own, 2)

    gate = dot(h2, full_gate)
    up = dot(h2, full_up)
    act = lax.optimization_barrier((gate / (1.0 + jnp.exp(-gate)) * up).astype(BF16))
    grad_down = dot_rows(cot_all, act).astype(BF16)
    d_act = dot(after(cot_all, grad_down), full_down)
    sg = 1.0 / (1.0 + jnp.exp(-gate))
    d_gate = (d_act * up * sg * (1.0 + gate * (1.0 - sg))).astype(BF16)
    d_up = (d_act * gate * sg).astype(BF16)
    d_h2_part = (dot_cols(d_gate, full_gate) + dot_cols(d_up, full_up)).astype(BF16)
    h2_late = after(h2, d_h2_part)
    grad_gate = dot_rows(h2_late, d_gate).astype(BF16)
    grad_up = dot_rows(h2_late, d_up).astype(BF16)
    lows, highs = return_rows(d_h2_part, 2, (grad_gate, grad_up))
    returned = (lows[0], highs[0])
    d_x2, d_x2_low, gain_mlp = row_pass(
        functools.partial(back_kernel, len(lows), len(highs), None),
        (cot_own, x2, gain_mlp_row, *lows, *highs),
        (row_f32, row_bf16, gain_shape),
        "middle_back",
    )
    y_part = dot_cols(after(act, d_x2_low), full_down).astype(BF16)
    branch = after(gather_rows(d_x2_low, ways), y_part)
    rows_down = scatter_weight(grad_down, 2)
    rows_gate = scatter_weight(after(grad_gate, (rows_down, returned)), 2)
    def one(both, split):
        return own_rows(both, pair, split, [(0, both.shape[1], 0, 0)], [both.shape[1]])[0]

    d_att = dot(branch, full_output).astype(BF16).reshape(q.shape)
    rows_up = scatter_weight(after(grad_up, (rows_gate, d_att)), 2)
    grad_output = dot_rows(branch, mixed).astype(BF16)
    shard_down = one(rows_down, 2)
    shard_gate = one(rows_gate, 2)
    d_q, d_kv = attend_back(info, q, d_att, heads, lse, full_kv, count, ways)
    y_lows, y_highs = return_rows(after(y_part, branch), 2, d_q)
    out_tokens = row_pass(
        functools.partial(result_kernel, len(y_lows), len(y_highs), ctx_count),
        (x2, *y_lows, *y_highs),
        row_bf16,
        "result",
    ).reshape(tokens.shape)
    d_qp, gain_q_sum = head_prep_back(
        d_q.reshape(-1, q_width), raw, cos, sin, gain_q, 0, False
    )
    d_h1_query = dot_cols(d_qp, full_qkv[:, :q_width])
    d_kv = after(
        d_kv.reshape(-1, kv_width),
        (rows_up, out_tokens),
    )
    d_kv = ctx_scatter(d_kv, ways)
    h1_late = after(h1, (d_h1_query, shard_down, shard_gate))
    grad_query = dot_rows(h1_late, d_qp).astype(BF16)
    grad_both = jnp.concatenate([grad_output, grad_query], axis=1)
    rows_both = scatter_weight(after(grad_both, d_kv), ways)
    d_kv = after(d_kv, grad_both)
    d_kvp, gain_k_sum = head_prep_back(d_kv, raw, cos, sin, gain_k, q_width // kv_width, True)
    grad_kv = dot_rows(h1, d_kvp).astype(BF16)
    d_h1 = (
        d_h1_query + dot_cols(after(d_kvp, grad_kv), full_qkv[:, q_width:])
    ).astype(BF16)
    gain_attn = jnp.sum(d_h1.astype(F32) * h1.astype(F32), axis=0) / gain_attn_row[0]
    gains = butterfly_sum(
        jnp.concatenate([gain_attn, gain_mlp[0], gain_q_sum[0], gain_k_sum[0]])
    )
    lows, highs = return_rows(d_h1, ways)
    rows_kv = scatter_weight(after(grad_kv, (rows_both, lows[0], highs[0])), ways)
    lows[0] = after(lows[0], gains)
    grad_tokens = row_pass(
        functools.partial(back_kernel, len(lows), len(highs), ctx_count),
        (d_x2, inputs, gain_attn_row, *lows, *highs),
        row_f32,
        "entry_back",
    )
    rows_up, rows_both, rows_kv = after((rows_up, rows_both, rows_kv), (lows, highs))
    shard_up = one(rows_up, 2)
    plan = [(0, q_width, 0, 0), (q_width, q_width, 1, 0)]
    shard_output, shard_query = own_rows(rows_both, pair, ways, plan, [q_width, q_width])
    plan = []
    for h in range(groups):
        for t in (0, 1):
            plan.append(((2 * h + t) * HD, HD, t, h * HD))
    shard_key, shard_value = own_rows(rows_kv, pair, ways, plan, [groups * HD, groups * HD])
    grad_tokens = grad_tokens.reshape(tokens.shape)
    return (
        out_tokens,
        grad_tokens,
        shard_query,
        shard_key,
        shard_value,
        shard_output,
        shard_gate,
        shard_up,
        shard_down,
        swap_blocks(gains[None, :width], ctx_count, 1)[0],
        swap_blocks(gains[None, width : 2 * width], ctx_count, 1)[0],
        gains[2 * width : 2 * width + HD],
        gains[2 * width + HD :],
    )


def solution(mesh):
    block = P("fsdp", "ctx", None, None, None)
    weight = P("ctx", "fsdp")
    return jax.shard_map(
        local,
        mesh=mesh,
        in_specs=(block, block, P()) + (weight,) * 7 + (P(),) * 4,
        out_specs=(block, block) + (weight,) * 7 + (P(),) * 4,
        check_vma=False,
    )
```

```python
import functools
import math

import jax
import jax.numpy as jnp
from jax import lax
from jax.experimental import pallas as pl
from jax.experimental.pallas import tpu as pltpu
from jax.sharding import PartitionSpec as P

QUERY_HEADS = 16
KEY_VALUE_HEADS = 8
HD = 128
DOCS = 4
CHUNK = 256
eps = 1e-06
rope_base = 1000000.0
SCALE = HD ** (-0.5)
EXP2_SCALE = SCALE * math.log2(math.e)
F32 = jnp.float32
BF16 = jnp.bfloat16


def xor_send(value, axis, step):
    count = lax.axis_size(axis)
    return lax.ppermute(value, axis, [(i, i ^ step) for i in range(count)])


def exchange_rows(rows, axis):
    return [rows] + [xor_send(rows, axis, r) for r in range(1, lax.axis_size(axis))]


def scatter_rows(partial, axis):
    count = lax.axis_size(axis)
    rows = partial.shape[0] // count
    total = partial[:rows].astype(F32)
    for r in range(1, count):
        total = total + xor_send(partial[r * rows : (r + 1) * rows], axis, r).astype(F32)
    return total


def pair_groups(count):
    return [[i for i in range(count) if (i >> 1) & 1 == bit] for bit in (0, 1)]


def swap_blocks(x, count, axis):
    shape = x.shape
    split = x.reshape(shape[:axis] + (count // 4, 2, 2, shape[axis] // count) + shape[axis + 1 :])
    return split.swapaxes(axis + 1, axis + 2).reshape(shape)


def assemble_kernel(plan, *refs):
    out_ref = refs[-1]
    place = 0
    for index, start, number in plan:
        out_ref[place : place + number, :] = refs[index][start : start + number, :]
        place += number


def assemble(arrays, plan):
    width = arrays[0].shape[1]
    rows = sum(number for _, _, number in plan)
    return pl.pallas_call(
        functools.partial(assemble_kernel, plan),
        out_shape=jax.ShapeDtypeStruct((rows, width), arrays[0].dtype),
        compiler_params=vmem_limit(32),
        cost_estimate=pl.CostEstimate(
            flops=0, bytes_accessed=4 * rows * width, transcendentals=0
        ),
        name="assemble",
    )(*arrays)


def gather_rows(rows, ways):
    count = lax.axis_size("fsdp")
    total = rows.shape[0]
    if ways == 1:
        return assemble(exchange_rows(rows, "fsdp"), [(r, 0, total) for r in range(count)])
    block = total // 2
    low = rows[:block]
    lows = exchange_rows(low, "fsdp")
    high = jnp.concatenate([rows[block:], xor_send(rows[block:], "ctx", 2)], axis=0)
    highs = exchange_rows(high, "fsdp")
    others = xor_send(jnp.concatenate(lows, axis=0), "ctx", 2)
    plan = []
    for r in range(count):
        plan += [(1 + r, 0, block), (0, r * block, block), (1 + count + r, 0, 2 * block)]
    return assemble([others] + lows + highs, plan)


def return_rows(partial, ways, filler=None):
    count = lax.axis_size("fsdp")
    if ways == 1:
        rows = partial.shape[0] // count
        terms = [partial[:rows]] + [
            xor_send(partial[r * rows : (r + 1) * rows], "fsdp", r) for r in range(1, count)
        ]
        return [t[: rows // 2] for t in terms], [t[rows // 2 :] for t in terms]
    block = partial.shape[0] // (4 * count)

    def rows(start, number):
        return partial[start * block : (start + number) * block]

    sent = jnp.concatenate([rows(4 * r + 1, 1) for r in range(count)], axis=0)
    pairs = [xor_send(rows(4 * r + 2, 2), "fsdp", r) for r in range(1, count)]
    other = xor_send(sent, "ctx", 2)
    if filler is not None:
        other, pairs = after((other, pairs), filler)
    first = [
        (rows(4 * r, 1).astype(F32) + other[r * block : (r + 1) * block].astype(F32)).astype(BF16)
        for r in range(count)
    ]
    second = rows(2, 2).astype(F32)
    for term in pairs:
        second = second + term.astype(F32)
    second = second.astype(BF16)
    lows = [first[0]] + [xor_send(first[r], "fsdp", r) for r in range(1, count)]
    return lows, [second[:block], xor_send(second[block:], "ctx", 2)]


def natural_columns(x, count):
    width = x.shape[1] // count
    order = [(i & ~3) | ((i & 1) << 1) | ((i >> 1) & 1) for i in range(count)]
    return jnp.concatenate([x[:, i * width : (i + 1) * width] for i in order], axis=1)


ROWS = 16


def over_rows(number, body, carry=None):
    def step(i, carry):
        return body(pl.multiple_of(i * ROWS, ROWS), carry)

    return lax.fori_loop(0, number // ROWS, step, carry)


def row_scale(x):
    return lax.rsqrt(jnp.mean(x * x, axis=-1, keepdims=True) + eps)


def entry_kernel(count, tok_ref, cot_ref, gain_ref, h_ref, x_ref, c_ref):
    def body(at, carry):
        rows = pl.ds(at, ROWS)
        x = natural_columns(tok_ref[rows, :], count)
        x_ref[rows, :] = x
        wide = x.astype(F32)
        h_ref[rows, :] = (wide * row_scale(wide) * gain_ref[...]).astype(BF16)
        c_ref[rows, :] = natural_columns(cot_ref[rows, :], count)
        return carry

    over_rows(tok_ref.shape[0], body, 0)


def sum_terms(refs, rows):
    total = refs[0][rows, :].astype(F32)
    for ref in refs[1:]:
        total = total + ref[rows, :].astype(F32)
    return total


def middle_kernel(lows, highs, *refs):
    x_ref, gain_ref, x2_ref, h_ref = refs[0], refs[1], refs[-2], refs[-1]
    block = x_ref.shape[0] // 2
    for half, terms in ((0, refs[2 : 2 + lows]), (1, refs[2 + lows : 2 + lows + highs])):

        def body(at, carry):
            rows = pl.ds(half * block + at, ROWS)
            x2 = x_ref[rows, :].astype(F32) + sum_terms(terms, pl.ds(at, ROWS))
            x2_ref[rows, :] = x2
            h_ref[rows, :] = (x2 * row_scale(x2) * gain_ref[...]).astype(BF16)
            return carry

        over_rows(block, body, 0)


def result_kernel(lows, highs, count, *refs):
    x_ref, out_ref = refs[0], refs[-1]
    block = x_ref.shape[0] // 2
    for half, terms in ((0, refs[1 : 1 + lows]), (1, refs[1 + lows : 1 + lows + highs])):

        def body(at, carry):
            rows = pl.ds(half * block + at, ROWS)
            total = x_ref[rows, :] + sum_terms(terms, pl.ds(at, ROWS))
            out_ref[rows, :] = natural_columns(total, count).astype(BF16)
            return carry

        over_rows(block, body, 0)


def back_kernel(lows, highs, count, *refs):
    base_ref, x_ref, gain_ref = refs[:3]
    wide_ref, gain_out = refs[3 + lows + highs], refs[-1]
    low_ref = refs[4 + lows + highs] if count is None else None
    block = x_ref.shape[0] // 2
    total = jnp.zeros((ROWS, x_ref.shape[1]), F32) if count is None else 0
    for half, terms in ((0, refs[3 : 3 + lows]), (1, refs[3 + lows : 3 + lows + highs])):

        def body(at, carry):
            rows = pl.ds(half * block + at, ROWS)
            grad = sum_terms(terms, pl.ds(at, ROWS))
            x = x_ref[rows, :].astype(F32)
            scale = row_scale(x)
            unit = x * scale
            scaled = grad * gain_ref[...]
            out = base_ref[rows, :].astype(F32) + scale * (
                scaled - unit * jnp.mean(scaled * unit, axis=-1, keepdims=True)
            )
            if count is None:
                wide_ref[rows, :] = out
                low_ref[rows, :] = out.astype(BF16)
            else:
                wide_ref[rows, :] = natural_columns(out, count)
            return carry + grad * unit if count is None else carry

        total = over_rows(block, body, total)
    if count is None:
        gain_out[...] = jnp.sum(total, axis=0, keepdims=True)


def row_pass(kernel, args, outs, name):
    return pl.pallas_call(
        kernel,
        out_shape=outs,
        compiler_params=vmem_limit(40),
        cost_estimate=pl.CostEstimate(
            flops=10 * args[0].size, bytes_accessed=10 * args[0].size, transcendentals=0
        ),
        name=name,
    )(*args)


def pair_columns(weights, pair, ways):
    shares = []
    for place in (pair, 1 - pair):
        parts = []
        for weight in weights:
            columns = weight.shape[1] // ways
            parts.append(lax.dynamic_slice_in_dim(weight, place * columns, columns, 1))
        shares.append(jnp.concatenate(parts, axis=1))
    return shares


def swap_shards(mine, theirs, pair):
    theirs = xor_send(theirs, "ctx", 2)
    return jnp.concatenate(
        [jnp.where(pair == 0, mine, theirs), jnp.where(pair == 0, theirs, mine)], axis=0
    )


def ctx_gather(rows, ways):
    groups = pair_groups(lax.axis_size("ctx")) if ways == 2 else None
    return lax.all_gather(rows, "ctx", axis=0, tiled=True, axis_index_groups=groups)


def ctx_scatter(rows, ways):
    groups = pair_groups(lax.axis_size("ctx")) if ways == 2 else None
    return lax.psum_scatter(
        rows, "ctx", scatter_dimension=0, tiled=True, axis_index_groups=groups
    )


def gather_weight(shard, ways):
    full = ctx_gather(shard, ways)
    return swap_blocks(full, lax.axis_size("ctx"), 0) if ways == 1 else full


def scatter_weight(grad, ways):
    if ways == 1:
        grad = swap_blocks(grad, lax.axis_size("ctx"), 0)
    return ctx_scatter(grad, ways)


def own_kernel(plan, pair_ref, both_ref, other_ref, *outs):
    pair = pair_ref[0]
    rows, width = other_ref.shape
    mine = pl.ds(pl.multiple_of(pair * rows, rows), rows)
    for source, columns, target, place in plan:
        half = outs[target].shape[1] // 2
        for ref, at, which in ((both_ref, mine, pair), (other_ref, slice(None), 1 - pair)):
            start = pl.multiple_of(which * half + place, HD)
            outs[target][:, pl.ds(start, columns)] = ref[at, source : source + columns].astype(F32)


def own_rows(both, pair, ways, plan, widths):
    if ways == 1:
        return [
            jnp.concatenate([both[:, s : s + n] for s, n, t, _ in plan if t == i], axis=1).astype(F32)
            for i in range(len(widths))
        ]
    rows = both.shape[0] // 2
    other = xor_send(lax.dynamic_slice_in_dim(both, (1 - pair) * rows, rows, 0), "ctx", 2)
    shapes = tuple(jax.ShapeDtypeStruct((rows, 2 * width), F32) for width in widths)
    whole = [pl.BlockSpec(t.shape, lambda i, m: (0, 0)) for t in (both, other) + shapes]
    return pl.pallas_call(
        functools.partial(own_kernel, plan),
        out_shape=shapes,
        grid_spec=pltpu.PrefetchScalarGridSpec(
            num_scalar_prefetch=1,
            grid=(1,),
            in_specs=whole[:2],
            out_specs=tuple(whole[2:]),
        ),
        cost_estimate=pl.CostEstimate(flops=0, bytes_accessed=8 * both.size, transcendentals=0),
        name="own_rows",
    )(pair.reshape(1), both, other)


def butterfly_sum(value):
    for axis in ("ctx", "fsdp"):
        step = 1
        while step < lax.axis_size(axis):
            value = value + xor_send(value, axis, step)
            step *= 2
    return value


def dot(left, right):
    return jnp.dot(left, right, preferred_element_type=F32)


def dot_rows(left, right):
    return lax.dot_general(left, right, (((0,), (0,)), ((), ())), preferred_element_type=F32)


def dot_cols(left, right):
    return lax.dot_general(left, right, (((1,), (1,)), ((), ())), preferred_element_type=F32)


def vmem_limit(mib):
    return pltpu.CompilerParams(vmem_limit_bytes=mib * 1024 * 1024)


def prep_kernel(query_heads, groups, raw_ref, cos_ref, sin_ref, gq_ref, gk_ref, q_ref, kv_ref):
    cos = cos_ref[...]
    sin = sin_ref[...]

    def rotate_norm(x, gain):
        scale = lax.rsqrt(jnp.mean(x * x, axis=-1, keepdims=True) + eps)
        u = x * scale * gain
        return u * cos + pltpu.roll(u, HD // 2, 1) * sin

    for h in range(query_heads):
        cols = slice(h * HD, (h + 1) * HD)
        q_ref[:, cols] = rotate_norm(raw_ref[:, cols], gq_ref[...]).astype(BF16)
    for h in range(2 * groups):
        x = raw_ref[:, (query_heads + h) * HD : (query_heads + h + 1) * HD]
        if h % 2 == 0:
            x = rotate_norm(x, gk_ref[...])
        kv_ref[:, h * HD : (h + 1) * HD] = x.astype(BF16)


def head_prep(raw, cos, sin, gq, gk, query_heads, groups):
    rows, width = raw.shape
    tile = 256
    vec = pl.BlockSpec((1, HD), lambda i: (0, 0))
    tab = pl.BlockSpec((tile, HD), lambda i: (i, 0))
    return pl.pallas_call(
        functools.partial(prep_kernel, query_heads, groups),
        out_shape=(
            jax.ShapeDtypeStruct((rows, query_heads * HD), BF16),
            jax.ShapeDtypeStruct((rows, 2 * groups * HD), BF16),
        ),
        grid=(rows // tile,),
        in_specs=[pl.BlockSpec((tile, width), lambda i: (i, 0)), tab, tab, vec, vec],
        out_specs=(
            pl.BlockSpec((tile, query_heads * HD), lambda i: (i, 0)),
            pl.BlockSpec((tile, 2 * groups * HD), lambda i: (i, 0)),
        ),
        cost_estimate=pl.CostEstimate(
            flops=20 * raw.size, bytes_accessed=6 * raw.size, transcendentals=0
        ),
        name="head_prep",
    )(raw, cos, sin, gq, gk)


def prep_back_kernel(heads, plain, d_ref, raw_ref, cos_ref, sin_ref, g_ref, out_ref, gain_ref):
    cos = cos_ref[...]
    sin = sin_ref[...]
    gain = g_ref[...]
    gain_sum = jnp.zeros((1, HD), F32)
    for h in range(heads):
        cols = slice(h * HD, (h + 1) * HD)
        d = d_ref[:, cols].astype(F32)
        if plain and h % 2 == 1:
            out_ref[:, cols] = d.astype(BF16)
            continue
        x = raw_ref[:, cols]
        t = d * cos - pltpu.roll(d, HD // 2, 1) * sin
        scale = lax.rsqrt(jnp.mean(x * x, axis=-1, keepdims=True) + eps)
        n = x * scale
        gain_sum = gain_sum + jnp.sum(t * n, axis=0, keepdims=True)
        e = t * gain
        out_ref[:, cols] = (scale * (e - n * jnp.mean(e * n, axis=-1, keepdims=True))).astype(BF16)

    @pl.when(pl.program_id(0) == 0)
    def _():
        gain_ref[...] = jnp.zeros_like(gain_ref)

    gain_ref[...] += gain_sum


def head_prep_back(grad, raw, cos, sin, gain, raw_block, plain):
    rows, width = grad.shape
    tile = 256
    tab = pl.BlockSpec((tile, HD), lambda i: (i, 0))
    return pl.pallas_call(
        functools.partial(prep_back_kernel, width // HD, plain),
        out_shape=(
            jax.ShapeDtypeStruct((rows, width), BF16),
            jax.ShapeDtypeStruct((1, HD), F32),
        ),
        grid=(rows // tile,),
        in_specs=[
            pl.BlockSpec((tile, width), lambda i: (i, 0)),
            pl.BlockSpec((tile, width), lambda i: (i, raw_block)),
            tab,
            tab,
            pl.BlockSpec((1, HD), lambda i: (0, 0)),
        ],
        out_specs=(
            pl.BlockSpec((tile, width), lambda i: (i, 0)),
            pl.BlockSpec((1, HD), lambda i: (0, 0)),
        ),
        cost_estimate=pl.CostEstimate(
            flops=20 * rows * width, bytes_accessed=10 * rows * width, transcendentals=0
        ),
        name="head_prep_back",
    )(grad, raw, cos, sin, gain)


def block_place(pair, shard, place, ways, count):
    owner = shard
    if ways == 2:
        other = (pair + place % 2) % 2 if isinstance(pair, int) else lax.rem(pair + place % 2, 2)
        owner = (shard // 2) * 4 + 2 * other + shard % 2
    return owner if place < ways else 2 * count - 1 - owner


def load_sequence(pair, ways, kv_ref, keys, values):
    shards, _, _, block, _ = kv_ref.shape
    for shard in range(shards):
        for place in range(2 * ways):
            index = block_place(pair, shard, place, ways, shards * ways)
            rows = pl.ds(pl.multiple_of(index * block, block), block)
            keys[rows, :] = kv_ref[shard, 0, place, :, :HD]
            values[rows, :] = kv_ref[shard, 0, place, :, HD:]


def stack_heads(tile, count):
    return jnp.concatenate([tile[:, h * HD : (h + 1) * HD] for h in range(count)], axis=0)


def row_positions(info_ref, place, block, count):
    base = pl.program_id(0) * (info_ref.shape[0] // pl.num_programs(0)) + 1 + 3 * place
    first = info_ref[base]
    lane = lax.broadcasted_iota(jnp.int32, (1, count * block), 1)
    position = first + lax.rem(lane, block)
    start_first, start_last = info_ref[base + 1], info_ref[base + 2]
    start = jnp.where(position >= start_last, start_last, start_first)
    return position, start, start_first // CHUNK, (first + block - 1) // CHUNK + 1


def valid_tile(chunk, position, start, shape):
    key_index = chunk * CHUNK + lax.broadcasted_iota(jnp.int32, shape, 0)
    return (key_index <= position) & (key_index >= start)


def forward_kernel(ways, count, info_ref, q_ref, kv_ref, o_ref, lse_ref, keys, values):
    load_sequence(info_ref[0], ways, kv_ref, keys, values)
    block = q_ref.shape[2]
    columns = count * block
    for place in range(2 * ways):
        queries = stack_heads(q_ref[0, place], count)
        position, start, low, high = row_positions(info_ref, place, block, count)

        def body(chunk, carry):
            total, norm = carry
            rows = pl.ds(pl.multiple_of(chunk * CHUNK, CHUNK), CHUNK)
            score = dot_cols(keys[rows, :], queries)
            weight = jnp.where(
                valid_tile(chunk, position, start, score.shape), jnp.exp2(score * EXP2_SCALE), 0.0
            )
            norm = norm + jnp.sum(weight, axis=0, keepdims=True)
            total = total + dot_rows(values[rows, :], weight.astype(BF16))
            return total, norm

        total, norm = lax.fori_loop(
            low, high, body, (jnp.zeros((HD, columns), F32), jnp.zeros((1, columns), F32))
        )
        out = (total / norm).T.astype(BF16)
        for h in range(count):
            o_ref[0, place, :, h * HD : (h + 1) * HD] = out[h * block : (h + 1) * block]
        lse_ref[0, 0, place] = jnp.log2(norm)


def backward_kernel(
    ways, count, info_ref, q_ref, do_ref, o_ref, lse_ref, kv_ref,
    dq_ref, dkv_ref, keys, values, grad_k, grad_v,
):
    pair = info_ref[0]
    load_sequence(pair, ways, kv_ref, keys, values)
    block = q_ref.shape[2]
    columns = count * block
    grad_k[...] = jnp.zeros_like(grad_k)
    grad_v[...] = jnp.zeros_like(grad_v)
    for place in range(2 * ways):
        queries = stack_heads(q_ref[0, place], count)
        grads = stack_heads(do_ref[0, place], count)
        outs = stack_heads(o_ref[0, place], count)
        delta = jnp.sum((grads.astype(F32) * outs.astype(F32)).T, axis=0, keepdims=True)
        lse = lse_ref[0, 0, place]
        position, start, low, high = row_positions(info_ref, place, block, count)

        def body(chunk, total):
            rows = pl.ds(pl.multiple_of(chunk * CHUNK, CHUNK), CHUNK)
            key_rows = keys[rows, :]
            score = dot_cols(key_rows, queries)
            prob = jnp.where(
                valid_tile(chunk, position, start, score.shape),
                jnp.exp2(score * EXP2_SCALE - lse),
                0.0,
            )
            grad_prob = dot_cols(values[rows, :], grads)
            grad_score = (prob * (grad_prob - delta)).astype(BF16)
            grad_v[rows, :] += dot(prob.astype(BF16), grads)
            grad_k[rows, :] += dot(grad_score, queries)
            return total + dot_rows(key_rows, grad_score)

        total = lax.fori_loop(low, high, body, jnp.zeros((HD, columns), F32))
        out = total.T * SCALE
        for h in range(count):
            dq_ref[0, place, :, h * HD : (h + 1) * HD] = out[h * block : (h + 1) * block]
    shards = dkv_ref.shape[0]
    for shard in range(shards):
        for place in range(2 * ways):
            index = block_place(pair, shard, place, ways, shards * ways)
            rows = pl.ds(pl.multiple_of(index * block, block), block)
            dkv_ref[shard, 0, place, :, :HD] = (grad_k[rows, :] * SCALE).astype(BF16)
            dkv_ref[shard, 0, place, :, HD:] = grad_v[rows, :].astype(BF16)


def attention_specs(q, kv, count):
    shards, sequences, places, block, width = kv.shape
    row = pl.BlockSpec((1, places, block, count * HD), lambda s, n, i: (s, 0, 0, n))
    part = pl.BlockSpec((shards, 1, places, block, 2 * HD), lambda s, n, i: (0, s, 0, 0, n))
    sums = pl.BlockSpec((1, 1, places, 1, count * block), lambda s, n, i: (s, n, 0, 0, 0))
    sums_shape = (sequences, width // (2 * HD), places, 1, count * block)
    return row, part, sums, sums_shape, shards * places * block


def attend(info, q, kv, count, ways):
    row, part, sums, sums_shape, length = attention_specs(q, kv, count)
    return pl.pallas_call(
        functools.partial(forward_kernel, ways, count),
        out_shape=(
            jax.ShapeDtypeStruct(q.shape, BF16),
            jax.ShapeDtypeStruct(sums_shape, F32),
        ),
        grid_spec=pltpu.PrefetchScalarGridSpec(
            num_scalar_prefetch=1,
            grid=sums_shape[:2],
            in_specs=[row, part],
            out_specs=(row, sums),
            scratch_shapes=[pltpu.VMEM((length, HD), BF16)] * 2,
        ),
        compiler_params=vmem_limit(48),
        cost_estimate=pl.CostEstimate(
            flops=4 * 8 * CHUNK * q.size, bytes_accessed=2 * kv.size, transcendentals=0
        ),
        name="attend",
    )(info, q, kv)


def attend_back(info, q, grad, out, lse, kv, count, ways):
    row, part, sums, sums_shape, length = attention_specs(q, kv, count)
    return pl.pallas_call(
        functools.partial(backward_kernel, ways, count),
        out_shape=(
            jax.ShapeDtypeStruct(q.shape, F32),
            jax.ShapeDtypeStruct(kv.shape, BF16),
        ),
        grid_spec=pltpu.PrefetchScalarGridSpec(
            num_scalar_prefetch=1,
            grid=sums_shape[:2],
            in_specs=[row, row, row, sums, part],
            out_specs=(row, part),
            scratch_shapes=[pltpu.VMEM((length, HD), BF16)] * 2
            + [pltpu.VMEM((length, HD), F32)] * 2,
        ),
        compiler_params=vmem_limit(56),
        cost_estimate=pl.CostEstimate(
            flops=10 * 8 * CHUNK * q.size, bytes_accessed=4 * kv.size, transcendentals=0
        ),
        name="attend_back",
    )(info, q, grad, out, lse, kv)


def interleave_heads(first, second):
    rows, width = first.shape
    heads = width // HD
    both = jnp.stack([first.reshape(rows, heads, HD), second.reshape(rows, heads, HD)], axis=2)
    return both.reshape(rows, 2 * width)


def after(value, earlier):
    return lax.optimization_barrier((value, earlier))[0]


def local(
    tokens,
    grad_out,
    segments,
    w_query,
    key_weight_matrix,
    value_weight_matrix,
    w_output,
    w_gate,
    w_up,
    w_down,
    norm_attn,
    norm_mlp,
    norm_query,
    norm_key,
):
    ctx_count = lax.axis_size("ctx")
    seq_count = lax.axis_size("fsdp")
    me = lax.axis_index("ctx").astype(jnp.int32)
    my_seq = lax.axis_index("fsdp").astype(jnp.int32)
    pair = lax.rem(me // 2, 2)
    block = tokens.shape[3]
    width = tokens.shape[4]
    own = 2 * block
    ways = 2 if (key_weight_matrix.shape[1] // HD) % 2 == 0 else 1
    query_heads = w_query.shape[1] // HD // ways
    groups = key_weight_matrix.shape[1] // HD // ways
    count = query_heads // groups
    q_width, kv_width = query_heads * HD, 2 * groups * HD
    hidden = w_gate.shape[1] // 2

    w_kv = interleave_heads(key_weight_matrix, value_weight_matrix)
    gain_attn_row = swap_blocks(norm_attn[None], ctx_count, 1)
    gain_mlp_row = swap_blocks(norm_mlp[None], ctx_count, 1)

    if ways == 2:
        qkv_shard = swap_shards(*pair_columns([w_query, w_kv], pair, 2), pair)
        output_shard = swap_shards(*pair_columns([w_output], pair, 2), pair)
    else:
        qkv_shard, output_shard = jnp.concatenate([w_query, w_kv], axis=1), w_output
    full_qkv = gather_weight(qkv_shard, ways)
    full_output = gather_weight(output_shard, ways)

    row_bf16 = jax.ShapeDtypeStruct((own, width), BF16)
    row_f32 = jax.ShapeDtypeStruct((own, width), F32)
    gain_shape = jax.ShapeDtypeStruct((1, width), F32)
    h1_own, inputs, cot_own = row_pass(
        functools.partial(entry_kernel, ctx_count),
        (tokens.reshape(own, width), grad_out.reshape(own, width), gain_attn_row),
        (row_bf16, row_bf16, row_bf16),
        "entry",
    )
    h1 = gather_rows(h1_own, ways)

    offsets = jnp.arange(block, dtype=jnp.int32)
    owners = [me, me + 2 - 4 * pair][:ways]
    firsts = [o * block for o in owners + [2 * ctx_count - 1 - o for o in owners]]
    freq = jnp.exp(jnp.arange(HD // 2, dtype=F32) * (-2.0 * math.log(rope_base) / HD))
    infos, positions = [], []
    for r in range(seq_count):
        line = lax.dynamic_index_in_dim(
            segments, lax.bitwise_xor(my_seq, jnp.int32(r)), 0, keepdims=False
        )
        doc_first = [jnp.sum((line < d).astype(jnp.int32)) for d in range(DOCS)]
        scalars = [pair]
        for first in firsts:
            mine = lax.dynamic_slice_in_dim(line, first, block)
            start = sum(jnp.where(mine == d, doc_first[d], 0) for d in range(DOCS))
            scalars += [first, start[0], start[block - 1]]
            positions.append(first + offsets - start)
        infos += scalars
    info = jnp.stack(infos)
    angle = jnp.concatenate(positions).astype(F32)[:, None] * freq
    cos, sin = jnp.cos(angle), jnp.sin(angle)
    cos, sin = jnp.concatenate([cos, cos], 1), jnp.concatenate([-sin, sin], 1)
    gain_q, gain_k = norm_query.reshape(1, HD), norm_key.reshape(1, HD)

    raw = dot(h1, full_qkv)
    q, kv = head_prep(raw, cos, sin, gain_q, gain_k, query_heads, groups)
    q = q.reshape(seq_count, 2 * ways, block, q_width)

    mine, theirs = pair_columns([w_gate, w_up, w_down], pair, 2)
    shards = swap_shards(mine, after(theirs, h1), pair)
    full_kv = ctx_gather(after(kv, full_output), ways).reshape(-1, seq_count, 2 * ways, block, kv_width)
    shards = after(shards, kv)
    full_gate, full_up, full_down = (
        gather_weight(shards[:, i * hidden : (i + 1) * hidden], 2) for i in range(3)
    )
    cot_all = gather_rows(after(cot_own, shards), 2)

    q = after(q, cot_all)
    heads, lse = attend(info, q, full_kv, count, ways)
    mixed = heads.reshape(-1, q_width)
    lows, highs = return_rows(dot_cols(mixed, full_output).astype(BF16), ways)
    x2, h2_own = row_pass(
        functools.partial(middle_kernel, len(lows), len(highs)),
        (inputs, gain_mlp_row, *lows, *highs),
        (row_f32, row_bf16),
        "middle",
    )
    h2 = gather_rows(h2_own, 2)

    gate = dot(h2, full_gate)
    up = dot(h2, full_up)
    act = lax.optimization_barrier((gate / (1.0 + jnp.exp(-gate)) * up).astype(BF16))
    grad_down = dot_rows(cot_all, act).astype(BF16)
    d_act = dot(after(cot_all, grad_down), full_down)
    sg = 1.0 / (1.0 + jnp.exp(-gate))
    d_gate = (d_act * up * sg * (1.0 + gate * (1.0 - sg))).astype(BF16)
    d_up = (d_act * gate * sg).astype(BF16)
    d_h2_part = (dot_cols(d_gate, full_gate) + dot_cols(d_up, full_up)).astype(BF16)
    h2_late = after(h2, d_h2_part)
    grad_gate = dot_rows(h2_late, d_gate).astype(BF16)
    grad_up = dot_rows(h2_late, d_up).astype(BF16)
    lows, highs = return_rows(d_h2_part, 2, (grad_gate, grad_up))
    returned = (lows[0], highs[0])
    d_x2, d_x2_low, gain_mlp = row_pass(
        functools.partial(back_kernel, len(lows), len(highs), None),
        (cot_own, x2, gain_mlp_row, *lows, *highs),
        (row_f32, row_bf16, gain_shape),
        "middle_back",
    )
    y_part = dot_cols(after(act, d_x2_low), full_down).astype(BF16)
    branch = after(gather_rows(d_x2_low, ways), y_part)
    rows_down = scatter_weight(grad_down, 2)
    rows_gate = scatter_weight(after(grad_gate, (rows_down, returned)), 2)
    def one(both, split):
        return own_rows(both, pair, split, [(0, both.shape[1], 0, 0)], [both.shape[1]])[0]

    d_att = dot(branch, full_output).astype(BF16).reshape(q.shape)
    rows_up = scatter_weight(after(grad_up, (rows_gate, d_att)), 2)
    grad_output = dot_rows(branch, mixed).astype(BF16)
    shard_down = one(rows_down, 2)
    shard_gate = one(rows_gate, 2)
    d_q, d_kv = attend_back(info, q, d_att, heads, lse, full_kv, count, ways)
    y_lows, y_highs = return_rows(after(y_part, branch), 2, d_q)
    out_tokens = row_pass(
        functools.partial(result_kernel, len(y_lows), len(y_highs), ctx_count),
        (x2, *y_lows, *y_highs),
        row_bf16,
        "result",
    ).reshape(tokens.shape)
    d_qp, gain_q_sum = head_prep_back(
        d_q.reshape(-1, q_width), raw, cos, sin, gain_q, 0, False
    )
    d_h1_query = dot_cols(d_qp, full_qkv[:, :q_width])
    d_kv = after(
        d_kv.reshape(-1, kv_width),
        (rows_up, out_tokens),
    )
    d_kv = ctx_scatter(d_kv, ways)
    shard_up = one(rows_up, 2)
    h1_late = after(h1, (d_h1_query, shard_down, shard_gate, shard_up))
    grad_query = dot_rows(h1_late, d_qp).astype(BF16)
    grad_both = jnp.concatenate([grad_output, grad_query], axis=1)
    rows_both = scatter_weight(after(grad_both, d_kv), ways)
    d_kv = after(d_kv, grad_both)
    d_kvp, gain_k_sum = head_prep_back(d_kv, raw, cos, sin, gain_k, q_width // kv_width, True)
    grad_kv = dot_rows(h1, d_kvp).astype(BF16)
    d_h1 = (
        d_h1_query + dot_cols(after(d_kvp, grad_kv), full_qkv[:, q_width:])
    ).astype(BF16)
    gain_attn = jnp.sum(d_h1.astype(F32) * h1.astype(F32), axis=0) / gain_attn_row[0]
    gains = butterfly_sum(
        jnp.concatenate([gain_attn, gain_mlp[0], gain_q_sum[0], gain_k_sum[0]])
    )
    lows, highs = return_rows(d_h1, ways)
    rows_kv = scatter_weight(after(grad_kv, (rows_both, lows[0], highs[0])), ways)
    plan = [(0, q_width, 0, 0), (q_width, q_width, 1, 0)]
    shard_output, shard_query = own_rows(
        after(rows_both, lows[0]), pair, ways, plan, [q_width, q_width]
    )
    lows[0] = after(lows[0], (gains, shard_output, shard_query))
    grad_tokens = row_pass(
        functools.partial(back_kernel, len(lows), len(highs), ctx_count),
        (d_x2, inputs, gain_attn_row, *lows, *highs),
        row_f32,
        "entry_back",
    )
    rows_kv = after(rows_kv, (lows, highs))
    plan = []
    for h in range(groups):
        for t in (0, 1):
            plan.append(((2 * h + t) * HD, HD, t, h * HD))
    shard_key, shard_value = own_rows(rows_kv, pair, ways, plan, [groups * HD, groups * HD])
    grad_tokens = grad_tokens.reshape(tokens.shape)
    return (
        out_tokens,
        grad_tokens,
        shard_query,
        shard_key,
        shard_value,
        shard_output,
        shard_gate,
        shard_up,
        shard_down,
        swap_blocks(gains[None, :width], ctx_count, 1)[0],
        swap_blocks(gains[None, width : 2 * width], ctx_count, 1)[0],
        gains[2 * width : 2 * width + HD],
        gains[2 * width + HD :],
    )


def solution(mesh):
    block = P("fsdp", "ctx", None, None, None)
    weight = P("ctx", "fsdp")
    return jax.shard_map(
        local,
        mesh=mesh,
        in_specs=(block, block, P()) + (weight,) * 7 + (P(),) * 4,
        out_specs=(block, block) + (weight,) * 7 + (P(),) * 4,
        check_vma=False,
    )
```
